32 devices in a mesh: gx: 8 (over z, y), gy: 4 (over x, core).
Axes of the slice: x: 2, y: 2, z: 4, core: 2. Of those that a mesh axis runs over, the one named last changes fastest.
Arguments:
- positions: float32 [3, 8, 4, 4, 256], P(None, 'gx', 'gy'), as said below
- counts: int32 [8, 4, 4], P('gx', 'gy'), may hold values from 128 to 256, as said below
- targets: float32 [3, 8, 4, 4, 256], P(None, 'gx', 'gy')
- landmark_index: int32 [8, 4, 4], replicated, may hold values from 0 to 1023, as said below
- coarse_matrix: float32 [128, 128], P('gy', 'gx'), as said below
Outputs:
- solution: float32 [3, 8, 4, 4, 256], P(None, 'gx', 'gy')
- residual: float32 [3, 8, 4, 4, 256], P(None, 'gx', 'gy')
The draws below stay inside these ranges and needn't reach their ends.
Inputs may be any that keep to these rules, and one draw needn't show every extreme that they name: `counts`: some cell holds all 256 points live. `landmark_index`: the 4 entries of a column name different live points of that column. `positions`: each point lies inside its cell: x in [i, i + 1), y in [j, j + 1), z in [layer, layer + 1). `coarse_matrix`: gram is symmetric positive definite.
All inputs are finite; a program needn't handle non-finite values.
Results may differ from the reference program's by a relative error of at most 0.0003.
Values sent between devices are 32-bit elements; how exact they have to be, the bound alone decides.
No kernel may reach another device: no remote copies, remote signals or barrier semaphores. Data moves between devices by JAX's collectives and lax.ppermute only.
A program may use at most 64 MiB of HBM per device.

```python
import math
import jax
import jax.numpy as jnp
from jax import lax

B = 256
CZ = 4
Q = 3
LM_DEV = 4
ITERS = 2
NX = 8
NY = 4
M = 128
N_GX = 8
N_GY = 4


def occupancy(key):
    count_key = jax.random.fold_in(key, 7)
    drawn_counts = jax.random.randint(count_key, (NX, NY, CZ), B // 2, B + 1, dtype=jnp.int32)
    chosen = jax.random.randint(jax.random.fold_in(key, 8), (), 0, NX * NY * CZ, dtype=jnp.int32)
    flat_ids = jnp.arange(NX * NY * CZ, dtype=jnp.int32).reshape(NX, NY, CZ)
    return jnp.where(flat_ids == chosen, B, drawn_counts).astype(jnp.int32)


def draw_counts(key, part):
    return occupancy(key)


def draw_landmark_index(key, part):
    live_counts = occupancy(key)
    slot_ids = jnp.arange(B, dtype=jnp.int32)
    dead_slots = (slot_ids[None, None, None, :] >= live_counts[:, :, :, None]).astype(jnp.int32).reshape(NX, NY, CZ * B)
    column_keys = jax.random.split(jax.random.fold_in(key, 9), NX * NY)

    def shuffle_one(column_key):
        return jax.random.permutation(column_key, CZ * B).astype(jnp.int32)
    shuffled = jax.vmap(shuffle_one)(column_keys).reshape(NX, NY, CZ * B)
    scores = shuffled + CZ * B * dead_slots
    picked = jnp.argsort(scores, axis=2)[:, :, :LM_DEV]
    return picked.astype(jnp.int32)


def draw_positions(key, part):
    unit_offsets = jax.random.uniform(key, (3, NX, NY, CZ, B), jnp.float32)
    corner_x = jnp.arange(NX, dtype=jnp.float32)[:, None, None, None]
    corner_y = jnp.arange(NY, dtype=jnp.float32)[None, :, None, None]
    corner_z = jnp.arange(CZ, dtype=jnp.float32)[None, None, :, None]
    return jnp.stack([unit_offsets[0] + corner_x, unit_offsets[1] + corner_y, unit_offsets[2] + corner_z])


def draw_targets(key, part):
    rising = 1.0 + 2.0 * jnp.arange(NX, dtype=jnp.float32) / max(NX - 1, 1)
    values = jax.random.normal(key, (Q, NX, NY, CZ, B), jnp.float32)
    return values * rising[None, :, None, None, None]


def draw_coarse_matrix(key, part):
    noise = jax.random.uniform(jax.random.fold_in(key, 3), (M, M), jnp.float32, -1.0, 1.0)
    symmetric = (noise + jnp.transpose(noise)) * (0.367 / math.sqrt(M))
    diagonal = jax.random.uniform(jax.random.fold_in(key, 4), (M,), jnp.float32, 0.9, 1.5)
    identity_mask = jnp.eye(M, dtype=bool)
    canonical = jnp.where(identity_mask, diagonal[:, None], symmetric)
    return jnp.transpose(canonical.reshape(N_GX, N_GY, LM_DEV, M), (1, 0, 2, 3)).reshape(M, M)


def setup_inputs(seed: int = 0) -> dict:
    key_list = jax.random.split(jax.random.key(seed), 6)
    positions = draw_positions(jax.random.fold_in(key_list[5], 71), 0)
    counts = draw_counts(jax.random.fold_in(key_list[5], 71), 0)
    targets = draw_targets(jax.random.fold_in(key_list[5], 71), 0)
    landmark_index = draw_landmark_index(jax.random.fold_in(key_list[5], 71), 0)
    coarse_matrix = draw_coarse_matrix(jax.random.fold_in(key_list[5], 71), 0)
    return dict(positions=positions, counts=counts, targets=targets, landmark_index=landmark_index, coarse_matrix=coarse_matrix)


RIDGE_WEIGHT = 2.0
HIGHEST_PRECISION = lax.Precision.HIGHEST

def wendland(points_a, points_b):
    square_sum = jnp.zeros((points_a.shape[1], points_b.shape[1]), jnp.float32)
    for coord in range(3):
        offset = points_a[coord][:, None] - points_b[coord][None, :]
        square_sum = square_sum + offset * offset
    distance = jnp.sqrt(square_sum)
    remain = jnp.maximum(1.0 - distance, 0.0)
    remain = remain * remain
    return remain * remain * (4.0 * distance + 1.0)

def pad_columns(field):
    return jnp.pad(field, ((0, 0), (1, 1), (1, 1), (0, 0), (0, 0)))

def kernel_apply(padded_pos, padded_vec):

    def one_row(row_start):
        pos_rows = lax.dynamic_slice_in_dim(padded_pos, row_start, 3, 1)
        vec_rows = lax.dynamic_slice_in_dim(padded_vec, row_start, 3, 1)
        layer_out = []
        for layer in range(CZ):
            low_layer = max(layer - 1, 0)
            high_layer = min(layer + 2, CZ)
            own_points = pos_rows[:, 1, 1:NY + 1, layer, :]
            near_pos = jnp.stack([pos_rows[:, shift_a, shift_b:shift_b + NY, low_layer:high_layer, :] for shift_a in range(3) for shift_b in range(3)], axis=2)
            near_vec = jnp.stack([vec_rows[:, shift_a, shift_b:shift_b + NY, low_layer:high_layer, :] for shift_a in range(3) for shift_b in range(3)], axis=2)
            near_pos = near_pos.reshape(3, NY, -1)
            near_vec = near_vec.reshape(Q, NY, -1)
            kern = jax.vmap(wendland, in_axes=(1, 1))(own_points, near_pos)
            layer_out.append(jnp.einsum('ybn,qyn->qyb', kern, near_vec, precision=HIGHEST_PRECISION))
        return jnp.stack(layer_out, axis=2)
    rows_out = lax.map(one_row, jnp.arange(NX, dtype=jnp.int32))
    return jnp.transpose(rows_out, (1, 0, 2, 3, 4))

def landmark_terms(padded_pos, padded_vec, landmark_pos, grid_x, grid_y):

    def one_landmark(point, start_x, start_y):
        zero_start = jnp.int32(0)
        window_pos = lax.dynamic_slice(padded_pos, (zero_start, start_x, start_y, zero_start, zero_start), (3, 3, 3, CZ, B)).reshape(3, -1)
        window_vec = lax.dynamic_slice(padded_vec, (zero_start, start_x, start_y, zero_start, zero_start), (Q, 3, 3, CZ, B)).reshape(Q, -1)
        kern = wendland(point[:, None], window_pos)[0]
        return jnp.dot(window_vec, kern, precision=HIGHEST_PRECISION)
    return jax.vmap(one_landmark, in_axes=(1, 0, 0))(landmark_pos, grid_x, grid_y)

def landmark_spread(padded_pos, landmark_pos, grid_x, grid_y, coarse):
    field_sum = jnp.zeros((Q, NX + 2, NY + 2, CZ, B), jnp.float32)
    for shift_a in range(3):
        for shift_b in range(3):
            cloud = padded_pos[:, grid_x + shift_a, grid_y + shift_b].reshape(3, M, CZ * B)

            def one_landmark(point, points_near):
                return wendland(point[:, None], points_near)[0]
            kern = jax.vmap(one_landmark, in_axes=(1, 1))(landmark_pos, cloud)
            weighted = kern[None, :, :] * jnp.transpose(coarse)[:, :, None]
            weighted = lax.optimization_barrier(jnp.sum(weighted.reshape(Q, NX, NY, LM_DEV, CZ, B), axis=3))
            field_sum = field_sum.at[:, shift_a:shift_a + NX, shift_b:shift_b + NY].add(weighted)
    return field_sum[:, 1:NX + 1, 1:NY + 1]

def per_component(values):
    return values[:, None, None, None, None]

def reference(positions, counts, targets, landmark_index, coarse_matrix):
    slot_ids = jnp.arange(B, dtype=jnp.int32)
    live_mask = (slot_ids[None, None, None, :] < counts[:, :, :, None]).astype(jnp.float32)
    rhs_field = live_mask[None] * targets
    padded_pos = pad_columns(positions)
    landmark_ids = jnp.arange(M, dtype=jnp.int32)
    grid_x = (landmark_ids // (NY * LM_DEV)).astype(jnp.int32)
    grid_y = (landmark_ids // LM_DEV % NY).astype(jnp.int32)
    flat_index = landmark_index.reshape(M).astype(jnp.int32)
    layer_of = flat_index // B
    slot_of = flat_index % B
    landmark_pos = positions[:, grid_x, grid_y, layer_of, slot_of]
    gram = jnp.transpose(coarse_matrix.reshape(N_GY, N_GX, LM_DEV, M), (1, 0, 2, 3)).reshape(M, M)

    def operator(vector):
        product = kernel_apply(padded_pos, pad_columns(vector))
        return live_mask[None] * product + RIDGE_WEIGHT * vector

    def precondition(vector):
        terms = landmark_terms(padded_pos, pad_columns(vector), landmark_pos, grid_x, grid_y)
        coarse = jnp.dot(gram, terms, precision=HIGHEST_PRECISION)
        spread = landmark_spread(padded_pos, landmark_pos, grid_x, grid_y, coarse)
        return vector / RIDGE_WEIGHT + live_mask[None] * spread

    def inner_sums(left, right):
        return lax.optimization_barrier(jnp.sum(left * right, axis=(1, 2, 3, 4)))
    solution = jnp.zeros_like(rhs_field)
    residual = rhs_field
    search = precondition(residual)
    gamma = inner_sums(residual, search)
    direction = search
    for iteration in range(ITERS):
        image = operator(direction)
        alpha = gamma / inner_sums(direction, image)
        solution = solution + per_component(alpha) * direction
        residual = residual - per_component(alpha) * image
        if iteration + 1 < ITERS:
            search = precondition(residual)
            gamma_new = inner_sums(residual, search)
            direction = search + per_component(gamma_new / gamma) * direction
            gamma = gamma_new
    return (solution, residual)
```

```python
import functools

import jax
import jax.numpy as jnp
from jax import lax
from jax.experimental import pallas as pl
from jax.experimental.pallas import tpu as pltpu
from jax.sharding import PartitionSpec as P

ITERS = 2


RIDGE_WEIGHT = 2.0
HIGHEST_PRECISION = lax.Precision.HIGHEST

F32 = jnp.float32
BF16 = jnp.bfloat16
LANES = 128
FAR = 4096.0
KERN_SCALE = 256.0
VMEM_BYTES = 34 * 2**20


def with_halo(x, sides, width):
    for axis, dim in sides:
        peers, length = (lax.axis_size(axis), x.shape[dim])
        up = [(i, (i + 1) % peers) for i in range(peers - 1)]
        down = [(j, i) for i, j in up]
        last = lax.slice_in_dim(x, length - width, length, axis=dim)
        leading = lax.slice_in_dim(x, 0, width, axis=dim)
        before = lax.ppermute(last, axis, up)
        after = lax.ppermute(leading, axis, down)
        x = jnp.concatenate([before, x, after], axis=dim)
    return x


def wendland(points_a, points_b):
    square_sum = jnp.zeros((points_a.shape[1], points_b.shape[1]), jnp.float32)
    for coord in range(3):
        offset = points_a[coord][:, None] - points_b[coord][None, :]
        square_sum = square_sum + offset * offset
    distance = jnp.sqrt(square_sum)
    remain = jnp.maximum(1.0 - distance, 0.0)
    remain = remain * remain
    return remain * remain * (4.0 * distance + 1.0)


def cell_rim(field):
    return with_halo(field, (("gx", 1), ("gy", 2)), 1)


def inner_sums(left, right):
    return jnp.sum(left * right, axis=(1, 2, 3, 4))


def per_component(values):
    return values[:, None, None, None, None]


def global_inner(values):
    return lax.psum(values, ("gx", "gy"))


def local_plain(positions, counts, targets, landmark_index, coarse_matrix):
    components = targets.shape[0]
    layer_count = positions.shape[3]
    slot_count = positions.shape[4]
    owned_count = landmark_index.shape[2]
    column_points = layer_count * slot_count
    slot_ids = jnp.arange(slot_count, dtype=jnp.int32)
    live_mask = (slot_ids[None, None, None, :] < counts[:, :, :, None]).astype(jnp.float32)
    live_flat = live_mask.reshape(1, column_points)
    rhs_field = live_mask[None] * targets
    ext_pos = cell_rim(positions)
    ext_cloud = ext_pos.reshape(3, 9 * column_points)
    own_points = positions.reshape(3, column_points)
    row_index = lax.axis_index("gx")
    col_index = lax.axis_index("gy")
    three_ids = jnp.arange(3, dtype=jnp.int32)
    near_rows = jnp.clip(row_index + three_ids - 1, 0, lax.axis_size("gx") - 1)
    near_cols = jnp.clip(col_index + three_ids - 1, 0, lax.axis_size("gy") - 1)
    near_index = landmark_index[near_rows[:, None], near_cols[None, :], :]
    ext_flat = ext_pos.reshape(3, 3, 3, column_points)
    near_pos = jnp.take_along_axis(ext_flat, near_index[None], axis=3)
    landmark_pos = near_pos[:, 1, 1, :]
    spread_kernel = wendland(own_points, near_pos.reshape(3, 9 * owned_count))

    def coarse_solve(terms):
        row_terms = lax.all_gather(terms, "gy", axis=0, tiled=True)
        return lax.psum_scatter(
            jnp.dot(coarse_matrix, row_terms, precision=HIGHEST_PRECISION),
            "gx",
            scatter_dimension=0,
            tiled=True,
        )

    def landmark_sums(vector):
        gather_kernel = wendland(landmark_pos, ext_cloud)
        ext_vec = cell_rim(vector).reshape(components, 9 * column_points)
        return jnp.einsum("kn,qn->kq", gather_kernel, ext_vec, precision=HIGHEST_PRECISION)

    def precondition(vector):
        terms = landmark_sums(vector)
        coarse = coarse_solve(terms)
        near_coarse = with_halo(
            coarse.reshape(1, 1, owned_count, components), (("gx", 0), ("gy", 1)), 1
        )
        near_coarse = near_coarse.reshape(9 * owned_count, components)
        spread = jnp.einsum("nm,mq->qn", spread_kernel, near_coarse, precision=HIGHEST_PRECISION)
        return vector / RIDGE_WEIGHT + (live_flat * spread).reshape(vector.shape)

    solution = jnp.zeros_like(rhs_field)
    residual = rhs_field
    search = precondition(residual)
    gamma = global_inner(inner_sums(residual, search))
    direction = search
    for iteration in range(ITERS):
        operator_ext_vec = cell_rim(direction)
        layer_out = []
        for layer in range(layer_count):
            low_layer = max(layer - 1, 0)
            high_layer = min(layer + 2, layer_count)
            near_points = ext_pos[:, :, :, low_layer:high_layer, :].reshape(3, -1)
            near_values = operator_ext_vec[:, :, :, low_layer:high_layer, :].reshape(components, -1)
            kern = wendland(positions[:, 0, 0, layer, :], near_points)
            layer_out.append(
                jnp.einsum("bn,qn->qb", kern, near_values, precision=HIGHEST_PRECISION)
            )
        product = jnp.stack(layer_out, axis=1).reshape(direction.shape)
        image = live_mask[None] * product + RIDGE_WEIGHT * direction
        alpha = gamma / global_inner(inner_sums(direction, image))
        solution = solution + per_component(alpha) * direction
        residual = residual - per_component(alpha) * image
        if iteration + 1 < ITERS:
            search = precondition(residual)
            gamma_new = global_inner(inner_sums(residual, search))
            direction = search + per_component(gamma_new / gamma) * direction
            gamma = gamma_new
    return (solution, residual)


def row_ids(lanes):
    return lax.broadcasted_iota(jnp.int32, (8, lanes), 0)


def lane_ids(rows, lanes):
    return lax.broadcasted_iota(jnp.int32, (rows, lanes), 1)


def split_three(values):
    high = values.astype(BF16).astype(F32)
    rest = values - high
    middle = rest.astype(BF16).astype(F32)
    low = (rest - middle).astype(BF16).astype(F32)
    return high, middle, low


def centred(column, centre):
    row = row_ids(column.shape[1])
    shift = jnp.where(row == 0, centre[0], jnp.where(row == 1, centre[1], centre[2]))
    xyz = jnp.where(row < 3, column - shift, 0.0)
    norm = 16.0 * jnp.sum(xyz * xyz, axis=0, keepdims=True)
    return row, xyz, norm + (1.0 - column[6:7, :]) * FAR


def near_features(column, centre):
    row, xyz, norm = centred(column, centre)
    high, middle, low = split_three(
        jnp.where(row == 3, norm, jnp.where(row == 4, 1.0, xyz))
    )
    return jnp.concatenate([high, middle, low, high, middle, high], axis=0)


def own_features(column, centre):
    row, xyz, norm = centred(column, centre)
    high, middle, low = split_three(
        jnp.where(row == 3, 1.0, jnp.where(row == 4, norm, -32.0 * xyz))
    )
    return jnp.concatenate([high, high, high, middle, middle, low], axis=0)


def scaled_wendland(square16):
    square16 = jnp.maximum(square16, 1e-6)
    four = square16 * lax.rsqrt(square16)
    remain = jnp.maximum(4.0 - four, 0.0)
    remain = remain * remain
    return remain * remain * (four + 1.0)


def bf16_dot(left, right):
    return jnp.dot(left, right, preferred_element_type=F32)


def full_dot(left, right, transposed=False):
    dims = (((1,), (1 if transposed else 0,)), ((), ()))
    return lax.dot_general(
        left, right, dims, precision=HIGHEST_PRECISION, preferred_element_type=F32
    )


def swap_partner(index, peers, odd):
    step = 1 - 2 * lax.rem(index + odd, 2)
    partner = index + step
    good = jnp.logical_and(partner >= 0, partner < peers)
    return jnp.where(good, partner, index)


def swap(x, axis, odd):
    peers = lax.axis_size(axis)
    pairs = []
    for i in range(odd, peers - 1, 2):
        pairs += [(i, i + 1), (i + 1, i)]
    return lax.ppermute(x, axis, pairs)


class Shape:
    def __init__(self, positions, landmark_index, nx, ny):
        self.nx, self.ny = nx, ny
        self.devices = nx * ny
        self.layers, self.slots = positions.shape[3], positions.shape[4]
        self.points = self.layers * self.slots
        self.owned = landmark_index.shape[2]
        self.row_landmarks = ny * self.owned
        self.landmarks = nx * self.row_landmarks
        self.window = 3 * self.row_landmarks
        self.blocks = []
        offset = 0
        for layer in range(self.layers):
            low, high = max(layer - 1, 0), min(layer + 2, self.layers)
            self.blocks.append((low, high, offset))
            offset += (high - low) * self.slots
        self.pairs = offset

    def centre(self, i, j):
        return (i.astype(F32) + 0.5, j.astype(F32) + 0.5, 0.5 * self.layers)

    def window_start(self, i):
        start = jnp.clip(i - 1, 0, self.nx - 3) * self.row_landmarks
        return pl.multiple_of(start, self.row_landmarks)

    def near_ids(self, i, j):
        rows = [i, swap_partner(i, self.nx, 0), swap_partner(i, self.nx, 1)]
        cols = [j, swap_partner(j, self.ny, 0), swap_partner(j, self.ny, 1)]
        return rows, cols


def prepare_kernel(sh, pos_ref, counts_ref, tgt_ref, own_ref):
    slot = lane_ids(1, sh.slots)
    for layer in range(sh.layers):
        live = (slot < counts_ref[0, 0, layer]).astype(F32)
        at = pl.ds(layer * sh.slots, sh.slots)
        own_ref[0:3, at] = pos_ref[:, 0, 0, layer, :]
        own_ref[3:6, at] = live * tgt_ref[:, 0, 0, layer, :]
        own_ref[6:7, at] = live
        own_ref[7:8, at] = jnp.zeros_like(live)


def terms_kernel(sh, index_ref, row_ref, even_ref, odd_ref, coarse_ref, pay_ref):
    i, j = lax.axis_index("gx"), lax.axis_index("gy")
    own = row_ref[0]
    lane = lane_ids(8, sh.points)
    row1 = lax.broadcasted_iota(jnp.int32, (8, 1), 0)
    marks = []
    for k in range(sh.owned):
        hit = jnp.where(lane == index_ref[i, j, k], own, 0.0)
        marks.append(jnp.sum(hit, axis=1, keepdims=True))
    coords = []
    for coord in range(3):
        column = jnp.zeros((8, 1), F32)
        for k in range(sh.owned):
            column = jnp.where(row1 == k, marks[k][coord : coord + 1, :], column)
        coords.append(column)

    def add_column(column, sums):
        square = jnp.zeros((8, sh.points), F32)
        for coord in range(3):
            offset = column[coord : coord + 1, :] - coords[coord]
            square = square + offset * offset
        kern = scaled_wendland(16.0 * square)
        return tuple(
            total + kern * column[3 + q : 4 + q, :] for q, total in enumerate(sums)
        )

    sums = tuple(jnp.zeros((8, sh.points), F32) for _ in range(3))
    for ref in (row_ref, even_ref, odd_ref):
        sums = lax.fori_loop(0, 3, lambda c, s, ref=ref: add_column(ref[c], s), sums)
    terms = [jnp.sum(s, axis=1, keepdims=True) * (1.0 / KERN_SCALE) for s in sums]
    lane8 = lane_ids(8, LANES)
    first = (i * sh.ny + j) * sh.owned
    tile = jnp.zeros((8, LANES), F32)
    for k in range(sh.owned):
        column = marks[k]
        for q in range(3):
            column = jnp.where(row1 == 3 + q, terms[q][k : k + 1, :], column)
        tile = jnp.where(lane8 == first + k, column, tile)
    extra = jnp.concatenate([coarse_ref[...], jnp.zeros((4, LANES), F32)], axis=0)
    for d in range(sh.devices):
        pay_ref[d, 0:8, :] = tile
        pay_ref[d, 8:16, :] = extra


def build_kernel(sh, row_ref, even_ref, odd_ref, high_ref, low_ref):
    centre = sh.centre(lax.axis_index("gx"), lax.axis_index("gy"))
    own = own_features(row_ref[0], centre).astype(BF16)

    def one(ref, group, c):
        near = near_features(ref[c], centre).T.astype(BF16)
        for layer, (low, high, offset) in enumerate(sh.blocks):
            lhs = near[layer * sh.slots : (layer + 1) * sh.slots]
            for target in range(low, high):
                square = bf16_dot(lhs, own[:, target * sh.slots : (target + 1) * sh.slots])
                kern = scaled_wendland(square)
                head = kern.astype(BF16)
                at = offset + (target - low) * sh.slots
                high_ref[group * 3 + c, :, at : at + sh.slots] = head
                low_ref[group * 3 + c, :, at : at + sh.slots] = (
                    kern - head.astype(F32)
                ).astype(BF16)
        return 0

    for group, ref in enumerate((row_ref, even_ref, odd_ref)):
        lax.fori_loop(0, 3, lambda c, _, ref=ref, group=group: one(ref, group, c), 0)


def apply_column(sh, high_ref, low_ref, c, values, out_ref):
    head = values.astype(BF16)
    tail = values - head.astype(F32)
    both = jnp.concatenate([head.astype(F32), tail], axis=0).astype(BF16)
    for layer, (low, high, offset) in enumerate(sh.blocks):
        at = slice(layer * sh.slots, (layer + 1) * sh.slots)
        width = (high - low) * sh.slots
        main = bf16_dot(both[:, at], high_ref[c, :, offset : offset + width])
        rest = bf16_dot(head[:, at], low_ref[c, :, offset : offset + width])
        out_ref[:, low * sh.slots : high * sh.slots] += main[:8] + main[8:] + rest


def gathered_matrix(sh, recv_ref, gram_ref):
    lane = lane_ids(sh.ny * 4, LANES)
    width = sh.row_landmarks
    groups = LANES // width
    for g in range(groups):
        total = jnp.zeros((sh.ny * 4, LANES), F32)
        for i in range(sh.nx):
            tiles = jnp.concatenate(
                [recv_ref[i * sh.ny + j, 8:16, :][0:4] for j in range(sh.ny)], axis=0
            )
            shift = ((i - g) * width) % LANES
            if shift:
                tiles = pltpu.roll(tiles, shift, axis=1)
            keep = jnp.logical_and(lane >= i * width, lane < (i + 1) * width)
            total = jnp.where(keep, tiles, total)
        for j in range(sh.ny):
            for r in range(4):
                p = groups * r + g
                at = (p // sh.owned) * width + j * sh.owned + p % sh.owned
                gram_ref[at : at + 1, :] = total[j * 4 + r : j * 4 + r + 1, :]


def first_kernel(
    sh, row_ref, even_ref, odd_ref, recv_ref, high_ref, low_ref,
    pay_ref, search_ref, spread_ref, gram_ref, image_ref, mark_ref,
):
    i, j = lax.axis_index("gx"), lax.axis_index("gy")
    centre = sh.centre(i, j)
    gathered = recv_ref[0, 0:8, :]
    for d in range(1, sh.devices):
        gathered = gathered + recv_ref[d, 0:8, :]
    gathered_matrix(sh, recv_ref, gram_ref)
    mark_ref[...] = own_features(gathered, centre).T.astype(BF16)
    row8 = row_ids(LANES)
    terms = jnp.where(row8 < 3, jnp.concatenate([gathered[3:8], gathered[0:3]], axis=0), 0.0)
    coarse = full_dot(terms, gram_ref[...], transposed=True)
    image_ref[...] = jnp.zeros_like(image_ref)
    rows, _ = sh.near_ids(i, j)
    keep3 = row_ids(sh.points) < 3
    for group, ref in enumerate((row_ref, even_ref, odd_ref)):
        start = sh.window_start(rows[group])
        marks = mark_ref[pl.ds(start, sh.window), :]
        part = pltpu.roll(coarse, lax.rem(LANES - start, LANES), axis=1)[:, : sh.window]

        def one(c, _, ref=ref, group=group, marks=marks, part=part):
            column = ref[c]
            near = near_features(column, centre).astype(BF16)
            spread = scaled_wendland(bf16_dot(marks, near)) * (1.0 / KERN_SCALE)
            spread_ref[group * 3 + c] = spread
            residual = jnp.where(
                keep3, jnp.concatenate([column[3:8], column[0:3]], axis=0), 0.0
            )
            search = residual * (1.0 / RIDGE_WEIGHT) + full_dot(part, spread)
            search_ref[group * 3 + c] = search
            apply_column(sh, high_ref, low_ref, group * 3 + c, search, image_ref)
            return 0

        lax.fori_loop(0, 3, one, 0)
    own = row_ref[0]
    residual = jnp.where(keep3, jnp.concatenate([own[3:8], own[0:3]], axis=0), 0.0)
    search = search_ref[0]
    image = image_ref[...] * (1.0 / KERN_SCALE) + RIDGE_WEIGHT * search
    image_ref[...] = image
    gamma = jnp.sum(residual * search, axis=1, keepdims=True)
    delta = jnp.sum(search * image, axis=1, keepdims=True)
    window = full_dot(image, spread_ref[0], transposed=True)
    lane = lane_ids(8, LANES)
    fill = jnp.zeros((8, LANES - sh.window), F32)
    tile = jnp.concatenate([window, fill], axis=1)
    tile = jnp.where(lane == sh.window, gamma, tile)
    tile = jnp.where(lane == sh.window + 1, delta, tile)
    for d in range(sh.devices):
        for q in range(3):
            pay_ref[d, :, q * sh.points : (q + 1) * sh.points] = image[q : q + 1, :]
            at = 3 * sh.points + q * LANES
            pay_ref[d, :, at : at + LANES] = tile[q : q + 1, :]


def second_kernel(
    sh, recv_ref, row_ref, search_ref, spread_ref, gram_ref, image_ref, high_ref, low_ref,
    pay_ref, residual_ref, next_ref, product_ref,
):
    i, j = lax.axis_index("gx"), lax.axis_index("gy")
    lane = lane_ids(8, LANES)
    terms = jnp.zeros((8, LANES), F32)
    scalars = jnp.zeros((8, LANES), F32)
    fill = jnp.zeros((5, LANES), F32)
    for a in range(sh.nx):
        parts = []
        for q in range(3):
            at = 3 * sh.points + q * LANES
            total = recv_ref[a * sh.ny, :, at : at + LANES]
            for b in range(1, sh.ny):
                total = total + recv_ref[a * sh.ny + b, :, at : at + LANES]
            parts.append(total)
        tile = jnp.concatenate(parts + [fill], axis=0)
        scalars = scalars + tile
        start = min(max(a - 1, 0), sh.nx - 3) * sh.row_landmarks
        tile = jnp.where(lane < sh.window, tile, 0.0)
        terms = terms + (pltpu.roll(tile, start, axis=1) if start else tile)
    gamma = scalars[:, sh.window : sh.window + 1]
    delta = scalars[:, sh.window + 1 : sh.window + 2]
    row1 = lax.broadcasted_iota(jnp.int32, (8, 1), 0)
    alpha = jnp.where(row1 < 3, gamma / jnp.where(row1 < 3, delta, 1.0), 0.0)
    coarse = full_dot(terms, gram_ref[...], transposed=True)
    product_ref[...] = jnp.zeros_like(product_ref)
    rows, cols = sh.near_ids(i, j)
    zeros5 = jnp.zeros((5, sh.points), F32)
    for group in range(3):
        start = sh.window_start(rows[group])
        part = pltpu.roll(coarse, lax.rem(LANES - start, LANES), axis=1)[:, : sh.window]
        for c in range(3):
            at = group * 3 + c
            source = rows[group] * sh.ny + cols[c]
            image = jnp.concatenate(
                [recv_ref[source, :, q * sh.points : (q + 1) * sh.points] for q in range(3)]
                + [zeros5],
                axis=0,
            )
            step = image * (1.0 / RIDGE_WEIGHT) + full_dot(part, spread_ref[at])
            search = search_ref[at] - alpha * step
            if at == 0:
                next_ref[...] = search
            apply_column(sh, high_ref, low_ref, at, search, product_ref)
    own = row_ref[0]
    keep3 = row_ids(sh.points) < 3
    residual = jnp.where(keep3, jnp.concatenate([own[3:8], own[0:3]], axis=0), 0.0)
    image = image_ref[...]
    residual = residual - alpha * image
    residual_ref[...] = residual
    search = next_ref[...]
    product = product_ref[...] * (1.0 / KERN_SCALE) + RIDGE_WEIGHT * search
    product_ref[...] = product
    sums = [
        jnp.sum(residual * search, axis=1, keepdims=True),
        jnp.sum(search * product, axis=1, keepdims=True),
        jnp.sum(search * image, axis=1, keepdims=True)
        + jnp.sum(search_ref[0] * product, axis=1, keepdims=True),
        gamma,
        delta,
    ]
    tile = jnp.zeros((8, LANES), F32)
    for at, value in enumerate(sums):
        tile = jnp.where(lane == at, value, tile)
    for d in range(sh.devices):
        pay_ref[d] = tile


def last_kernel(
    sh, recv_ref, sums_ref, search_ref, image_ref, residual_ref, next_ref, product_ref,
    solution_ref, final_ref,
):
    total = recv_ref[0]
    for d in range(1, sh.devices):
        total = total + recv_ref[d]
    own = sums_ref[0]
    row1 = lax.broadcasted_iota(jnp.int32, (8, 1), 0)
    good = row1 < 3
    gamma, delta = own[:, 3:4], own[:, 4:5]
    gamma_new, inner, cross = total[:, 0:1], total[:, 1:2], total[:, 2:3]
    safe_gamma = jnp.where(good, gamma, 1.0)
    safe_delta = jnp.where(good, delta, 1.0)
    alpha = gamma / safe_delta
    beta = gamma_new / safe_gamma
    curve = inner + beta * cross + beta * beta * delta
    step = gamma_new / jnp.where(good, curve, 1.0)
    direction = next_ref[...] + beta * search_ref[0]
    image = product_ref[...] + beta * image_ref[...]
    solution = alpha * search_ref[0] + step * direction
    residual = residual_ref[...] - step * image
    for layer in range(sh.layers):
        at = slice(layer * sh.slots, (layer + 1) * sh.slots)
        solution_ref[:, 0, 0, layer, :] = solution[0:3, at]
        final_ref[:, 0, 0, layer, :] = residual[0:3, at]


def local_fast(positions, counts, targets, landmark_index, coarse_matrix):
    both = ("gx", "gy")
    sh = Shape(positions, landmark_index, lax.axis_size("gx"), lax.axis_size("gy"))
    field = jax.ShapeDtypeStruct((8, sh.points), F32)
    vmem = pl.BlockSpec(memory_space=pltpu.VMEM)
    smem = pl.BlockSpec(memory_space=pltpu.SMEM)

    def call(kernel, name, out_shape, in_specs, cost=10**6, limit=VMEM_BYTES, scratch=()):
        return pl.pallas_call(
            functools.partial(kernel, sh),
            out_shape=out_shape,
            in_specs=in_specs,
            out_specs=jax.tree.map(lambda _: vmem, out_shape),
            scratch_shapes=scratch,
            name=name,
            compiler_params=pltpu.CompilerParams(vmem_limit_bytes=limit),
            cost_estimate=pl.CostEstimate(flops=cost, bytes_accessed=10**5, transcendentals=0),
        )

    def exchange(payload):
        return lax.all_to_all(payload, both, 0, 0)

    own = call(prepare_kernel, "prepare", field, [vmem, smem, vmem])(
        positions, counts, targets
    )
    row = jnp.stack([own, swap(own, "gy", 0), swap(own, "gy", 1)])
    even, odd = swap(row, "gx", 0), swap(row, "gx", 1)
    coarse_rows = coarse_matrix.reshape(coarse_matrix.size // LANES, LANES)

    terms = call(
        terms_kernel,
        "terms",
        jax.ShapeDtypeStruct((sh.devices, 16, LANES), F32),
        [smem, vmem, vmem, vmem, vmem],
    )(landmark_index, row, even, odd, coarse_rows)
    terms = exchange(terms)

    kern = jax.ShapeDtypeStruct((9, sh.slots, sh.pairs), BF16)
    high, low = call(
        build_kernel, "build", (kern, kern), [vmem] * 3, cost=2 * 10**10
    )(row, even, odd)

    wide = 3 * sh.points + 3 * LANES
    payload, search, spread, gram, image = call(
        first_kernel,
        "first",
        (
            jax.ShapeDtypeStruct((sh.devices, 1, wide), F32),
            jax.ShapeDtypeStruct((9, 8, sh.points), F32),
            jax.ShapeDtypeStruct((9, sh.window, sh.points), F32),
            jax.ShapeDtypeStruct((sh.landmarks, LANES), F32),
            field,
        ),
        [vmem] * 6,
        scratch=[pltpu.VMEM((sh.landmarks, 48), BF16)],
    )(row, even, odd, terms, high, low)
    images = exchange(payload)

    sums, residual, following, product = call(
        second_kernel,
        "second",
        (jax.ShapeDtypeStruct((sh.devices, 8, LANES), F32), field, field, field),
        [vmem] * 8,
    )(images, row, search, spread, gram, image, high, low)
    totals = exchange(sums)

    out = jax.ShapeDtypeStruct(targets.shape, F32)
    return call(last_kernel, "last", (out, out), [vmem] * 7)(
        totals, sums, search, image, residual, following, product
    )


def local(positions, counts, targets, landmark_index, coarse_matrix):
    nx, ny = lax.axis_size("gx"), lax.axis_size("gy")
    landmarks = nx * ny * landmark_index.shape[2]
    if landmarks == LANES and nx >= 3 and targets.shape[0] == 3:
        return local_fast(positions, counts, targets, landmark_index, coarse_matrix)
    return local_plain(positions, counts, targets, landmark_index, coarse_matrix)


def solution(mesh):
    return jax.shard_map(
        local,
        mesh=mesh,
        in_specs=(
            P(None, "gx", "gy", None, None),
            P("gx", "gy", None),
            P(None, "gx", "gy", None, None),
            P(),
            P("gy", "gx"),
        ),
        out_specs=(P(None, "gx", "gy", None, None), P(None, "gx", "gy", None, None)),
        check_vma=False,
    )
```

```python
import functools

import jax
import jax.numpy as jnp
from jax import lax
from jax.experimental import pallas as pl
from jax.experimental.pallas import tpu as pltpu
from jax.sharding import PartitionSpec as P

ITERS = 2


RIDGE_WEIGHT = 2.0
HIGHEST_PRECISION = lax.Precision.HIGHEST

F32 = jnp.float32
BF16 = jnp.bfloat16
LANES = 128
FAR = 4096.0
KERN_SCALE = 256.0
VMEM_BYTES = 24 * 2**20


def with_halo(x, sides, width):
    for axis, dim in sides:
        peers, length = (lax.axis_size(axis), x.shape[dim])
        up = [(i, (i + 1) % peers) for i in range(peers - 1)]
        down = [(j, i) for i, j in up]
        last = lax.slice_in_dim(x, length - width, length, axis=dim)
        leading = lax.slice_in_dim(x, 0, width, axis=dim)
        before = lax.ppermute(last, axis, up)
        after = lax.ppermute(leading, axis, down)
        x = jnp.concatenate([before, x, after], axis=dim)
    return x


def wendland(points_a, points_b):
    square_sum = jnp.zeros((points_a.shape[1], points_b.shape[1]), jnp.float32)
    for coord in range(3):
        offset = points_a[coord][:, None] - points_b[coord][None, :]
        square_sum = square_sum + offset * offset
    distance = jnp.sqrt(square_sum)
    remain = jnp.maximum(1.0 - distance, 0.0)
    remain = remain * remain
    return remain * remain * (4.0 * distance + 1.0)


def cell_rim(field):
    return with_halo(field, (("gx", 1), ("gy", 2)), 1)


def inner_sums(left, right):
    return jnp.sum(left * right, axis=(1, 2, 3, 4))


def per_component(values):
    return values[:, None, None, None, None]


def global_inner(values):
    return lax.psum(values, ("gx", "gy"))


def local_plain(positions, counts, targets, landmark_index, coarse_matrix):
    components = targets.shape[0]
    layer_count = positions.shape[3]
    slot_count = positions.shape[4]
    owned_count = landmark_index.shape[2]
    column_points = layer_count * slot_count
    slot_ids = jnp.arange(slot_count, dtype=jnp.int32)
    live_mask = (slot_ids[None, None, None, :] < counts[:, :, :, None]).astype(jnp.float32)
    live_flat = live_mask.reshape(1, column_points)
    rhs_field = live_mask[None] * targets
    ext_pos = cell_rim(positions)
    ext_cloud = ext_pos.reshape(3, 9 * column_points)
    own_points = positions.reshape(3, column_points)
    row_index = lax.axis_index("gx")
    col_index = lax.axis_index("gy")
    three_ids = jnp.arange(3, dtype=jnp.int32)
    near_rows = jnp.clip(row_index + three_ids - 1, 0, lax.axis_size("gx") - 1)
    near_cols = jnp.clip(col_index + three_ids - 1, 0, lax.axis_size("gy") - 1)
    near_index = landmark_index[near_rows[:, None], near_cols[None, :], :]
    ext_flat = ext_pos.reshape(3, 3, 3, column_points)
    near_pos = jnp.take_along_axis(ext_flat, near_index[None], axis=3)
    landmark_pos = near_pos[:, 1, 1, :]
    spread_kernel = wendland(own_points, near_pos.reshape(3, 9 * owned_count))

    def coarse_solve(terms):
        row_terms = lax.all_gather(terms, "gy", axis=0, tiled=True)
        return lax.psum_scatter(
            jnp.dot(coarse_matrix, row_terms, precision=HIGHEST_PRECISION),
            "gx",
            scatter_dimension=0,
            tiled=True,
        )

    def landmark_sums(vector):
        gather_kernel = wendland(landmark_pos, ext_cloud)
        ext_vec = cell_rim(vector).reshape(components, 9 * column_points)
        return jnp.einsum("kn,qn->kq", gather_kernel, ext_vec, precision=HIGHEST_PRECISION)

    def precondition(vector):
        terms = landmark_sums(vector)
        coarse = coarse_solve(terms)
        near_coarse = with_halo(
            coarse.reshape(1, 1, owned_count, components), (("gx", 0), ("gy", 1)), 1
        )
        near_coarse = near_coarse.reshape(9 * owned_count, components)
        spread = jnp.einsum("nm,mq->qn", spread_kernel, near_coarse, precision=HIGHEST_PRECISION)
        return vector / RIDGE_WEIGHT + (live_flat * spread).reshape(vector.shape)

    solution = jnp.zeros_like(rhs_field)
    residual = rhs_field
    search = precondition(residual)
    gamma = global_inner(inner_sums(residual, search))
    direction = search
    for iteration in range(ITERS):
        operator_ext_vec = cell_rim(direction)
        layer_out = []
        for layer in range(layer_count):
            low_layer = max(layer - 1, 0)
            high_layer = min(layer + 2, layer_count)
            near_points = ext_pos[:, :, :, low_layer:high_layer, :].reshape(3, -1)
            near_values = operator_ext_vec[:, :, :, low_layer:high_layer, :].reshape(components, -1)
            kern = wendland(positions[:, 0, 0, layer, :], near_points)
            layer_out.append(
                jnp.einsum("bn,qn->qb", kern, near_values, precision=HIGHEST_PRECISION)
            )
        product = jnp.stack(layer_out, axis=1).reshape(direction.shape)
        image = live_mask[None] * product + RIDGE_WEIGHT * direction
        alpha = gamma / global_inner(inner_sums(direction, image))
        solution = solution + per_component(alpha) * direction
        residual = residual - per_component(alpha) * image
        if iteration + 1 < ITERS:
            search = precondition(residual)
            gamma_new = global_inner(inner_sums(residual, search))
            direction = search + per_component(gamma_new / gamma) * direction
            gamma = gamma_new
    return (solution, residual)


def row_ids(lanes):
    return lax.broadcasted_iota(jnp.int32, (8, lanes), 0)


def lane_ids(rows, lanes):
    return lax.broadcasted_iota(jnp.int32, (rows, lanes), 1)


def split_three(values):
    high = values.astype(BF16).astype(F32)
    rest = values - high
    middle = rest.astype(BF16).astype(F32)
    low = (rest - middle).astype(BF16).astype(F32)
    return high, middle, low


def centred(column, centre):
    row = row_ids(column.shape[1])
    shift = jnp.where(row == 0, centre[0], jnp.where(row == 1, centre[1], centre[2]))
    xyz = jnp.where(row < 3, column - shift, 0.0)
    norm = 16.0 * jnp.sum(xyz * xyz, axis=0, keepdims=True)
    return row, xyz, norm + (1.0 - column[6:7, :]) * FAR


def near_features(column, centre):
    row, xyz, norm = centred(column, centre)
    high, middle, low = split_three(
        jnp.where(row == 3, norm, jnp.where(row == 4, 1.0, xyz))
    )
    return jnp.concatenate([high, middle, low, high, middle, high], axis=0)


def own_features(column, centre):
    row, xyz, norm = centred(column, centre)
    high, middle, low = split_three(
        jnp.where(row == 3, 1.0, jnp.where(row == 4, norm, -32.0 * xyz))
    )
    return jnp.concatenate([high, high, high, middle, middle, low], axis=0)


def scaled_wendland(square16):
    square16 = jnp.maximum(square16, 1e-6)
    four = square16 * lax.rsqrt(square16)
    remain = jnp.maximum(4.0 - four, 0.0)
    remain = remain * remain
    return remain * remain * (four + 1.0)


def bf16_dot(left, right):
    return jnp.dot(left, right, preferred_element_type=F32)


def full_dot(left, right, transposed=False):
    dims = (((1,), (1 if transposed else 0,)), ((), ()))
    return lax.dot_general(
        left, right, dims, precision=HIGHEST_PRECISION, preferred_element_type=F32
    )


def swap_partner(index, peers, odd):
    step = 1 - 2 * lax.rem(index + odd, 2)
    partner = index + step
    good = jnp.logical_and(partner >= 0, partner < peers)
    return jnp.where(good, partner, index)


def swap(x, axis, odd):
    peers = lax.axis_size(axis)
    pairs = []
    for i in range(odd, peers - 1, 2):
        pairs += [(i, i + 1), (i + 1, i)]
    return lax.ppermute(x, axis, pairs)


class Shape:
    def __init__(self, positions, landmark_index, nx, ny):
        self.nx, self.ny = nx, ny
        self.devices = nx * ny
        self.layers, self.slots = positions.shape[3], positions.shape[4]
        self.points = self.layers * self.slots
        self.owned = landmark_index.shape[2]
        self.row_landmarks = ny * self.owned
        self.landmarks = nx * self.row_landmarks
        self.window = 3 * self.row_landmarks
        self.blocks = []
        offset = 0
        for layer in range(self.layers):
            low, high = max(layer - 1, 0), min(layer + 2, self.layers)
            self.blocks.append((low, high, offset))
            offset += (high - low) * self.slots
        self.pairs = offset

    def centre(self, i, j):
        return (i.astype(F32) + 0.5, j.astype(F32) + 0.5, 0.5 * self.layers)

    def window_start(self, i):
        start = jnp.clip(i - 1, 0, self.nx - 3) * self.row_landmarks
        return pl.multiple_of(start, self.row_landmarks)

    def near_ids(self, i, j):
        rows = [i, swap_partner(i, self.nx, 0), swap_partner(i, self.nx, 1)]
        cols = [j, swap_partner(j, self.ny, 0), swap_partner(j, self.ny, 1)]
        return rows, cols


def prepare_kernel(sh, pos_ref, counts_ref, tgt_ref, own_ref):
    slot = lane_ids(1, sh.slots)
    for layer in range(sh.layers):
        live = (slot < counts_ref[0, 0, layer]).astype(F32)
        at = pl.ds(layer * sh.slots, sh.slots)
        own_ref[0:3, at] = pos_ref[:, 0, 0, layer, :]
        own_ref[3:6, at] = live * tgt_ref[:, 0, 0, layer, :]
        own_ref[6:7, at] = live
        own_ref[7:8, at] = jnp.zeros_like(live)


def terms_kernel(sh, index_ref, row_ref, even_ref, odd_ref, coarse_ref, pay_ref):
    i, j = lax.axis_index("gx"), lax.axis_index("gy")
    own = row_ref[0]
    lane = lane_ids(8, sh.points)
    row1 = lax.broadcasted_iota(jnp.int32, (8, 1), 0)
    marks = []
    for k in range(sh.owned):
        hit = jnp.where(lane == index_ref[i, j, k], own, 0.0)
        marks.append(jnp.sum(hit, axis=1, keepdims=True))
    coords = []
    for coord in range(3):
        column = jnp.zeros((8, 1), F32)
        for k in range(sh.owned):
            column = jnp.where(row1 == k, marks[k][coord : coord + 1, :], column)
        coords.append(column)

    def add_column(column, sums):
        square = jnp.zeros((8, sh.points), F32)
        for coord in range(3):
            offset = column[coord : coord + 1, :] - coords[coord]
            square = square + offset * offset
        kern = scaled_wendland(16.0 * square)
        return tuple(
            total + kern * column[3 + q : 4 + q, :] for q, total in enumerate(sums)
        )

    sums = tuple(jnp.zeros((8, sh.points), F32) for _ in range(3))
    for ref in (row_ref, even_ref, odd_ref):
        sums = lax.fori_loop(0, 3, lambda c, s, ref=ref: add_column(ref[c], s), sums)
    terms = [jnp.sum(s, axis=1, keepdims=True) * (1.0 / KERN_SCALE) for s in sums]
    lane8 = lane_ids(8, LANES)
    first = (i * sh.ny + j) * sh.owned
    tile = jnp.zeros((8, LANES), F32)
    for k in range(sh.owned):
        column = marks[k]
        for q in range(3):
            column = jnp.where(row1 == 3 + q, terms[q][k : k + 1, :], column)
        tile = jnp.where(lane8 == first + k, column, tile)
    extra = jnp.concatenate([coarse_ref[...], jnp.zeros((4, LANES), F32)], axis=0)
    for d in range(sh.devices):
        pay_ref[d, 0:8, :] = tile
        pay_ref[d, 8:16, :] = extra


def build_kernel(sh, row_ref, even_ref, odd_ref, high_ref, low_ref):
    centre = sh.centre(lax.axis_index("gx"), lax.axis_index("gy"))
    own = own_features(row_ref[0], centre).astype(BF16)

    def one(ref, group, c):
        near = near_features(ref[c], centre).T.astype(BF16)
        for layer, (low, high, offset) in enumerate(sh.blocks):
            lhs = near[layer * sh.slots : (layer + 1) * sh.slots]
            for target in range(low, high):
                square = bf16_dot(lhs, own[:, target * sh.slots : (target + 1) * sh.slots])
                kern = scaled_wendland(square)
                head = kern.astype(BF16)
                at = offset + (target - low) * sh.slots
                high_ref[group * 3 + c, :, at : at + sh.slots] = head
                low_ref[group * 3 + c, :, at : at + sh.slots] = (
                    kern - head.astype(F32)
                ).astype(BF16)
        return 0

    for group, ref in enumerate((row_ref, even_ref, odd_ref)):
        lax.fori_loop(0, 3, lambda c, _, ref=ref, group=group: one(ref, group, c), 0)


def apply_column(sh, high_ref, low_ref, c, values, out_ref):
    head = values.astype(BF16)
    tail = values - head.astype(F32)
    both = jnp.concatenate([head.astype(F32), tail], axis=0).astype(BF16)
    for layer, (low, high, offset) in enumerate(sh.blocks):
        at = slice(layer * sh.slots, (layer + 1) * sh.slots)
        width = (high - low) * sh.slots
        main = bf16_dot(both[:, at], high_ref[c, :, offset : offset + width])
        rest = bf16_dot(head[:, at], low_ref[c, :, offset : offset + width])
        out_ref[:, low * sh.slots : high * sh.slots] += main[:8] + main[8:] + rest


def gathered_matrix(sh, recv_ref, gram_ref):
    lane = lane_ids(sh.ny * 4, LANES)
    width = sh.row_landmarks
    groups = LANES // width
    for g in range(groups):
        total = jnp.zeros((sh.ny * 4, LANES), F32)
        for i in range(sh.nx):
            tiles = jnp.concatenate(
                [recv_ref[i * sh.ny + j, 8:16, :][0:4] for j in range(sh.ny)], axis=0
            )
            shift = ((i - g) * width) % LANES
            if shift:
                tiles = pltpu.roll(tiles, shift, axis=1)
            keep = jnp.logical_and(lane >= i * width, lane < (i + 1) * width)
            total = jnp.where(keep, tiles, total)
        for j in range(sh.ny):
            for r in range(4):
                p = groups * r + g
                at = (p // sh.owned) * width + j * sh.owned + p % sh.owned
                gram_ref[at : at + 1, :] = total[j * 4 + r : j * 4 + r + 1, :]


def first_kernel(
    sh, row_ref, even_ref, odd_ref, recv_ref, high_ref, low_ref,
    pay_ref, search_ref, spread_ref, gram_ref, image_ref, mark_ref,
):
    i, j = lax.axis_index("gx"), lax.axis_index("gy")
    centre = sh.centre(i, j)
    gathered = recv_ref[0, 0:8, :]
    for d in range(1, sh.devices):
        gathered = gathered + recv_ref[d, 0:8, :]
    gathered_matrix(sh, recv_ref, gram_ref)
    mark_ref[...] = own_features(gathered, centre).T.astype(BF16)
    row8 = row_ids(LANES)
    terms = jnp.where(row8 < 3, jnp.concatenate([gathered[3:8], gathered[0:3]], axis=0), 0.0)
    coarse = full_dot(terms, gram_ref[...], transposed=True)
    image_ref[...] = jnp.zeros_like(image_ref)
    rows, _ = sh.near_ids(i, j)
    keep3 = row_ids(sh.points) < 3
    for group, ref in enumerate((row_ref, even_ref, odd_ref)):
        start = sh.window_start(rows[group])
        marks = mark_ref[pl.ds(start, sh.window), :]
        part = pltpu.roll(coarse, lax.rem(LANES - start, LANES), axis=1)[:, : sh.window]

        def one(c, _, ref=ref, group=group, marks=marks, part=part):
            column = ref[c]
            near = near_features(column, centre).astype(BF16)
            spread = scaled_wendland(bf16_dot(marks, near)) * (1.0 / KERN_SCALE)
            spread_ref[group * 3 + c] = spread
            residual = jnp.where(
                keep3, jnp.concatenate([column[3:8], column[0:3]], axis=0), 0.0
            )
            search = residual * (1.0 / RIDGE_WEIGHT) + full_dot(part, spread)
            search_ref[group * 3 + c] = search
            apply_column(sh, high_ref, low_ref, group * 3 + c, search, image_ref)
            return 0

        lax.fori_loop(0, 3, one, 0)
    own = row_ref[0]
    residual = jnp.where(keep3, jnp.concatenate([own[3:8], own[0:3]], axis=0), 0.0)
    search = search_ref[0]
    image = image_ref[...] * (1.0 / KERN_SCALE) + RIDGE_WEIGHT * search
    image_ref[...] = image
    gamma = jnp.sum(residual * search, axis=1, keepdims=True)
    delta = jnp.sum(search * image, axis=1, keepdims=True)
    window = full_dot(image, spread_ref[0], transposed=True)
    lane = lane_ids(8, LANES)
    fill = jnp.zeros((8, LANES - sh.window), F32)
    tile = jnp.concatenate([window, fill], axis=1)
    tile = jnp.where(lane == sh.window, gamma, tile)
    tile = jnp.where(lane == sh.window + 1, delta, tile)
    for d in range(sh.devices):
        for q in range(3):
            pay_ref[d, :, q * sh.points : (q + 1) * sh.points] = image[q : q + 1, :]
            at = 3 * sh.points + q * LANES
            pay_ref[d, :, at : at + LANES] = tile[q : q + 1, :]


def second_kernel(
    sh, recv_ref, row_ref, search_ref, spread_ref, gram_ref, image_ref, high_ref, low_ref,
    pay_ref, residual_ref, next_ref, product_ref,
):
    i, j = lax.axis_index("gx"), lax.axis_index("gy")
    lane = lane_ids(8, LANES)
    terms = jnp.zeros((8, LANES), F32)
    scalars = jnp.zeros((8, LANES), F32)
    fill = jnp.zeros((5, LANES), F32)
    for a in range(sh.nx):
        parts = []
        for q in range(3):
            at = 3 * sh.points + q * LANES
            total = recv_ref[a * sh.ny, :, at : at + LANES]
            for b in range(1, sh.ny):
                total = total + recv_ref[a * sh.ny + b, :, at : at + LANES]
            parts.append(total)
        tile = jnp.concatenate(parts + [fill], axis=0)
        scalars = scalars + tile
        start = min(max(a - 1, 0), sh.nx - 3) * sh.row_landmarks
        tile = jnp.where(lane < sh.window, tile, 0.0)
        terms = terms + (pltpu.roll(tile, start, axis=1) if start else tile)
    gamma = scalars[:, sh.window : sh.window + 1]
    delta = scalars[:, sh.window + 1 : sh.window + 2]
    row1 = lax.broadcasted_iota(jnp.int32, (8, 1), 0)
    alpha = jnp.where(row1 < 3, gamma / jnp.where(row1 < 3, delta, 1.0), 0.0)
    coarse = full_dot(terms, gram_ref[...], transposed=True)
    product_ref[...] = jnp.zeros_like(product_ref)
    rows, cols = sh.near_ids(i, j)
    zeros5 = jnp.zeros((5, sh.points), F32)
    for group in range(3):
        start = sh.window_start(rows[group])
        part = pltpu.roll(coarse, lax.rem(LANES - start, LANES), axis=1)[:, : sh.window]
        for c in range(3):
            at = group * 3 + c
            source = rows[group] * sh.ny + cols[c]
            image = jnp.concatenate(
                [recv_ref[source, :, q * sh.points : (q + 1) * sh.points] for q in range(3)]
                + [zeros5],
                axis=0,
            )
            step = image * (1.0 / RIDGE_WEIGHT) + full_dot(part, spread_ref[at])
            search = search_ref[at] - alpha * step
            if at == 0:
                next_ref[...] = search
            apply_column(sh, high_ref, low_ref, at, search, product_ref)
    own = row_ref[0]
    keep3 = row_ids(sh.points) < 3
    residual = jnp.where(keep3, jnp.concatenate([own[3:8], own[0:3]], axis=0), 0.0)
    image = image_ref[...]
    residual = residual - alpha * image
    residual_ref[...] = residual
    search = next_ref[...]
    product = product_ref[...] * (1.0 / KERN_SCALE) + RIDGE_WEIGHT * search
    product_ref[...] = product
    sums = [
        jnp.sum(residual * search, axis=1, keepdims=True),
        jnp.sum(search * product, axis=1, keepdims=True),
        jnp.sum(search * image, axis=1, keepdims=True)
        + jnp.sum(search_ref[0] * product, axis=1, keepdims=True),
        gamma,
        delta,
    ]
    tile = jnp.zeros((8, LANES), F32)
    for at, value in enumerate(sums):
        tile = jnp.where(lane == at, value, tile)
    for d in range(sh.devices):
        pay_ref[d] = tile


def last_kernel(
    sh, recv_ref, sums_ref, search_ref, image_ref, residual_ref, next_ref, product_ref,
    solution_ref, final_ref,
):
    total = recv_ref[0]
    for d in range(1, sh.devices):
        total = total + recv_ref[d]
    own = sums_ref[0]
    row1 = lax.broadcasted_iota(jnp.int32, (8, 1), 0)
    good = row1 < 3
    gamma, delta = own[:, 3:4], own[:, 4:5]
    gamma_new, inner, cross = total[:, 0:1], total[:, 1:2], total[:, 2:3]
    safe_gamma = jnp.where(good, gamma, 1.0)
    safe_delta = jnp.where(good, delta, 1.0)
    alpha = gamma / safe_delta
    beta = gamma_new / safe_gamma
    curve = inner + beta * cross + beta * beta * delta
    step = gamma_new / jnp.where(good, curve, 1.0)
    direction = next_ref[...] + beta * search_ref[0]
    image = product_ref[...] + beta * image_ref[...]
    solution = alpha * search_ref[0] + step * direction
    residual = residual_ref[...] - step * image
    for layer in range(sh.layers):
        at = slice(layer * sh.slots, (layer + 1) * sh.slots)
        solution_ref[:, 0, 0, layer, :] = solution[0:3, at]
        final_ref[:, 0, 0, layer, :] = residual[0:3, at]


def local_fast(positions, counts, targets, landmark_index, coarse_matrix):
    both = ("gx", "gy")
    sh = Shape(positions, landmark_index, lax.axis_size("gx"), lax.axis_size("gy"))
    field = jax.ShapeDtypeStruct((8, sh.points), F32)
    vmem = pl.BlockSpec(memory_space=pltpu.VMEM)
    smem = pl.BlockSpec(memory_space=pltpu.SMEM)

    def call(kernel, name, out_shape, in_specs, cost=10**6, limit=VMEM_BYTES, scratch=()):
        return pl.pallas_call(
            functools.partial(kernel, sh),
            out_shape=out_shape,
            in_specs=in_specs,
            out_specs=jax.tree.map(lambda _: vmem, out_shape),
            scratch_shapes=scratch,
            name=name,
            compiler_params=pltpu.CompilerParams(vmem_limit_bytes=limit),
            cost_estimate=pl.CostEstimate(flops=cost, bytes_accessed=10**5, transcendentals=0),
        )

    def exchange(payload):
        return lax.all_to_all(payload, both, 0, 0)

    own = call(prepare_kernel, "prepare", field, [vmem, smem, vmem])(
        positions, counts, targets
    )
    row = jnp.stack([own, swap(own, "gy", 0), swap(own, "gy", 1)])
    even, odd = swap(row, "gx", 0), swap(row, "gx", 1)
    coarse_rows = coarse_matrix.reshape(coarse_matrix.size // LANES, LANES)

    terms = call(
        terms_kernel,
        "terms",
        jax.ShapeDtypeStruct((sh.devices, 16, LANES), F32),
        [smem, vmem, vmem, vmem, vmem],
    )(landmark_index, row, even, odd, coarse_rows)
    terms, row, even, odd = lax.optimization_barrier((exchange(terms), row, even, odd))

    kern = jax.ShapeDtypeStruct((9, sh.slots, sh.pairs), BF16)
    high, low = call(
        build_kernel, "build", (kern, kern), [vmem] * 3, cost=2 * 10**10
    )(row, even, odd)

    wide = 3 * sh.points + 3 * LANES
    payload, search, spread, gram, image = call(
        first_kernel,
        "first",
        (
            jax.ShapeDtypeStruct((sh.devices, 1, wide), F32),
            jax.ShapeDtypeStruct((9, 8, sh.points), F32),
            jax.ShapeDtypeStruct((9, sh.window, sh.points), F32),
            jax.ShapeDtypeStruct((sh.landmarks, LANES), F32),
            field,
        ),
        [vmem] * 6,
        scratch=[pltpu.VMEM((sh.landmarks, 48), BF16)],
    )(row, even, odd, terms, high, low)
    images = exchange(payload)

    sums, residual, following, product = call(
        second_kernel,
        "second",
        (jax.ShapeDtypeStruct((sh.devices, 8, LANES), F32), field, field, field),
        [vmem] * 8,
    )(images, row, search, spread, gram, image, high, low)
    totals = exchange(sums)

    out = jax.ShapeDtypeStruct(targets.shape, F32)
    return call(last_kernel, "last", (out, out), [vmem] * 7)(
        totals, sums, search, image, residual, following, product
    )


def local(positions, counts, targets, landmark_index, coarse_matrix):
    nx, ny = lax.axis_size("gx"), lax.axis_size("gy")
    landmarks = nx * ny * landmark_index.shape[2]
    if landmarks == LANES and nx >= 3 and targets.shape[0] == 3:
        return local_fast(positions, counts, targets, landmark_index, coarse_matrix)
    return local_plain(positions, counts, targets, landmark_index, coarse_matrix)


def solution(mesh):
    return jax.shard_map(
        local,
        mesh=mesh,
        in_specs=(
            P(None, "gx", "gy", None, None),
            P("gx", "gy", None),
            P(None, "gx", "gy", None, None),
            P(),
            P("gy", "gx"),
        ),
        out_specs=(P(None, "gx", "gy", None, None), P(None, "gx", "gy", None, None)),
        check_vma=False,
    )
```

```python
import functools

import jax
import jax.numpy as jnp
from jax import lax
from jax.experimental import pallas as pl
from jax.experimental.pallas import tpu as pltpu
from jax.sharding import PartitionSpec as P

ITERS = 2


RIDGE_WEIGHT = 2.0
HIGHEST_PRECISION = lax.Precision.HIGHEST

F32 = jnp.float32
BF16 = jnp.bfloat16
LANES = 128
FAR = 4096.0
KERN_SCALE = 256.0
VMEM_BYTES = 8 * 2**20


def with_halo(x, sides, width):
    for axis, dim in sides:
        peers, length = (lax.axis_size(axis), x.shape[dim])
        up = [(i, (i + 1) % peers) for i in range(peers - 1)]
        down = [(j, i) for i, j in up]
        last = lax.slice_in_dim(x, length - width, length, axis=dim)
        leading = lax.slice_in_dim(x, 0, width, axis=dim)
        before = lax.ppermute(last, axis, up)
        after = lax.ppermute(leading, axis, down)
        x = jnp.concatenate([before, x, after], axis=dim)
    return x


def wendland(points_a, points_b):
    square_sum = jnp.zeros((points_a.shape[1], points_b.shape[1]), jnp.float32)
    for coord in range(3):
        offset = points_a[coord][:, None] - points_b[coord][None, :]
        square_sum = square_sum + offset * offset
    distance = jnp.sqrt(square_sum)
    remain = jnp.maximum(1.0 - distance, 0.0)
    remain = remain * remain
    return remain * remain * (4.0 * distance + 1.0)


def cell_rim(field):
    return with_halo(field, (("gx", 1), ("gy", 2)), 1)


def inner_sums(left, right):
    return jnp.sum(left * right, axis=(1, 2, 3, 4))


def per_component(values):
    return values[:, None, None, None, None]


def global_inner(values):
    return lax.psum(values, ("gx", "gy"))


def local_plain(positions, counts, targets, landmark_index, coarse_matrix):
    components = targets.shape[0]
    layer_count = positions.shape[3]
    slot_count = positions.shape[4]
    owned_count = landmark_index.shape[2]
    column_points = layer_count * slot_count
    slot_ids = jnp.arange(slot_count, dtype=jnp.int32)
    live_mask = (slot_ids[None, None, None, :] < counts[:, :, :, None]).astype(jnp.float32)
    live_flat = live_mask.reshape(1, column_points)
    rhs_field = live_mask[None] * targets
    ext_pos = cell_rim(positions)
    ext_cloud = ext_pos.reshape(3, 9 * column_points)
    own_points = positions.reshape(3, column_points)
    row_index = lax.axis_index("gx")
    col_index = lax.axis_index("gy")
    three_ids = jnp.arange(3, dtype=jnp.int32)
    near_rows = jnp.clip(row_index + three_ids - 1, 0, lax.axis_size("gx") - 1)
    near_cols = jnp.clip(col_index + three_ids - 1, 0, lax.axis_size("gy") - 1)
    near_index = landmark_index[near_rows[:, None], near_cols[None, :], :]
    ext_flat = ext_pos.reshape(3, 3, 3, column_points)
    near_pos = jnp.take_along_axis(ext_flat, near_index[None], axis=3)
    landmark_pos = near_pos[:, 1, 1, :]
    spread_kernel = wendland(own_points, near_pos.reshape(3, 9 * owned_count))

    def coarse_solve(terms):
        row_terms = lax.all_gather(terms, "gy", axis=0, tiled=True)
        return lax.psum_scatter(
            jnp.dot(coarse_matrix, row_terms, precision=HIGHEST_PRECISION),
            "gx",
            scatter_dimension=0,
            tiled=True,
        )

    def landmark_sums(vector):
        gather_kernel = wendland(landmark_pos, ext_cloud)
        ext_vec = cell_rim(vector).reshape(components, 9 * column_points)
        return jnp.einsum("kn,qn->kq", gather_kernel, ext_vec, precision=HIGHEST_PRECISION)

    def precondition(vector):
        terms = landmark_sums(vector)
        coarse = coarse_solve(terms)
        near_coarse = with_halo(
            coarse.reshape(1, 1, owned_count, components), (("gx", 0), ("gy", 1)), 1
        )
        near_coarse = near_coarse.reshape(9 * owned_count, components)
        spread = jnp.einsum("nm,mq->qn", spread_kernel, near_coarse, precision=HIGHEST_PRECISION)
        return vector / RIDGE_WEIGHT + (live_flat * spread).reshape(vector.shape)

    solution = jnp.zeros_like(rhs_field)
    residual = rhs_field
    search = precondition(residual)
    gamma = global_inner(inner_sums(residual, search))
    direction = search
    for iteration in range(ITERS):
        operator_ext_vec = cell_rim(direction)
        layer_out = []
        for layer in range(layer_count):
            low_layer = max(layer - 1, 0)
            high_layer = min(layer + 2, layer_count)
            near_points = ext_pos[:, :, :, low_layer:high_layer, :].reshape(3, -1)
            near_values = operator_ext_vec[:, :, :, low_layer:high_layer, :].reshape(components, -1)
            kern = wendland(positions[:, 0, 0, layer, :], near_points)
            layer_out.append(
                jnp.einsum("bn,qn->qb", kern, near_values, precision=HIGHEST_PRECISION)
            )
        product = jnp.stack(layer_out, axis=1).reshape(direction.shape)
        image = live_mask[None] * product + RIDGE_WEIGHT * direction
        alpha = gamma / global_inner(inner_sums(direction, image))
        solution = solution + per_component(alpha) * direction
        residual = residual - per_component(alpha) * image
        if iteration + 1 < ITERS:
            search = precondition(residual)
            gamma_new = global_inner(inner_sums(residual, search))
            direction = search + per_component(gamma_new / gamma) * direction
            gamma = gamma_new
    return (solution, residual)


def row_ids(lanes):
    return lax.broadcasted_iota(jnp.int32, (8, lanes), 0)


def lane_ids(rows, lanes):
    return lax.broadcasted_iota(jnp.int32, (rows, lanes), 1)


def split_three(values):
    high = values.astype(BF16).astype(F32)
    rest = values - high
    middle = rest.astype(BF16).astype(F32)
    low = (rest - middle).astype(BF16).astype(F32)
    return high, middle, low


def centred(column, centre):
    row = row_ids(column.shape[1])
    shift = jnp.where(row == 0, centre[0], jnp.where(row == 1, centre[1], centre[2]))
    xyz = jnp.where(row < 3, column - shift, 0.0)
    norm = 16.0 * jnp.sum(xyz * xyz, axis=0, keepdims=True)
    return row, xyz, norm + (1.0 - column[6:7, :]) * FAR


def near_features(column, centre):
    row, xyz, norm = centred(column, centre)
    high, middle, low = split_three(
        jnp.where(row == 3, norm, jnp.where(row == 4, 1.0, xyz))
    )
    return jnp.concatenate([high, middle, low, high, middle, high], axis=0)


def own_features(column, centre):
    row, xyz, norm = centred(column, centre)
    high, middle, low = split_three(
        jnp.where(row == 3, 1.0, jnp.where(row == 4, norm, -32.0 * xyz))
    )
    return jnp.concatenate([high, high, high, middle, middle, low], axis=0)


def scaled_wendland(square16):
    square16 = jnp.maximum(square16, 1e-6)
    four = square16 * lax.rsqrt(square16)
    remain = jnp.maximum(4.0 - four, 0.0)
    remain = remain * remain
    return remain * remain * (four + 1.0)


def bf16_dot(left, right):
    return jnp.dot(left, right, preferred_element_type=F32)


def full_dot(left, right, transposed=False):
    dims = (((1,), (1 if transposed else 0,)), ((), ()))
    return lax.dot_general(
        left, right, dims, precision=HIGHEST_PRECISION, preferred_element_type=F32
    )


def swap_partner(index, peers, odd):
    step = 1 - 2 * lax.rem(index + odd, 2)
    partner = index + step
    good = jnp.logical_and(partner >= 0, partner < peers)
    return jnp.where(good, partner, index)


def swap(x, axis, odd):
    peers = lax.axis_size(axis)
    pairs = []
    for i in range(odd, peers - 1, 2):
        pairs += [(i, i + 1), (i + 1, i)]
    return lax.ppermute(x, axis, pairs)


class Shape:
    def __init__(self, positions, landmark_index, nx, ny):
        self.nx, self.ny = nx, ny
        self.devices = nx * ny
        self.layers, self.slots = positions.shape[3], positions.shape[4]
        self.points = self.layers * self.slots
        self.owned = landmark_index.shape[2]
        self.row_landmarks = ny * self.owned
        self.landmarks = nx * self.row_landmarks
        self.window = 3 * self.row_landmarks
        self.blocks = []
        offset = 0
        for layer in range(self.layers):
            low, high = max(layer - 1, 0), min(layer + 2, self.layers)
            self.blocks.append((low, high, offset))
            offset += (high - low) * self.slots
        self.pairs = offset

    def centre(self, i, j):
        return (i.astype(F32) + 0.5, j.astype(F32) + 0.5, 0.5 * self.layers)

    def window_start(self, i):
        start = jnp.clip(i - 1, 0, self.nx - 3) * self.row_landmarks
        return pl.multiple_of(start, self.row_landmarks)

    def near_ids(self, i, j):
        rows = [i, swap_partner(i, self.nx, 0), swap_partner(i, self.nx, 1)]
        cols = [j, swap_partner(j, self.ny, 0), swap_partner(j, self.ny, 1)]
        return rows, cols


def prepare_kernel(sh, pos_hbm, counts_hbm, tgt_hbm, own_ref, pos_ref, counts_ref, tgt_ref, sems):
    copies = [
        pltpu.make_async_copy(counts_hbm, counts_ref, sems.at[0]),
        pltpu.make_async_copy(pos_hbm, pos_ref, sems.at[1]),
        pltpu.make_async_copy(tgt_hbm, tgt_ref, sems.at[2]),
    ]
    for copy in copies:
        copy.start()
    for copy in copies:
        copy.wait()
    slot = lane_ids(1, sh.slots)
    for layer in range(sh.layers):
        live = (slot < counts_ref[0, 0, layer]).astype(F32)
        at = pl.ds(layer * sh.slots, sh.slots)
        own_ref[0:3, at] = pos_ref[:, 0, 0, layer, :]
        own_ref[3:6, at] = live * tgt_ref[:, 0, 0, layer, :]
        own_ref[6:7, at] = live
        own_ref[7:8, at] = jnp.zeros_like(live)


def terms_kernel(
    sh, index_hbm, coarse_hbm, after_ref, row_ref, even_ref, odd_ref, pay_ref,
    index_ref, coarse_ref, sems,
):
    copies = [
        pltpu.make_async_copy(index_hbm, index_ref, sems.at[0]),
        pltpu.make_async_copy(coarse_hbm, coarse_ref, sems.at[1]),
    ]
    for copy in copies:
        copy.start()
    for copy in copies:
        copy.wait()
    i, j = lax.axis_index("gx"), lax.axis_index("gy")
    own = row_ref[0]
    lane = lane_ids(8, sh.points)
    row1 = lax.broadcasted_iota(jnp.int32, (8, 1), 0)
    marks = []
    for k in range(sh.owned):
        hit = jnp.where(lane == index_ref[i, j, k], own, 0.0)
        marks.append(jnp.sum(hit, axis=1, keepdims=True))
    coords = []
    for coord in range(3):
        column = jnp.zeros((8, 1), F32)
        for k in range(sh.owned):
            column = jnp.where(row1 == k, marks[k][coord : coord + 1, :], column)
        coords.append(column)

    def add_column(column, sums):
        square = jnp.zeros((8, sh.points), F32)
        for coord in range(3):
            offset = column[coord : coord + 1, :] - coords[coord]
            square = square + offset * offset
        kern = scaled_wendland(16.0 * square)
        return tuple(
            total + kern * column[3 + q : 4 + q, :] for q, total in enumerate(sums)
        )

    sums = tuple(jnp.zeros((8, sh.points), F32) for _ in range(3))
    for ref in (row_ref, even_ref, odd_ref):
        sums = lax.fori_loop(0, 3, lambda c, s, ref=ref: add_column(ref[c], s), sums)
    terms = [jnp.sum(s, axis=1, keepdims=True) * (1.0 / KERN_SCALE) for s in sums]
    lane8 = lane_ids(8, LANES)
    row8 = row_ids(LANES)
    half = LANES // 2
    first = (i * sh.ny + j) * sh.owned
    tile = jnp.zeros((8, LANES), F32)
    for k in range(sh.owned):
        column = jnp.where(row1 < 3, marks[k], 0.0)
        for q in range(3):
            column = jnp.where(row1 == 3 + q, terms[q][k : k + 1, :], column)
        tile = jnp.where(lane8 == first + k, column, tile)
    groups = half // sh.row_landmarks
    pieces = [coarse_ref[pl.ds(g, 8, stride=groups), :] for g in range(groups)]
    block = jnp.concatenate(pieces + pieces, axis=1)
    own_half = (lane8 >= half) == (first >= half)
    tile = jnp.where(own_half, tile, block)
    for d in range(sh.devices):
        pay_ref[d] = tile


def build_kernel(sh, count, row_ref, *refs):
    group_refs, (high_ref, low_ref, near_ref) = refs[: count], refs[count :]
    centre = sh.centre(lax.axis_index("gx"), lax.axis_index("gy"))
    own = own_features(row_ref[0], centre).astype(BF16)

    def one(ref, group, c):
        features = near_features(ref[c], centre)
        near_ref[group * 3 + c] = features.astype(BF16)
        near = features.T.astype(BF16)
        for layer, (low, high, offset) in enumerate(sh.blocks):
            lhs = near[layer * sh.slots : (layer + 1) * sh.slots]
            for target in range(low, high):
                square = bf16_dot(lhs, own[:, target * sh.slots : (target + 1) * sh.slots])
                kern = scaled_wendland(square)
                head = kern.astype(BF16)
                at = offset + (target - low) * sh.slots
                high_ref[group * 3 + c, :, at : at + sh.slots] = head
                low_ref[group * 3 + c, :, at : at + sh.slots] = (
                    kern - head.astype(F32)
                ).astype(BF16)
        return 0

    for group, ref in enumerate(group_refs):
        lax.fori_loop(0, 3, lambda c, _, ref=ref, group=group: one(ref, group, c), 0)


def split_rows(values):
    head = values.astype(BF16)
    tail = values - head.astype(F32)
    return head, jnp.concatenate([head.astype(F32), tail], axis=0).astype(BF16)


def apply_column(sh, high_ref, low_ref, c, values, out_ref):
    head, both = split_rows(values)
    for layer, (low, high, offset) in enumerate(sh.blocks):
        at = slice(layer * sh.slots, (layer + 1) * sh.slots)
        width = (high - low) * sh.slots
        main = bf16_dot(both[:, at], high_ref[c, :, offset : offset + width])
        rest = bf16_dot(head[:, at], low_ref[c, :, offset : offset + width])
        out_ref[:, low * sh.slots : high * sh.slots] += main[:8] + main[8:] + rest


def spread_dot(part, high, low):
    head, both = split_rows(part)
    main = bf16_dot(both, high)
    return main[:8] + main[8:] + bf16_dot(head, low)


def gathered_matrix(sh, recv_ref, gram_ref):
    width = sh.row_landmarks
    half = LANES // 2
    groups = half // width
    lane = lane_ids(sh.ny * 8, LANES)
    for g in range(groups):
        total = jnp.zeros((sh.ny * 8, LANES), F32)
        for i in range(sh.nx):
            tiles = jnp.concatenate([recv_ref[i * sh.ny + j] for j in range(sh.ny)], axis=0)
            base = half if i * width < half else 0
            shift = (i * width - base - g * width) % LANES
            if shift:
                tiles = pltpu.roll(tiles, shift, axis=1)
            keep = jnp.logical_and(lane >= i * width, lane < (i + 1) * width)
            total = jnp.where(keep, tiles, total)
        for j in range(sh.ny):
            for r in range(8):
                p = groups * r + g
                at = (p // sh.owned) * width + j * sh.owned + p % sh.owned
                gram_ref[at : at + 1, :] = total[j * 8 + r : j * 8 + r + 1, :]


def rhs_rows(column, lanes):
    return jnp.where(
        row_ids(lanes) < 3, jnp.concatenate([column[3:8], column[0:3]], axis=0), 0.0
    )


def first_kernel(
    sh, row_ref, even_ref, odd_ref, recv_ref, near0_ref, near1_ref,
    high0_ref, low0_ref, high1_ref, low1_ref,
    pay_ref, search_ref, spread_ref, rest_ref, gram_ref, image_ref, mark_ref,
):
    i, j = lax.axis_index("gx"), lax.axis_index("gy")
    centre = sh.centre(i, j)
    half = LANES // 2
    totals = [jnp.zeros((8, LANES), F32), jnp.zeros((8, LANES), F32)]
    for d in range(sh.devices):
        side = 0 if d * sh.owned < half else 1
        totals[side] = totals[side] + recv_ref[d]
    gathered = jnp.where(lane_ids(8, LANES) < half, totals[0], totals[1])
    gathered = jnp.where(row_ids(LANES) == 6, 1.0, gathered)
    gathered_matrix(sh, recv_ref, gram_ref)
    mark_ref[...] = own_features(gathered, centre).T.astype(BF16)
    coarse = full_dot(rhs_rows(gathered, LANES), gram_ref[...], transposed=True)
    image_ref[...] = jnp.zeros_like(image_ref)
    rows, _ = sh.near_ids(i, j)
    for group, ref in enumerate((row_ref, even_ref, odd_ref)):
        start = sh.window_start(rows[group])
        marks = mark_ref[pl.ds(start, sh.window), :]
        part = pltpu.roll(coarse, lax.rem(LANES - start, LANES), axis=1)[:, : sh.window]
        near_ref = near1_ref if group else near0_ref
        high_ref = high1_ref if group else high0_ref
        low_ref = low1_ref if group else low0_ref
        base = max(group - 1, 0) * 3

        def one(
            c, _, ref=ref, group=group, marks=marks, part=part,
            near_ref=near_ref, high_ref=high_ref, low_ref=low_ref, base=base,
        ):
            spread = scaled_wendland(bf16_dot(marks, near_ref[base + c])) * (1.0 / KERN_SCALE)
            head = spread.astype(BF16)
            rest = (spread - head.astype(F32)).astype(BF16)
            spread_ref[group * 3 + c] = head
            rest_ref[group * 3 + c] = rest
            residual = rhs_rows(ref[c], sh.points)
            search = residual * (1.0 / RIDGE_WEIGHT) + spread_dot(part, head, rest)
            search_ref[group * 3 + c] = search
            apply_column(sh, high_ref, low_ref, base + c, search, image_ref)
            return 0

        lax.fori_loop(0, 3, one, 0)
    residual = rhs_rows(row_ref[0], sh.points)
    search = search_ref[0]
    image = image_ref[...] * (1.0 / KERN_SCALE) + RIDGE_WEIGHT * search
    image_ref[...] = image
    gamma = jnp.sum(residual * search, axis=1, keepdims=True)
    delta = jnp.sum(search * image, axis=1, keepdims=True)
    head, both = split_rows(image)
    across = (((1,), (1,)), ((), ()))
    main = lax.dot_general(both, spread_ref[0], across, preferred_element_type=F32)
    tail = lax.dot_general(head, rest_ref[0], across, preferred_element_type=F32)
    window = main[:8] + main[8:] + tail
    lane = lane_ids(8, LANES)
    fill = jnp.zeros((8, LANES - sh.window), F32)
    tile = jnp.concatenate([window, fill], axis=1)
    tile = jnp.where(lane == sh.window, gamma, tile)
    tile = jnp.where(lane == sh.window + 1, delta, tile)
    for d in range(sh.devices):
        for q in range(3):
            pay_ref[d, :, q * sh.points : (q + 1) * sh.points] = image[q : q + 1, :]
            at = 3 * sh.points + q * LANES
            pay_ref[d, :, at : at + LANES] = tile[q : q + 1, :]


def second_kernel(
    sh, recv_ref, row_ref, search_ref, spread_ref, rest_ref, gram_ref, image_ref,
    high0_ref, low0_ref, high1_ref, low1_ref,
    pay_ref, sums_ref, residual_ref, next_ref, product_ref,
):
    i, j = lax.axis_index("gx"), lax.axis_index("gy")
    lane = lane_ids(8, LANES)
    terms = jnp.zeros((8, LANES), F32)
    scalars = jnp.zeros((8, LANES), F32)
    fill = jnp.zeros((5, LANES), F32)
    for a in range(sh.nx):
        parts = []
        for q in range(3):
            at = 3 * sh.points + q * LANES
            total = recv_ref[a * sh.ny, :, at : at + LANES]
            for b in range(1, sh.ny):
                total = total + recv_ref[a * sh.ny + b, :, at : at + LANES]
            parts.append(total)
        tile = jnp.concatenate(parts + [fill], axis=0)
        scalars = scalars + tile
        start = min(max(a - 1, 0), sh.nx - 3) * sh.row_landmarks
        tile = jnp.where(lane < sh.window, tile, 0.0)
        terms = terms + (pltpu.roll(tile, start, axis=1) if start else tile)
    gamma = scalars[:, sh.window : sh.window + 1]
    delta = scalars[:, sh.window + 1 : sh.window + 2]
    row1 = lax.broadcasted_iota(jnp.int32, (8, 1), 0)
    alpha = jnp.where(row1 < 3, gamma / jnp.where(row1 < 3, delta, 1.0), 0.0)
    coarse = full_dot(terms, gram_ref[...], transposed=True)
    product_ref[...] = jnp.zeros_like(product_ref)
    rows, cols = sh.near_ids(i, j)
    zeros5 = jnp.zeros((5, sh.points), F32)
    for group in range(3):
        start = sh.window_start(rows[group])
        part = pltpu.roll(coarse, lax.rem(LANES - start, LANES), axis=1)[:, : sh.window]
        high_ref = high1_ref if group else high0_ref
        low_ref = low1_ref if group else low0_ref
        base = max(group - 1, 0) * 3
        for c in range(3):
            at = group * 3 + c
            source = rows[group] * sh.ny + cols[c]
            image = jnp.concatenate(
                [recv_ref[source, :, q * sh.points : (q + 1) * sh.points] for q in range(3)]
                + [zeros5],
                axis=0,
            )
            step = image * (1.0 / RIDGE_WEIGHT) + spread_dot(part, spread_ref[at], rest_ref[at])
            search = search_ref[at] - alpha * step
            if at == 0:
                next_ref[...] = search
            apply_column(sh, high_ref, low_ref, base + c, search, product_ref)
    residual = rhs_rows(row_ref[0], sh.points)
    image = image_ref[...]
    residual = residual - alpha * image
    residual_ref[...] = residual
    search = next_ref[...]
    product = product_ref[...] * (1.0 / KERN_SCALE) + RIDGE_WEIGHT * search
    product_ref[...] = product
    sums = [
        jnp.sum(residual * search, axis=1, keepdims=True),
        jnp.sum(search * product, axis=1, keepdims=True),
        jnp.sum(search * image, axis=1, keepdims=True)
        + jnp.sum(search_ref[0] * product, axis=1, keepdims=True),
    ]
    line = jnp.zeros((1, LANES), F32)
    lane1 = lane_ids(1, LANES)
    for at, value in enumerate(sums):
        for q in range(3):
            line = jnp.where(lane1 == 3 * at + q, value[q : q + 1, :], line)
    for d in range(sh.devices):
        pay_ref[d] = line
    sums_ref[...] = jnp.where(lane == 0, gamma, jnp.where(lane == 1, delta, 0.0))


def last_kernel(
    sh, recv_ref, sums_ref, search_ref, image_ref, residual_ref, next_ref, product_ref,
    solution_ref, final_ref,
):
    total = recv_ref[0]
    for d in range(1, sh.devices):
        total = total + recv_ref[d]
    row1 = lax.broadcasted_iota(jnp.int32, (8, 1), 0)
    good = row1 < 3

    def column(at):
        value = jnp.zeros((8, 1), F32)
        for q in range(3):
            value = jnp.where(row1 == q, total[:, 3 * at + q : 3 * at + q + 1], value)
        return value

    own = sums_ref[...]
    gamma, delta = own[:, 0:1], own[:, 1:2]
    gamma_new, inner, cross = column(0), column(1), column(2)
    safe_gamma = jnp.where(good, gamma, 1.0)
    safe_delta = jnp.where(good, delta, 1.0)
    alpha = gamma / safe_delta
    beta = gamma_new / safe_gamma
    curve = inner + beta * cross + beta * beta * delta
    step = gamma_new / jnp.where(good, curve, 1.0)
    direction = next_ref[...] + beta * search_ref[0]
    image = product_ref[...] + beta * image_ref[...]
    solution = alpha * search_ref[0] + step * direction
    residual = residual_ref[...] - step * image
    for layer in range(sh.layers):
        at = slice(layer * sh.slots, (layer + 1) * sh.slots)
        solution_ref[:, 0, 0, layer, :] = solution[0:3, at]
        final_ref[:, 0, 0, layer, :] = residual[0:3, at]


def local_fast(positions, counts, targets, landmark_index, coarse_matrix):
    both = ("gx", "gy")
    sh = Shape(positions, landmark_index, lax.axis_size("gx"), lax.axis_size("gy"))
    field = jax.ShapeDtypeStruct((8, sh.points), F32)
    vmem = pl.BlockSpec(memory_space=pltpu.VMEM)
    anyw = pl.BlockSpec(memory_space=pltpu.HBM)

    def call(kernel, name, out_shape, in_specs, cost=10**6, scratch=()):
        return pl.pallas_call(
            kernel,
            out_shape=out_shape,
            in_specs=in_specs,
            out_specs=jax.tree.map(lambda _: vmem, out_shape),
            scratch_shapes=scratch,
            name=name,
            compiler_params=pltpu.CompilerParams(vmem_limit_bytes=VMEM_BYTES),
            cost_estimate=pl.CostEstimate(flops=cost, bytes_accessed=10**5, transcendentals=0),
        )

    def part(kernel, *fixed):
        return functools.partial(kernel, sh, *fixed)

    def exchange(payload):
        return lax.all_to_all(payload, both, 0, 0)

    own = call(
        part(prepare_kernel),
        "prepare",
        field,
        [anyw] * 3,
        scratch=[
            pltpu.VMEM(positions.shape, F32),
            pltpu.SMEM(counts.shape, jnp.int32),
            pltpu.VMEM(targets.shape, F32),
            pltpu.SemaphoreType.DMA((3,)),
        ],
    )(positions, counts, targets)
    row = jnp.stack([own, swap(own, "gy", 0), swap(own, "gy", 1)])
    even, odd = swap(row, "gx", 0), swap(row, "gx", 1)

    def build(name, *groups):
        columns = 3 * len(groups)
        kern = jax.ShapeDtypeStruct((columns, sh.slots, sh.pairs), BF16)
        near = jax.ShapeDtypeStruct((columns, 48, sh.points), BF16)
        return call(
            part(build_kernel, len(groups)),
            name,
            (kern, kern, near),
            [vmem] * (1 + len(groups)),
            cost=len(groups) * 10**10,
        )(row, *groups)

    high0, low0, near0 = build("build_row", row)
    terms = call(
        part(terms_kernel),
        "terms",
        jax.ShapeDtypeStruct((sh.devices, 8, LANES), F32),
        [anyw, anyw, anyw, vmem, vmem, vmem],
        scratch=[
            pltpu.SMEM(landmark_index.shape, jnp.int32),
            pltpu.VMEM(coarse_matrix.shape, F32),
            pltpu.SemaphoreType.DMA((2,)),
        ],
    )(landmark_index, coarse_matrix, near0, row, even, odd)
    terms, even, odd = lax.optimization_barrier((exchange(terms), even, odd))
    high1, low1, near1 = build("build_rest", even, odd)

    wide = 3 * sh.points + 3 * LANES
    spread_shape = jax.ShapeDtypeStruct((9, sh.window, sh.points), BF16)
    payload, search, spread, rest, gram, image = call(
        part(first_kernel),
        "first",
        (
            jax.ShapeDtypeStruct((sh.devices, 1, wide), F32),
            jax.ShapeDtypeStruct((9, 8, sh.points), F32),
            spread_shape,
            spread_shape,
            jax.ShapeDtypeStruct((sh.landmarks, LANES), F32),
            field,
        ),
        [vmem] * 10,
        scratch=[pltpu.VMEM((sh.landmarks, 48), BF16)],
    )(row, even, odd, terms, near0, near1, high0, low0, high1, low1)
    images = exchange(payload)

    line = jax.ShapeDtypeStruct((sh.devices, 1, LANES), F32)
    tile = jax.ShapeDtypeStruct((8, LANES), F32)
    totals, sums, residual, following, product = call(
        part(second_kernel), "second", (line, tile, field, field, field), [vmem] * 11
    )(images, row, search, spread, rest, gram, image, high0, low0, high1, low1)
    totals = exchange(totals)

    out = jax.ShapeDtypeStruct(targets.shape, F32)
    return call(part(last_kernel), "last", (out, out), [vmem] * 7)(
        totals, sums, search, image, residual, following, product
    )


def fits_fast(positions, targets, landmark_index, coarse_matrix, nx, ny):
    owned = landmark_index.shape[2]
    return (
        nx * ny * owned == LANES
        and nx >= 3
        and targets.shape[0] == 3
        and coarse_matrix.shape[0] == 8 * (LANES // 2 // (ny * owned))
    )


def local(positions, counts, targets, landmark_index, coarse_matrix):
    nx, ny = lax.axis_size("gx"), lax.axis_size("gy")
    if fits_fast(positions, targets, landmark_index, coarse_matrix, nx, ny):
        return local_fast(positions, counts, targets, landmark_index, coarse_matrix)
    return local_plain(positions, counts, targets, landmark_index, coarse_matrix)


def solution(mesh):
    return jax.shard_map(
        local,
        mesh=mesh,
        in_specs=(
            P(None, "gx", "gy", None, None),
            P("gx", "gy", None),
            P(None, "gx", "gy", None, None),
            P(),
            P("gy", "gx"),
        ),
        out_specs=(P(None, "gx", "gy", None, None), P(None, "gx", "gy", None, None)),
        check_vma=False,
    )
```

```python
import functools

import jax
import jax.numpy as jnp
from jax import lax
from jax.experimental import pallas as pl
from jax.experimental.pallas import tpu as pltpu
from jax.sharding import PartitionSpec as P

ITERS = 2


RIDGE_WEIGHT = 2.0
HIGHEST_PRECISION = lax.Precision.HIGHEST

F32 = jnp.float32
BF16 = jnp.bfloat16
LANES = 128
FAR = 4096.0
KERN_SCALE = 256.0
VMEM_BYTES = 8 * 2**20


def with_halo(x, sides, width):
    for axis, dim in sides:
        peers, length = (lax.axis_size(axis), x.shape[dim])
        up = [(i, (i + 1) % peers) for i in range(peers - 1)]
        down = [(j, i) for i, j in up]
        last = lax.slice_in_dim(x, length - width, length, axis=dim)
        leading = lax.slice_in_dim(x, 0, width, axis=dim)
        before = lax.ppermute(last, axis, up)
        after = lax.ppermute(leading, axis, down)
        x = jnp.concatenate([before, x, after], axis=dim)
    return x


def wendland(points_a, points_b):
    square_sum = jnp.zeros((points_a.shape[1], points_b.shape[1]), jnp.float32)
    for coord in range(3):
        offset = points_a[coord][:, None] - points_b[coord][None, :]
        square_sum = square_sum + offset * offset
    distance = jnp.sqrt(square_sum)
    remain = jnp.maximum(1.0 - distance, 0.0)
    remain = remain * remain
    return remain * remain * (4.0 * distance + 1.0)


def cell_rim(field):
    return with_halo(field, (("gx", 1), ("gy", 2)), 1)


def inner_sums(left, right):
    return jnp.sum(left * right, axis=(1, 2, 3, 4))


def per_component(values):
    return values[:, None, None, None, None]


def global_inner(values):
    return lax.psum(values, ("gx", "gy"))


def local_plain(positions, counts, targets, landmark_index, coarse_matrix):
    components = targets.shape[0]
    layer_count = positions.shape[3]
    slot_count = positions.shape[4]
    owned_count = landmark_index.shape[2]
    column_points = layer_count * slot_count
    slot_ids = jnp.arange(slot_count, dtype=jnp.int32)
    live_mask = (slot_ids[None, None, None, :] < counts[:, :, :, None]).astype(jnp.float32)
    live_flat = live_mask.reshape(1, column_points)
    rhs_field = live_mask[None] * targets
    ext_pos = cell_rim(positions)
    ext_cloud = ext_pos.reshape(3, 9 * column_points)
    own_points = positions.reshape(3, column_points)
    row_index = lax.axis_index("gx")
    col_index = lax.axis_index("gy")
    three_ids = jnp.arange(3, dtype=jnp.int32)
    near_rows = jnp.clip(row_index + three_ids - 1, 0, lax.axis_size("gx") - 1)
    near_cols = jnp.clip(col_index + three_ids - 1, 0, lax.axis_size("gy") - 1)
    near_index = landmark_index[near_rows[:, None], near_cols[None, :], :]
    ext_flat = ext_pos.reshape(3, 3, 3, column_points)
    near_pos = jnp.take_along_axis(ext_flat, near_index[None], axis=3)
    landmark_pos = near_pos[:, 1, 1, :]
    spread_kernel = wendland(own_points, near_pos.reshape(3, 9 * owned_count))

    def coarse_solve(terms):
        row_terms = lax.all_gather(terms, "gy", axis=0, tiled=True)
        return lax.psum_scatter(
            jnp.dot(coarse_matrix, row_terms, precision=HIGHEST_PRECISION),
            "gx",
            scatter_dimension=0,
            tiled=True,
        )

    def landmark_sums(vector):
        gather_kernel = wendland(landmark_pos, ext_cloud)
        ext_vec = cell_rim(vector).reshape(components, 9 * column_points)
        return jnp.einsum("kn,qn->kq", gather_kernel, ext_vec, precision=HIGHEST_PRECISION)

    def precondition(vector):
        terms = landmark_sums(vector)
        coarse = coarse_solve(terms)
        near_coarse = with_halo(
            coarse.reshape(1, 1, owned_count, components), (("gx", 0), ("gy", 1)), 1
        )
        near_coarse = near_coarse.reshape(9 * owned_count, components)
        spread = jnp.einsum("nm,mq->qn", spread_kernel, near_coarse, precision=HIGHEST_PRECISION)
        return vector / RIDGE_WEIGHT + (live_flat * spread).reshape(vector.shape)

    solution = jnp.zeros_like(rhs_field)
    residual = rhs_field
    search = precondition(residual)
    gamma = global_inner(inner_sums(residual, search))
    direction = search
    for iteration in range(ITERS):
        operator_ext_vec = cell_rim(direction)
        layer_out = []
        for layer in range(layer_count):
            low_layer = max(layer - 1, 0)
            high_layer = min(layer + 2, layer_count)
            near_points = ext_pos[:, :, :, low_layer:high_layer, :].reshape(3, -1)
            near_values = operator_ext_vec[:, :, :, low_layer:high_layer, :].reshape(components, -1)
            kern = wendland(positions[:, 0, 0, layer, :], near_points)
            layer_out.append(
                jnp.einsum("bn,qn->qb", kern, near_values, precision=HIGHEST_PRECISION)
            )
        product = jnp.stack(layer_out, axis=1).reshape(direction.shape)
        image = live_mask[None] * product + RIDGE_WEIGHT * direction
        alpha = gamma / global_inner(inner_sums(direction, image))
        solution = solution + per_component(alpha) * direction
        residual = residual - per_component(alpha) * image
        if iteration + 1 < ITERS:
            search = precondition(residual)
            gamma_new = global_inner(inner_sums(residual, search))
            direction = search + per_component(gamma_new / gamma) * direction
            gamma = gamma_new
    return (solution, residual)


def row_ids(lanes):
    return lax.broadcasted_iota(jnp.int32, (8, lanes), 0)


def lane_ids(rows, lanes):
    return lax.broadcasted_iota(jnp.int32, (rows, lanes), 1)


def split_three(values):
    high = values.astype(BF16).astype(F32)
    rest = values - high
    middle = rest.astype(BF16).astype(F32)
    low = (rest - middle).astype(BF16).astype(F32)
    return high, middle, low


def centred(column, centre):
    row = row_ids(column.shape[1])
    shift = jnp.where(row == 0, centre[0], jnp.where(row == 1, centre[1], centre[2]))
    xyz = jnp.where(row < 3, column - shift, 0.0)
    norm = 16.0 * jnp.sum(xyz * xyz, axis=0, keepdims=True)
    return row, xyz, norm + (1.0 - column[6:7, :]) * FAR


def near_features(column, centre):
    row, xyz, norm = centred(column, centre)
    high, middle, low = split_three(
        jnp.where(row == 3, norm, jnp.where(row == 4, 1.0, xyz))
    )
    return jnp.concatenate([high, middle, low, high, middle, high], axis=0)


def own_features(column, centre):
    row, xyz, norm = centred(column, centre)
    high, middle, low = split_three(
        jnp.where(row == 3, 1.0, jnp.where(row == 4, norm, -32.0 * xyz))
    )
    return jnp.concatenate([high, high, high, middle, middle, low], axis=0)


def scaled_wendland(square16):
    square16 = jnp.maximum(square16, 1e-6)
    four = square16 * lax.rsqrt(square16)
    remain = jnp.maximum(4.0 - four, 0.0)
    remain = remain * remain
    return remain * remain * (four + 1.0)


def bf16_dot(left, right):
    return jnp.dot(left, right, preferred_element_type=F32)


def full_dot(left, right, transposed=False):
    dims = (((1,), (1 if transposed else 0,)), ((), ()))
    return lax.dot_general(
        left, right, dims, precision=HIGHEST_PRECISION, preferred_element_type=F32
    )


def swap_partner(index, peers, odd):
    step = 1 - 2 * lax.rem(index + odd, 2)
    partner = index + step
    good = jnp.logical_and(partner >= 0, partner < peers)
    return jnp.where(good, partner, index)


def swap(x, axis, odd):
    peers = lax.axis_size(axis)
    pairs = []
    for i in range(odd, peers - 1, 2):
        pairs += [(i, i + 1), (i + 1, i)]
    return lax.ppermute(x, axis, pairs)


class Shape:
    def __init__(self, positions, landmark_index, nx, ny):
        self.nx, self.ny = nx, ny
        self.devices = nx * ny
        self.layers, self.slots = positions.shape[3], positions.shape[4]
        self.points = self.layers * self.slots
        self.owned = landmark_index.shape[2]
        self.row_landmarks = ny * self.owned
        self.landmarks = nx * self.row_landmarks
        self.window = 3 * self.row_landmarks
        self.blocks = []
        offset = 0
        for layer in range(self.layers):
            low, high = max(layer - 1, 0), min(layer + 2, self.layers)
            self.blocks.append((low, high, offset))
            offset += (high - low) * self.slots
        self.pairs = offset

    def centre(self, i, j):
        return (i.astype(F32) + 0.5, j.astype(F32) + 0.5, 0.5 * self.layers)

    def window_start(self, i):
        start = jnp.clip(i - 1, 0, self.nx - 3) * self.row_landmarks
        return pl.multiple_of(start, self.row_landmarks)

    def near_ids(self, i, j):
        rows = [i, swap_partner(i, self.nx, 0), swap_partner(i, self.nx, 1)]
        cols = [j, swap_partner(j, self.ny, 0), swap_partner(j, self.ny, 1)]
        return rows, cols


def prepare_kernel(
    sh, pos_hbm, counts_hbm, tgt_hbm, index_hbm, coarse_hbm, own_ref, mark_ref, block_ref,
    pos_ref, counts_ref, tgt_ref, index_ref, coarse_ref, turned_ref, sems,
):
    copies = [
        pltpu.make_async_copy(source, target, sems.at[at])
        for at, (source, target) in enumerate(
            (
                (counts_hbm, counts_ref),
                (pos_hbm, pos_ref),
                (tgt_hbm, tgt_ref),
                (index_hbm, index_ref),
                (coarse_hbm, coarse_ref),
            )
        )
    ]
    for copy in copies:
        copy.start()
    for copy in copies:
        copy.wait()
    slot = lane_ids(1, sh.slots)
    for layer in range(sh.layers):
        live = (slot < counts_ref[0, 0, layer]).astype(F32)
        at = pl.ds(layer * sh.slots, sh.slots)
        own_ref[0:3, at] = pos_ref[:, 0, 0, layer, :]
        own_ref[3:6, at] = live * tgt_ref[:, 0, 0, layer, :]
        own_ref[6:7, at] = live
        own_ref[7:8, at] = jnp.zeros_like(live)
    i, j = lax.axis_index("gx"), lax.axis_index("gy")
    own = own_ref[...]
    lane = lane_ids(8, sh.points)
    lane8 = lane_ids(8, LANES)
    marks = jnp.zeros((8, LANES), F32)
    for k in range(sh.owned):
        hit = jnp.where(lane == index_ref[j, k, i], own, 0.0)
        marks = jnp.where(lane8 == k, jnp.sum(hit, axis=1, keepdims=True), marks)
    mark_ref[...] = marks
    count, width = coarse_ref.shape[1], coarse_ref.shape[0]
    fill = jnp.zeros((width, LANES - count), F32)
    turned_ref[...] = jnp.concatenate([coarse_ref[...], fill], axis=1).T
    groups = LANES // 2 // width
    pieces = [turned_ref[pl.ds(g, 8, stride=groups), :] for g in range(groups)]
    block_ref[...] = jnp.concatenate(pieces + pieces, axis=1)


def terms_kernel(
    sh, after_ref, mark_ref, block_ref, row_ref, even_ref, odd_ref, pay_ref,
):
    i, j = lax.axis_index("gx"), lax.axis_index("gy")
    row1 = lax.broadcasted_iota(jnp.int32, (8, 1), 0)
    marks = [mark_ref[:, k : k + 1] for k in range(sh.owned)]
    coords = []
    for coord in range(3):
        column = jnp.zeros((8, 1), F32)
        for k in range(sh.owned):
            column = jnp.where(row1 == k, marks[k][coord : coord + 1, :], column)
        coords.append(column)

    def add_column(column, sums):
        square = jnp.zeros((8, sh.points), F32)
        for coord in range(3):
            offset = column[coord : coord + 1, :] - coords[coord]
            square = square + offset * offset
        kern = scaled_wendland(16.0 * square)
        return tuple(
            total + kern * column[3 + q : 4 + q, :] for q, total in enumerate(sums)
        )

    sums = tuple(jnp.zeros((8, sh.points), F32) for _ in range(3))
    for ref in (row_ref, even_ref, odd_ref):
        sums = lax.fori_loop(0, 3, lambda c, s, ref=ref: add_column(ref[c], s), sums)
    terms = [jnp.sum(s, axis=1, keepdims=True) * (1.0 / KERN_SCALE) for s in sums]
    lane8 = lane_ids(8, LANES)
    row8 = row_ids(LANES)
    half = LANES // 2
    first = (i * sh.ny + j) * sh.owned
    tile = jnp.zeros((8, LANES), F32)
    for k in range(sh.owned):
        column = jnp.where(row1 < 3, marks[k], 0.0)
        for q in range(3):
            column = jnp.where(row1 == 3 + q, terms[q][k : k + 1, :], column)
        tile = jnp.where(lane8 == first + k, column, tile)
    block = block_ref[...]
    own_half = (lane8 >= half) == (first >= half)
    tile = jnp.where(own_half, tile, block)
    for d in range(sh.devices):
        pay_ref[d] = tile


def build_kernel(sh, count, row_ref, *refs):
    group_refs, (high_ref, low_ref, near_ref) = refs[: count], refs[count :]
    centre = sh.centre(lax.axis_index("gx"), lax.axis_index("gy"))
    own = own_features(row_ref[0], centre).astype(BF16)

    def one(ref, group, c):
        features = near_features(ref[c], centre).astype(BF16)
        near_ref[group * 3 + c] = features
        near = features.T
        for layer, (low, high, offset) in enumerate(sh.blocks):
            lhs = near[layer * sh.slots : (layer + 1) * sh.slots]
            for target in range(low, high):
                square = bf16_dot(lhs, own[:, target * sh.slots : (target + 1) * sh.slots])
                kern = scaled_wendland(square)
                head = kern.astype(BF16)
                at = offset + (target - low) * sh.slots
                high_ref[group * 3 + c, :, at : at + sh.slots] = head
                head = high_ref[group * 3 + c, :, at : at + sh.slots]
                low_ref[group * 3 + c, :, at : at + sh.slots] = (
                    kern - head.astype(F32)
                ).astype(BF16)
        return 0

    for group, ref in enumerate(group_refs):
        lax.fori_loop(0, 3, lambda c, _, ref=ref, group=group: one(ref, group, c), 0)


def split_rows(values):
    head = values.astype(BF16)
    tail = values - head.astype(F32)
    return head, jnp.concatenate([head.astype(F32), tail], axis=0).astype(BF16)


def apply_column(sh, high_ref, low_ref, c, values, out_ref):
    head, both = split_rows(values)
    for layer, (low, high, offset) in enumerate(sh.blocks):
        at = slice(layer * sh.slots, (layer + 1) * sh.slots)
        width = (high - low) * sh.slots
        main = bf16_dot(both[:, at], high_ref[c, :, offset : offset + width])
        rest = bf16_dot(head[:, at], low_ref[c, :, offset : offset + width])
        out_ref[:, low * sh.slots : high * sh.slots] += main[:8] + main[8:] + rest


def spread_dot(part, high, low):
    head, both = split_rows(part)
    main = bf16_dot(both, high)
    return main[:8] + main[8:] + bf16_dot(head, low)


def gathered_matrix(sh, recv_ref, gram_ref):
    width = sh.row_landmarks
    half = LANES // 2
    groups = half // width
    lane = lane_ids(sh.ny * 8, LANES)
    for g in range(groups):
        total = jnp.zeros((sh.ny * 8, LANES), F32)
        for i in range(sh.nx):
            tiles = jnp.concatenate([recv_ref[i * sh.ny + j] for j in range(sh.ny)], axis=0)
            base = half if i * width < half else 0
            shift = (i * width - base - g * width) % LANES
            if shift:
                tiles = pltpu.roll(tiles, shift, axis=1)
            keep = jnp.logical_and(lane >= i * width, lane < (i + 1) * width)
            total = jnp.where(keep, tiles, total)
        for j in range(sh.ny):
            for r in range(8):
                p = groups * r + g
                at = (p // sh.owned) * width + j * sh.owned + p % sh.owned
                gram_ref[at : at + 1, :] = total[j * 8 + r : j * 8 + r + 1, :]


def rhs_rows(column, lanes):
    return jnp.where(
        row_ids(lanes) < 3, jnp.concatenate([column[3:8], column[0:3]], axis=0), 0.0
    )


def first_kernel(
    sh, row_ref, even_ref, odd_ref, recv_ref, near0_ref, near1_ref,
    high0_ref, low0_ref, high1_ref, low1_ref,
    pay_ref, search_ref, spread_ref, rest_ref, gram_ref, image_ref, mark_ref,
):
    i, j = lax.axis_index("gx"), lax.axis_index("gy")
    centre = sh.centre(i, j)
    half = LANES // 2
    totals = [jnp.zeros((8, LANES), F32), jnp.zeros((8, LANES), F32)]
    for d in range(sh.devices):
        side = 0 if d * sh.owned < half else 1
        totals[side] = totals[side] + recv_ref[d]
    gathered = jnp.where(lane_ids(8, LANES) < half, totals[0], totals[1])
    gathered = jnp.where(row_ids(LANES) == 6, 1.0, gathered)
    gathered_matrix(sh, recv_ref, gram_ref)
    mark_ref[...] = own_features(gathered, centre).T.astype(BF16)
    coarse = full_dot(rhs_rows(gathered, LANES), gram_ref[...], transposed=True)
    image_ref[...] = jnp.zeros_like(image_ref)
    rows, _ = sh.near_ids(i, j)
    for group, ref in enumerate((row_ref, even_ref, odd_ref)):
        start = sh.window_start(rows[group])
        marks = mark_ref[pl.ds(start, sh.window), :]
        part = pltpu.roll(coarse, lax.rem(LANES - start, LANES), axis=1)[:, : sh.window]
        near_ref = near1_ref if group else near0_ref
        high_ref = high1_ref if group else high0_ref
        low_ref = low1_ref if group else low0_ref
        base = max(group - 1, 0) * 3

        for c in range(3):
            spread = scaled_wendland(bf16_dot(marks, near_ref[base + c])) * (1.0 / KERN_SCALE)
            head = spread.astype(BF16)
            rest = (spread - head.astype(F32)).astype(BF16)
            spread_ref[group * 3 + c] = head
            rest_ref[group * 3 + c] = rest
            residual = rhs_rows(ref[c], sh.points)
            search = residual * (1.0 / RIDGE_WEIGHT) + spread_dot(part, head, rest)
            search_ref[group * 3 + c] = search
            apply_column(sh, high_ref, low_ref, base + c, search, image_ref)
    residual = rhs_rows(row_ref[0], sh.points)
    search = search_ref[0]
    image = image_ref[...] * (1.0 / KERN_SCALE) + RIDGE_WEIGHT * search
    image_ref[...] = image
    gamma = jnp.sum(residual * search, axis=1, keepdims=True)
    delta = jnp.sum(search * image, axis=1, keepdims=True)
    head, both = split_rows(image)
    across = (((1,), (1,)), ((), ()))
    main = lax.dot_general(both, spread_ref[0], across, preferred_element_type=F32)
    tail = lax.dot_general(head, rest_ref[0], across, preferred_element_type=F32)
    window = main[:8] + main[8:] + tail
    lane = lane_ids(8, LANES)
    fill = jnp.zeros((8, LANES - sh.window), F32)
    tile = jnp.concatenate([window, fill], axis=1)
    tile = jnp.where(lane == sh.window, gamma, tile)
    tile = jnp.where(lane == sh.window + 1, delta, tile)
    for d in range(sh.devices):
        for q in range(3):
            pay_ref[d, :, q * sh.points : (q + 1) * sh.points] = image[q : q + 1, :]
            at = 3 * sh.points + q * LANES
            pay_ref[d, :, at : at + LANES] = tile[q : q + 1, :]


def second_kernel(
    sh, recv_ref, row_ref, search_ref, spread_ref, rest_ref, gram_ref, image_ref,
    high0_ref, low0_ref, high1_ref, low1_ref,
    pay_ref, sums_ref, residual_ref, next_ref, product_ref,
):
    i, j = lax.axis_index("gx"), lax.axis_index("gy")
    lane = lane_ids(8, LANES)
    terms = jnp.zeros((8, LANES), F32)
    scalars = jnp.zeros((8, LANES), F32)
    fill = jnp.zeros((5, LANES), F32)
    for a in range(sh.nx):
        parts = []
        for q in range(3):
            at = 3 * sh.points + q * LANES
            total = recv_ref[a * sh.ny, :, at : at + LANES]
            for b in range(1, sh.ny):
                total = total + recv_ref[a * sh.ny + b, :, at : at + LANES]
            parts.append(total)
        tile = jnp.concatenate(parts + [fill], axis=0)
        scalars = scalars + tile
        start = min(max(a - 1, 0), sh.nx - 3) * sh.row_landmarks
        tile = jnp.where(lane < sh.window, tile, 0.0)
        terms = terms + (pltpu.roll(tile, start, axis=1) if start else tile)
    gamma = scalars[:, sh.window : sh.window + 1]
    delta = scalars[:, sh.window + 1 : sh.window + 2]
    row1 = lax.broadcasted_iota(jnp.int32, (8, 1), 0)
    alpha = jnp.where(row1 < 3, gamma / jnp.where(row1 < 3, delta, 1.0), 0.0)
    coarse = full_dot(terms, gram_ref[...], transposed=True)
    product_ref[...] = jnp.zeros_like(product_ref)
    rows, cols = sh.near_ids(i, j)
    zeros5 = jnp.zeros((5, sh.points), F32)
    for group in range(3):
        start = sh.window_start(rows[group])
        part = pltpu.roll(coarse, lax.rem(LANES - start, LANES), axis=1)[:, : sh.window]
        high_ref = high1_ref if group else high0_ref
        low_ref = low1_ref if group else low0_ref
        base = max(group - 1, 0) * 3
        for c in range(3):
            at = group * 3 + c
            source = rows[group] * sh.ny + cols[c]
            image = jnp.concatenate(
                [recv_ref[source, :, q * sh.points : (q + 1) * sh.points] for q in range(3)]
                + [zeros5],
                axis=0,
            )
            step = image * (1.0 / RIDGE_WEIGHT) + spread_dot(part, spread_ref[at], rest_ref[at])
            search = search_ref[at] - alpha * step
            if at == 0:
                next_ref[...] = search
            apply_column(sh, high_ref, low_ref, base + c, search, product_ref)
    residual = rhs_rows(row_ref[0], sh.points)
    image = image_ref[...]
    residual = residual - alpha * image
    residual_ref[...] = residual
    search = next_ref[...]
    product = product_ref[...] * (1.0 / KERN_SCALE) + RIDGE_WEIGHT * search
    product_ref[...] = product
    sums = [
        jnp.sum(residual * search, axis=1, keepdims=True),
        jnp.sum(search * product, axis=1, keepdims=True),
        jnp.sum(search * image, axis=1, keepdims=True)
        + jnp.sum(search_ref[0] * product, axis=1, keepdims=True),
    ]
    line = jnp.zeros((1, LANES), F32)
    lane1 = lane_ids(1, LANES)
    for at, value in enumerate(sums):
        for q in range(3):
            line = jnp.where(lane1 == 3 * at + q, value[q : q + 1, :], line)
    for d in range(sh.devices):
        pay_ref[d] = line
    sums_ref[...] = jnp.where(lane == 0, gamma, jnp.where(lane == 1, delta, 0.0))


def last_kernel(
    sh, recv_ref, sums_ref, search_ref, image_ref, residual_ref, next_ref, product_ref,
    solution_ref, final_ref,
):
    total = recv_ref[0]
    for d in range(1, sh.devices):
        total = total + recv_ref[d]
    row1 = lax.broadcasted_iota(jnp.int32, (8, 1), 0)
    good = row1 < 3

    def column(at):
        value = jnp.zeros((8, 1), F32)
        for q in range(3):
            value = jnp.where(row1 == q, total[:, 3 * at + q : 3 * at + q + 1], value)
        return value

    own = sums_ref[...]
    gamma, delta = own[:, 0:1], own[:, 1:2]
    gamma_new, inner, cross = column(0), column(1), column(2)
    safe_gamma = jnp.where(good, gamma, 1.0)
    safe_delta = jnp.where(good, delta, 1.0)
    alpha = gamma / safe_delta
    beta = gamma_new / safe_gamma
    curve = inner + beta * cross + beta * beta * delta
    step = gamma_new / jnp.where(good, curve, 1.0)
    direction = next_ref[...] + beta * search_ref[0]
    image = product_ref[...] + beta * image_ref[...]
    solution = alpha * search_ref[0] + step * direction
    residual = residual_ref[...] - step * image
    for layer in range(sh.layers):
        at = slice(layer * sh.slots, (layer + 1) * sh.slots)
        solution_ref[:, 0, 0, layer, :] = solution[0:3, at]
        final_ref[:, 0, 0, layer, :] = residual[0:3, at]


def local_fast(positions, counts, targets, landmark_index, coarse_matrix):
    both = ("gx", "gy")
    sh = Shape(positions, landmark_index, lax.axis_size("gx"), lax.axis_size("gy"))
    field = jax.ShapeDtypeStruct((8, sh.points), F32)
    vmem = pl.BlockSpec(memory_space=pltpu.VMEM)
    anyw = pl.BlockSpec(memory_space=pltpu.HBM)

    def call(kernel, name, out_shape, in_specs, cost=10**6, scratch=()):
        return pl.pallas_call(
            kernel,
            out_shape=out_shape,
            in_specs=in_specs,
            out_specs=jax.tree.map(lambda _: vmem, out_shape),
            scratch_shapes=scratch,
            name=name,
            compiler_params=pltpu.CompilerParams(vmem_limit_bytes=VMEM_BYTES),
            cost_estimate=pl.CostEstimate(flops=cost, bytes_accessed=10**5, transcendentals=0),
        )

    def part(kernel, *fixed):
        return functools.partial(kernel, sh, *fixed)

    def exchange(payload):
        return lax.all_to_all(payload, both, 0, 0)

    index = jnp.transpose(landmark_index, (1, 2, 0))
    turned = jnp.transpose(coarse_matrix)
    tile = jax.ShapeDtypeStruct((8, LANES), F32)
    own, marks, block = call(
        part(prepare_kernel),
        "prepare",
        (field, tile, tile),
        [anyw] * 5,
        scratch=[
            pltpu.VMEM(positions.shape, F32),
            pltpu.SMEM(counts.shape, jnp.int32),
            pltpu.VMEM(targets.shape, F32),
            pltpu.SMEM(index.shape, jnp.int32),
            pltpu.VMEM(turned.shape, F32),
            pltpu.VMEM((LANES, turned.shape[0]), F32),
            pltpu.SemaphoreType.DMA((5,)),
        ],
    )(*(pltpu.with_memory_space_constraint(x, pltpu.HBM)
        for x in (positions, counts, targets, index, turned)))
    row = jnp.stack([own, swap(own, "gy", 0), swap(own, "gy", 1)])
    even, odd = swap(row, "gx", 0), swap(row, "gx", 1)

    def build(name, *groups):
        columns = 3 * len(groups)
        kern = jax.ShapeDtypeStruct((columns, sh.slots, sh.pairs), BF16)
        near = jax.ShapeDtypeStruct((columns, 48, sh.points), BF16)
        return call(
            part(build_kernel, len(groups)),
            name,
            (kern, kern, near),
            [vmem] * (1 + len(groups)),
            cost=len(groups) * 10**10,
        )(row, *groups)

    high0, low0, near0 = build("build_row", row)
    terms = call(
        part(terms_kernel),
        "terms",
        jax.ShapeDtypeStruct((sh.devices, 8, LANES), F32),
        [anyw] + [vmem] * 5,
    )(near0, marks, block, row, even, odd)
    terms, even, odd = lax.optimization_barrier((exchange(terms), even, odd))
    high1, low1, near1 = build("build_rest", even, odd)

    wide = 3 * sh.points + 3 * LANES
    spread_shape = jax.ShapeDtypeStruct((9, sh.window, sh.points), BF16)
    payload, search, spread, rest, gram, image = call(
        part(first_kernel),
        "first",
        (
            jax.ShapeDtypeStruct((sh.devices, 1, wide), F32),
            jax.ShapeDtypeStruct((9, 8, sh.points), F32),
            spread_shape,
            spread_shape,
            jax.ShapeDtypeStruct((sh.landmarks, LANES), F32),
            field,
        ),
        [vmem] * 10,
        scratch=[pltpu.VMEM((sh.landmarks, 48), BF16)],
    )(row, even, odd, terms, near0, near1, high0, low0, high1, low1)
    images = exchange(payload)

    line = jax.ShapeDtypeStruct((sh.devices, 1, LANES), F32)
    totals, sums, residual, following, product = call(
        part(second_kernel), "second", (line, tile, field, field, field), [vmem] * 11
    )(images, row, search, spread, rest, gram, image, high0, low0, high1, low1)
    totals = exchange(totals)

    out = jax.ShapeDtypeStruct(targets.shape, F32)
    return call(part(last_kernel), "last", (out, out), [vmem] * 7)(
        totals, sums, search, image, residual, following, product
    )


def fits_fast(positions, targets, landmark_index, coarse_matrix, nx, ny):
    owned = landmark_index.shape[2]
    return (
        nx * ny * owned == LANES
        and nx >= 3
        and targets.shape[0] == 3
        and coarse_matrix.shape[0] == 8 * (LANES // 2 // (ny * owned))
    )


def local(positions, counts, targets, landmark_index, coarse_matrix):
    nx, ny = lax.axis_size("gx"), lax.axis_size("gy")
    if fits_fast(positions, targets, landmark_index, coarse_matrix, nx, ny):
        return local_fast(positions, counts, targets, landmark_index, coarse_matrix)
    return local_plain(positions, counts, targets, landmark_index, coarse_matrix)


def solution(mesh):
    return jax.shard_map(
        local,
        mesh=mesh,
        in_specs=(
            P(None, "gx", "gy", None, None),
            P("gx", "gy", None),
            P(None, "gx", "gy", None, None),
            P(),
            P("gy", "gx"),
        ),
        out_specs=(P(None, "gx", "gy", None, None), P(None, "gx", "gy", None, None)),
        check_vma=False,
    )
```

```python
import functools

import jax
import jax.numpy as jnp
from jax import lax
from jax.experimental import pallas as pl
from jax.experimental.pallas import tpu as pltpu
from jax.sharding import PartitionSpec as P

ITERS = 2


RIDGE_WEIGHT = 2.0
HIGHEST_PRECISION = lax.Precision.HIGHEST

F32 = jnp.float32
BF16 = jnp.bfloat16
LANES = 128
FAR = 4096.0
KERN_SCALE = 256.0
VMEM_BYTES = 8 * 2**20


def with_halo(x, sides, width):
    for axis, dim in sides:
        peers, length = (lax.axis_size(axis), x.shape[dim])
        up = [(i, (i + 1) % peers) for i in range(peers - 1)]
        down = [(j, i) for i, j in up]
        last = lax.slice_in_dim(x, length - width, length, axis=dim)
        leading = lax.slice_in_dim(x, 0, width, axis=dim)
        before = lax.ppermute(last, axis, up)
        after = lax.ppermute(leading, axis, down)
        x = jnp.concatenate([before, x, after], axis=dim)
    return x


def wendland(points_a, points_b):
    square_sum = jnp.zeros((points_a.shape[1], points_b.shape[1]), jnp.float32)
    for coord in range(3):
        offset = points_a[coord][:, None] - points_b[coord][None, :]
        square_sum = square_sum + offset * offset
    distance = jnp.sqrt(square_sum)
    remain = jnp.maximum(1.0 - distance, 0.0)
    remain = remain * remain
    return remain * remain * (4.0 * distance + 1.0)


def cell_rim(field):
    return with_halo(field, (("gx", 1), ("gy", 2)), 1)


def inner_sums(left, right):
    return jnp.sum(left * right, axis=(1, 2, 3, 4))


def per_component(values):
    return values[:, None, None, None, None]


def global_inner(values):
    return lax.psum(values, ("gx", "gy"))


def local_plain(positions, counts, targets, landmark_index, coarse_matrix):
    components = targets.shape[0]
    layer_count = positions.shape[3]
    slot_count = positions.shape[4]
    owned_count = landmark_index.shape[2]
    column_points = layer_count * slot_count
    slot_ids = jnp.arange(slot_count, dtype=jnp.int32)
    live_mask = (slot_ids[None, None, None, :] < counts[:, :, :, None]).astype(jnp.float32)
    live_flat = live_mask.reshape(1, column_points)
    rhs_field = live_mask[None] * targets
    ext_pos = cell_rim(positions)
    ext_cloud = ext_pos.reshape(3, 9 * column_points)
    own_points = positions.reshape(3, column_points)
    row_index = lax.axis_index("gx")
    col_index = lax.axis_index("gy")
    three_ids = jnp.arange(3, dtype=jnp.int32)
    near_rows = jnp.clip(row_index + three_ids - 1, 0, lax.axis_size("gx") - 1)
    near_cols = jnp.clip(col_index + three_ids - 1, 0, lax.axis_size("gy") - 1)
    near_index = landmark_index[near_rows[:, None], near_cols[None, :], :]
    ext_flat = ext_pos.reshape(3, 3, 3, column_points)
    near_pos = jnp.take_along_axis(ext_flat, near_index[None], axis=3)
    landmark_pos = near_pos[:, 1, 1, :]
    spread_kernel = wendland(own_points, near_pos.reshape(3, 9 * owned_count))

    def coarse_solve(terms):
        row_terms = lax.all_gather(terms, "gy", axis=0, tiled=True)
        return lax.psum_scatter(
            jnp.dot(coarse_matrix, row_terms, precision=HIGHEST_PRECISION),
            "gx",
            scatter_dimension=0,
            tiled=True,
        )

    def landmark_sums(vector):
        gather_kernel = wendland(landmark_pos, ext_cloud)
        ext_vec = cell_rim(vector).reshape(components, 9 * column_points)
        return jnp.einsum("kn,qn->kq", gather_kernel, ext_vec, precision=HIGHEST_PRECISION)

    def precondition(vector):
        terms = landmark_sums(vector)
        coarse = coarse_solve(terms)
        near_coarse = with_halo(
            coarse.reshape(1, 1, owned_count, components), (("gx", 0), ("gy", 1)), 1
        )
        near_coarse = near_coarse.reshape(9 * owned_count, components)
        spread = jnp.einsum("nm,mq->qn", spread_kernel, near_coarse, precision=HIGHEST_PRECISION)
        return vector / RIDGE_WEIGHT + (live_flat * spread).reshape(vector.shape)

    solution = jnp.zeros_like(rhs_field)
    residual = rhs_field
    search = precondition(residual)
    gamma = global_inner(inner_sums(residual, search))
    direction = search
    for iteration in range(ITERS):
        operator_ext_vec = cell_rim(direction)
        layer_out = []
        for layer in range(layer_count):
            low_layer = max(layer - 1, 0)
            high_layer = min(layer + 2, layer_count)
            near_points = ext_pos[:, :, :, low_layer:high_layer, :].reshape(3, -1)
            near_values = operator_ext_vec[:, :, :, low_layer:high_layer, :].reshape(components, -1)
            kern = wendland(positions[:, 0, 0, layer, :], near_points)
            layer_out.append(
                jnp.einsum("bn,qn->qb", kern, near_values, precision=HIGHEST_PRECISION)
            )
        product = jnp.stack(layer_out, axis=1).reshape(direction.shape)
        image = live_mask[None] * product + RIDGE_WEIGHT * direction
        alpha = gamma / global_inner(inner_sums(direction, image))
        solution = solution + per_component(alpha) * direction
        residual = residual - per_component(alpha) * image
        if iteration + 1 < ITERS:
            search = precondition(residual)
            gamma_new = global_inner(inner_sums(residual, search))
            direction = search + per_component(gamma_new / gamma) * direction
            gamma = gamma_new
    return (solution, residual)


def row_ids(lanes):
    return lax.broadcasted_iota(jnp.int32, (8, lanes), 0)


def lane_ids(rows, lanes):
    return lax.broadcasted_iota(jnp.int32, (rows, lanes), 1)


def split_three(values):
    high = values.astype(BF16).astype(F32)
    rest = values - high
    middle = rest.astype(BF16).astype(F32)
    low = (rest - middle).astype(BF16).astype(F32)
    return high, middle, low


def centred(column, centre):
    row = row_ids(column.shape[1])
    shift = jnp.where(row == 0, centre[0], jnp.where(row == 1, centre[1], centre[2]))
    xyz = jnp.where(row < 3, column - shift, 0.0)
    norm = 16.0 * jnp.sum(xyz * xyz, axis=0, keepdims=True)
    return row, xyz, norm + (1.0 - column[6:7, :]) * FAR


def near_features(column, centre):
    row, xyz, norm = centred(column, centre)
    high, middle, low = split_three(
        jnp.where(row == 3, norm, jnp.where(row == 4, 1.0, xyz))
    )
    return jnp.concatenate([high, middle, low, high, middle, high], axis=0)


def own_features(column, centre):
    row, xyz, norm = centred(column, centre)
    high, middle, low = split_three(
        jnp.where(row == 3, 1.0, jnp.where(row == 4, norm, -32.0 * xyz))
    )
    return jnp.concatenate([high, high, high, middle, middle, low], axis=0)


def scaled_wendland(square16):
    square16 = jnp.maximum(square16, 1e-6)
    four = square16 * lax.rsqrt(square16)
    remain = jnp.maximum(4.0 - four, 0.0)
    remain = remain * remain
    return remain * remain * (four + 1.0)


def bf16_dot(left, right):
    return jnp.dot(left, right, preferred_element_type=F32)


def full_dot(left, right, transposed=False):
    dims = (((1,), (1 if transposed else 0,)), ((), ()))
    return lax.dot_general(
        left, right, dims, precision=HIGHEST_PRECISION, preferred_element_type=F32
    )


def swap_partner(index, peers, odd):
    step = 1 - 2 * lax.rem(index + odd, 2)
    partner = index + step
    good = jnp.logical_and(partner >= 0, partner < peers)
    return jnp.where(good, partner, index)


def swap(x, axis, odd):
    peers = lax.axis_size(axis)
    pairs = []
    for i in range(odd, peers - 1, 2):
        pairs += [(i, i + 1), (i + 1, i)]
    return lax.ppermute(x, axis, pairs)


class Shape:
    def __init__(self, positions, landmark_index, nx, ny):
        self.nx, self.ny = nx, ny
        self.devices = nx * ny
        self.layers, self.slots = positions.shape[3], positions.shape[4]
        self.points = self.layers * self.slots
        self.owned = landmark_index.shape[2]
        self.row_landmarks = ny * self.owned
        self.landmarks = nx * self.row_landmarks
        self.window = 3 * self.row_landmarks
        self.blocks = []
        offset = 0
        for layer in range(self.layers):
            low, high = max(layer - 1, 0), min(layer + 2, self.layers)
            self.blocks.append((low, high, offset))
            offset += (high - low) * self.slots
        self.pairs = offset

    def centre(self, i, j):
        return (i.astype(F32) + 0.5, j.astype(F32) + 0.5, 0.5 * self.layers)

    def window_start(self, i):
        start = jnp.clip(i - 1, 0, self.nx - 3) * self.row_landmarks
        return pl.multiple_of(start, self.row_landmarks)

    def window_of(self, lanes, start):
        shift = lax.rem(LANES - start, LANES)
        return pltpu.roll(lanes, shift, axis=1)[:, : self.window]

    def near_ids(self, i, j):
        rows = [i, swap_partner(i, self.nx, 0), swap_partner(i, self.nx, 1)]
        cols = [j, swap_partner(j, self.ny, 0), swap_partner(j, self.ny, 1)]
        return rows, cols


def prepare_kernel(
    sh, pos_hbm, counts_hbm, tgt_hbm, index_hbm, coarse_hbm, own_ref, mark_ref, block_ref,
    pos_ref, counts_ref, tgt_ref, index_ref, coarse_ref, turned_ref, sems,
):
    copies = [
        pltpu.make_async_copy(source, target, sems.at[at])
        for at, (source, target) in enumerate(
            (
                (counts_hbm, counts_ref),
                (pos_hbm, pos_ref),
                (tgt_hbm, tgt_ref),
                (index_hbm, index_ref),
                (coarse_hbm, coarse_ref),
            )
        )
    ]
    for copy in copies:
        copy.start()
    for copy in copies:
        copy.wait()
    slot = lane_ids(1, sh.slots)
    for layer in range(sh.layers):
        live = (slot < counts_ref[0, 0, layer]).astype(F32)
        at = pl.ds(layer * sh.slots, sh.slots)
        own_ref[0:3, at] = pos_ref[:, 0, 0, layer, :]
        own_ref[3:6, at] = live * tgt_ref[:, 0, 0, layer, :]
        own_ref[6:7, at] = live
        own_ref[7:8, at] = jnp.zeros_like(live)
    i, j = lax.axis_index("gx"), lax.axis_index("gy")
    own = own_ref[...]
    lane = lane_ids(8, sh.points)
    lane8 = lane_ids(8, LANES)
    marks = jnp.zeros((8, LANES), F32)
    for k in range(sh.owned):
        hit = jnp.where(lane == index_ref[j, k, i], own, 0.0)
        marks = jnp.where(lane8 == k, jnp.sum(hit, axis=1, keepdims=True), marks)
    mark_ref[...] = marks
    count, width = coarse_ref.shape[1], coarse_ref.shape[0]
    fill = jnp.zeros((width, LANES - count), F32)
    turned_ref[...] = jnp.concatenate([coarse_ref[...], fill], axis=1).T
    groups = LANES // 2 // width
    pieces = [turned_ref[pl.ds(g, 8, stride=groups), :] for g in range(groups)]
    block_ref[...] = jnp.concatenate(pieces + pieces, axis=1)


def terms_kernel(
    sh, after_ref, mark_ref, block_ref, row_ref, even_ref, odd_ref, pay_ref,
):
    i, j = lax.axis_index("gx"), lax.axis_index("gy")
    row1 = lax.broadcasted_iota(jnp.int32, (8, 1), 0)
    marks = [mark_ref[:, k : k + 1] for k in range(sh.owned)]
    coords = []
    for coord in range(3):
        column = jnp.zeros((8, 1), F32)
        for k in range(sh.owned):
            column = jnp.where(row1 == k, marks[k][coord : coord + 1, :], column)
        coords.append(column)

    def add_column(column, sums):
        square = jnp.zeros((8, sh.points), F32)
        for coord in range(3):
            offset = column[coord : coord + 1, :] - coords[coord]
            square = square + offset * offset
        kern = scaled_wendland(16.0 * square)
        return tuple(
            total + kern * column[3 + q : 4 + q, :] for q, total in enumerate(sums)
        )

    sums = tuple(jnp.zeros((8, sh.points), F32) for _ in range(3))
    for ref in (row_ref, even_ref, odd_ref):
        for c in range(3):
            sums = add_column(ref[c], sums)
    terms = [jnp.sum(s, axis=1, keepdims=True) * (1.0 / KERN_SCALE) for s in sums]
    lane8 = lane_ids(8, LANES)
    row8 = row_ids(LANES)
    half = LANES // 2
    first = (i * sh.ny + j) * sh.owned
    tile = jnp.zeros((8, LANES), F32)
    for k in range(sh.owned):
        column = jnp.where(row1 < 3, marks[k], 0.0)
        for q in range(3):
            column = jnp.where(row1 == 3 + q, terms[q][k : k + 1, :], column)
        tile = jnp.where(lane8 == first + k, column, tile)
    block = block_ref[...]
    own_half = (lane8 >= half) == (first >= half)
    tile = jnp.where(own_half, tile, block)
    for d in range(sh.devices):
        pay_ref[d] = tile


def build_kernel(sh, spans, own_ref, *refs):
    group_refs, (high_ref, low_ref, near_ref) = refs[: len(spans)], refs[len(spans) :]
    centre = sh.centre(lax.axis_index("gx"), lax.axis_index("gy"))
    own = own_features(own_ref[...], centre).astype(BF16)

    def one(ref, c, to):
        features = near_features(ref[c], centre).astype(BF16)
        near_ref[to] = features
        near = features.T
        for layer, (low, high, offset) in enumerate(sh.blocks):
            lhs = near[layer * sh.slots : (layer + 1) * sh.slots]
            for target in range(low, high):
                square = bf16_dot(lhs, own[:, target * sh.slots : (target + 1) * sh.slots])
                kern = scaled_wendland(square)
                head = kern.astype(BF16)
                at = offset + (target - low) * sh.slots
                high_ref[to, :, at : at + sh.slots] = head
                head = high_ref[to, :, at : at + sh.slots]
                low_ref[to, :, at : at + sh.slots] = (
                    kern - head.astype(F32)
                ).astype(BF16)
        return 0

    base = 0
    for ref, (start, stop) in zip(group_refs, spans):
        shift = base - start
        lax.fori_loop(start, stop, lambda c, _, ref=ref, shift=shift: one(ref, c, c + shift), 0)
        base += stop - start


def built(refs, group, c):
    if group:
        return refs[2], (group - 1) * 3 + c
    return (refs[1], c - 1) if c else (refs[0], 0)


def split_rows(values):
    head = values.astype(BF16)
    tail = values - head.astype(F32)
    return head, jnp.concatenate([head.astype(F32), tail], axis=0).astype(BF16)


def apply_column(sh, high_ref, low_ref, c, values, out_ref):
    head, both = split_rows(values)
    for layer, (low, high, offset) in enumerate(sh.blocks):
        at = slice(layer * sh.slots, (layer + 1) * sh.slots)
        width = (high - low) * sh.slots
        main = bf16_dot(both[:, at], high_ref[c, :, offset : offset + width])
        rest = bf16_dot(head[:, at], low_ref[c, :, offset : offset + width])
        out_ref[:, low * sh.slots : high * sh.slots] += main[:8] + main[8:] + rest


def spread_dot(part, high, low):
    head, both = split_rows(part)
    main = bf16_dot(both, high)
    return main[:8] + main[8:] + bf16_dot(head, low)


def coarse_dot(terms, gram_ref):
    gram = gram_ref[...]
    high = gram.astype(BF16)
    return spread_dot(terms, high, (gram - high.astype(F32)).astype(BF16))


def gathered_matrix(sh, recv_ref, gram_ref):
    width = sh.row_landmarks
    half = LANES // 2
    groups = half // width
    lane = lane_ids(sh.ny * 8, LANES)
    for g in range(groups):
        total = jnp.zeros((sh.ny * 8, LANES), F32)
        for i in range(sh.nx):
            tiles = jnp.concatenate([recv_ref[i * sh.ny + j] for j in range(sh.ny)], axis=0)
            base = half if i * width < half else 0
            shift = (i * width - base - g * width) % LANES
            if shift:
                tiles = pltpu.roll(tiles, shift, axis=1)
            keep = jnp.logical_and(lane >= i * width, lane < (i + 1) * width)
            total = jnp.where(keep, tiles, total)
        for j in range(sh.ny):
            for r in range(8):
                p = groups * r + g
                at = (p // sh.owned) * width + j * sh.owned + p % sh.owned
                gram_ref[at : at + 1, :] = total[j * 8 + r : j * 8 + r + 1, :]


def rhs_rows(column, lanes):
    return jnp.where(
        row_ids(lanes) < 3, jnp.concatenate([column[3:8], column[0:3]], axis=0), 0.0
    )


def first_kernel(
    sh, row_ref, even_ref, odd_ref, recv_ref, *refs,
):
    near_refs, high_refs, low_refs = refs[0:3], refs[3:6], refs[6:9]
    first_body(sh, row_ref, even_ref, odd_ref, recv_ref, near_refs, high_refs, low_refs, *refs[9:])


def first_body(
    sh, row_ref, even_ref, odd_ref, recv_ref, near_refs, high_refs, low_refs,
    pay_ref, search_ref, spread_ref, rest_ref, gram_ref, image_ref, mark_ref,
):
    i, j = lax.axis_index("gx"), lax.axis_index("gy")
    centre = sh.centre(i, j)
    half = LANES // 2
    totals = [jnp.zeros((8, LANES), F32), jnp.zeros((8, LANES), F32)]
    for d in range(sh.devices):
        side = 0 if d * sh.owned < half else 1
        totals[side] = totals[side] + recv_ref[d]
    gathered = jnp.where(lane_ids(8, LANES) < half, totals[0], totals[1])
    gathered = jnp.where(row_ids(LANES) == 6, 1.0, gathered)
    gathered_matrix(sh, recv_ref, gram_ref)
    mark_ref[...] = own_features(gathered, centre).T.astype(BF16)
    coarse = coarse_dot(rhs_rows(gathered, LANES), gram_ref)
    image_ref[...] = jnp.zeros_like(image_ref)
    rows, _ = sh.near_ids(i, j)
    marks, parts = [], []
    for near_row in rows:
        start = sh.window_start(near_row)
        marks.append(mark_ref[pl.ds(start, sh.window), :])
        parts.append(sh.window_of(coarse, start))
    for group, ref in enumerate((row_ref, even_ref, odd_ref)):
        for c in range(3):
            near_ref, at = built(near_refs, group, c)
            high_ref, low_ref = built(high_refs, group, c)[0], built(low_refs, group, c)[0]
            spread = scaled_wendland(bf16_dot(marks[c], near_ref[at])) * (1.0 / KERN_SCALE)
            head = spread.astype(BF16)
            rest = (spread - head.astype(F32)).astype(BF16)
            spread_ref[group * 3 + c] = head
            rest_ref[group * 3 + c] = rest
            residual = rhs_rows(ref[c], sh.points)
            search = residual * (1.0 / RIDGE_WEIGHT) + spread_dot(parts[c], head, rest)
            search_ref[group * 3 + c] = search
            apply_column(sh, high_ref, low_ref, at, search, image_ref)
    residual = rhs_rows(row_ref[0], sh.points)
    search = search_ref[0]
    image = image_ref[...] * (1.0 / KERN_SCALE) + RIDGE_WEIGHT * search
    image_ref[...] = image
    gamma = jnp.sum(residual * search, axis=1, keepdims=True)
    delta = jnp.sum(search * image, axis=1, keepdims=True)
    head, both = split_rows(image)
    across = (((1,), (1,)), ((), ()))
    main = lax.dot_general(both, spread_ref[0], across, preferred_element_type=F32)
    tail = lax.dot_general(head, rest_ref[0], across, preferred_element_type=F32)
    window = main[:8] + main[8:] + tail
    lane = lane_ids(8, LANES)
    fill = jnp.zeros((8, LANES - sh.window), F32)
    tile = jnp.concatenate([window, fill], axis=1)
    tile = jnp.where(lane == 2 * sh.window, gamma, tile)
    tile = jnp.where(lane == 2 * sh.window + 1, delta, tile)
    moved = pltpu.roll(tile, sh.window, axis=1)
    lane1 = lane_ids(1, LANES)
    pair = jnp.where(
        jnp.logical_and(lane1 >= sh.window, lane1 < 2 * sh.window), moved[1:2], tile[0:1]
    )
    ends = jnp.where(lane1 == 2 * sh.window + 2, gamma[1:2], pair)
    ends = jnp.where(lane1 == 2 * sh.window + 3, delta[1:2], ends)
    lines = [ends, tile[2:3]]
    for d in range(sh.devices):
        for q in range(3):
            pay_ref[d, :, q * sh.points : (q + 1) * sh.points] = image[q : q + 1, :]
        for at, line in enumerate(lines):
            start = 3 * sh.points + at * LANES
            pay_ref[d, :, start : start + LANES] = line


def second_kernel(
    sh, recv_ref, row_ref, search_ref, spread_ref, rest_ref, gram_ref, image_ref, *refs,
):
    second_body(
        sh, recv_ref, row_ref, search_ref, spread_ref, rest_ref, gram_ref, image_ref,
        refs[0:3], refs[3:6], *refs[6:],
    )


def second_body(
    sh, recv_ref, row_ref, search_ref, spread_ref, rest_ref, gram_ref, image_ref,
    high_refs, low_refs, pay_ref, sums_ref, residual_ref, next_ref, product_ref,
):
    i, j = lax.axis_index("gx"), lax.axis_index("gy")
    lane = lane_ids(8, LANES)
    row8 = row_ids(LANES)
    terms = jnp.zeros((8, LANES), F32)
    scalars = jnp.zeros((8, LANES), F32)
    for a in range(sh.nx):
        lines = []
        for at in (3 * sh.points, 3 * sh.points + LANES):
            total = recv_ref[a * sh.ny, :, at : at + LANES]
            for b in range(1, sh.ny):
                total = total + recv_ref[a * sh.ny + b, :, at : at + LANES]
            lines.append(total)
        pair = jnp.broadcast_to(lines[0], (8, LANES))
        third = jnp.broadcast_to(lines[1], (8, LANES))
        tile = jnp.where(row8 == 2, third, pair)
        scalars = scalars + tile
        start = min(max(a - 1, 0), sh.nx - 3) * sh.row_landmarks
        first = pltpu.roll(tile, start, axis=1) if start else tile
        other = pltpu.roll(tile, (start - sh.window) % LANES, axis=1)
        inside = jnp.logical_and(lane >= start, lane < start + sh.window)
        value = jnp.where(row8 == 1, other, first)
        terms = terms + jnp.where(jnp.logical_and(inside, row8 < 3), value, 0.0)
    ends = 2 * sh.window

    def column(at):
        second = scalars[:, ends + 2 + at : ends + 3 + at]
        value = scalars[:, ends + at : ends + at + 1]
        return jnp.where(lax.broadcasted_iota(jnp.int32, (8, 1), 0) == 1, second, value)

    gamma, delta = column(0), column(1)
    row1 = lax.broadcasted_iota(jnp.int32, (8, 1), 0)
    alpha = jnp.where(row1 < 3, gamma / jnp.where(row1 < 3, delta, 1.0), 0.0)
    coarse = coarse_dot(terms, gram_ref)
    product_ref[...] = jnp.zeros_like(product_ref)
    rows, cols = sh.near_ids(i, j)
    zeros5 = jnp.zeros((5, sh.points), F32)
    parts = [sh.window_of(coarse, sh.window_start(near_row)) for near_row in rows]
    for group in range(3):
        for c in range(3):
            at = group * 3 + c
            high_ref, kern_at = built(high_refs, group, c)
            low_ref = built(low_refs, group, c)[0]
            source = rows[c] * sh.ny + cols[group]
            image = jnp.concatenate(
                [recv_ref[source, :, q * sh.points : (q + 1) * sh.points] for q in range(3)]
                + [zeros5],
                axis=0,
            )
            step = image * (1.0 / RIDGE_WEIGHT) + spread_dot(parts[c], spread_ref[at], rest_ref[at])
            search = search_ref[at] - alpha * step
            if at == 0:
                next_ref[...] = search
            apply_column(sh, high_ref, low_ref, kern_at, search, product_ref)
    residual = rhs_rows(row_ref[0], sh.points)
    image = image_ref[...]
    residual = residual - alpha * image
    residual_ref[...] = residual
    search = next_ref[...]
    product = product_ref[...] * (1.0 / KERN_SCALE) + RIDGE_WEIGHT * search
    product_ref[...] = product
    sums = [
        jnp.sum(residual * search, axis=1, keepdims=True),
        jnp.sum(search * product, axis=1, keepdims=True),
        jnp.sum(search * image, axis=1, keepdims=True)
        + jnp.sum(search_ref[0] * product, axis=1, keepdims=True),
    ]
    line = jnp.zeros((1, LANES), F32)
    lane1 = lane_ids(1, LANES)
    for at, value in enumerate(sums):
        for q in range(3):
            line = jnp.where(lane1 == 3 * at + q, value[q : q + 1, :], line)
    for d in range(sh.devices):
        pay_ref[d] = line
    sums_ref[...] = jnp.where(lane == 0, gamma, jnp.where(lane == 1, delta, 0.0))


def last_kernel(
    sh, recv_ref, sums_ref, search_ref, image_ref, residual_ref, next_ref, product_ref,
    solution_ref, final_ref,
):
    total = recv_ref[0]
    for d in range(1, sh.devices):
        total = total + recv_ref[d]
    row1 = lax.broadcasted_iota(jnp.int32, (8, 1), 0)
    good = row1 < 3

    def column(at):
        value = jnp.zeros((8, 1), F32)
        for q in range(3):
            value = jnp.where(row1 == q, total[:, 3 * at + q : 3 * at + q + 1], value)
        return value

    own = sums_ref[...]
    gamma, delta = own[:, 0:1], own[:, 1:2]
    gamma_new, inner, cross = column(0), column(1), column(2)
    safe_gamma = jnp.where(good, gamma, 1.0)
    safe_delta = jnp.where(good, delta, 1.0)
    alpha = gamma / safe_delta
    beta = gamma_new / safe_gamma
    curve = inner + beta * cross + beta * beta * delta
    step = gamma_new / jnp.where(good, curve, 1.0)
    direction = next_ref[...] + beta * search_ref[0]
    image = product_ref[...] + beta * image_ref[...]
    solution = alpha * search_ref[0] + step * direction
    residual = residual_ref[...] - step * image
    for layer in range(sh.layers):
        at = slice(layer * sh.slots, (layer + 1) * sh.slots)
        solution_ref[:, 0, 0, layer, :] = solution[0:3, at]
        final_ref[:, 0, 0, layer, :] = residual[0:3, at]


def local_fast(positions, counts, targets, landmark_index, coarse_matrix):
    both = ("gx", "gy")
    sh = Shape(positions, landmark_index, lax.axis_size("gx"), lax.axis_size("gy"))
    field = jax.ShapeDtypeStruct((8, sh.points), F32)
    vmem = pl.BlockSpec(memory_space=pltpu.VMEM)
    anyw = pl.BlockSpec(memory_space=pltpu.HBM)

    def call(kernel, name, out_shape, in_specs, cost=10**6, scratch=()):
        return pl.pallas_call(
            kernel,
            out_shape=out_shape,
            in_specs=in_specs,
            out_specs=jax.tree.map(lambda _: vmem, out_shape),
            scratch_shapes=scratch,
            name=name,
            compiler_params=pltpu.CompilerParams(vmem_limit_bytes=VMEM_BYTES),
            cost_estimate=pl.CostEstimate(flops=cost, bytes_accessed=10**5, transcendentals=0),
        )

    def part(kernel, *fixed):
        return functools.partial(kernel, sh, *fixed)

    def exchange(payload):
        return lax.all_to_all(payload, both, 0, 0)

    index = jnp.transpose(landmark_index, (1, 2, 0))
    turned = jnp.transpose(coarse_matrix)
    tile = jax.ShapeDtypeStruct((8, LANES), F32)
    own, marks, block = call(
        part(prepare_kernel),
        "prepare",
        (field, tile, tile),
        [anyw] * 5,
        scratch=[
            pltpu.VMEM(positions.shape, F32),
            pltpu.SMEM(counts.shape, jnp.int32),
            pltpu.VMEM(targets.shape, F32),
            pltpu.SMEM(index.shape, jnp.int32),
            pltpu.VMEM(turned.shape, F32),
            pltpu.VMEM((LANES, turned.shape[0]), F32),
            pltpu.SemaphoreType.DMA((5,)),
        ],
    )(*(pltpu.with_memory_space_constraint(x, pltpu.HBM)
        for x in (positions, counts, targets, index, turned)))
    row = jnp.stack([own, swap(own, "gx", 0), swap(own, "gx", 1)])

    def build(name, spans, *groups):
        columns = sum(stop - start for start, stop in spans)
        kern = jax.ShapeDtypeStruct((columns, sh.slots, sh.pairs), BF16)
        near = jax.ShapeDtypeStruct((columns, 48, sh.points), BF16)
        return call(
            part(build_kernel, spans),
            name,
            (kern, kern, near),
            [vmem] * (1 + len(groups)),
            cost=columns * 3 * 10**9,
        )(own, *groups)

    high0, low0, near0 = build("build_own", [(0, 1)], own[None])
    row, near0 = lax.optimization_barrier((row, near0))
    even, odd = swap(row, "gy", 0), swap(row, "gy", 1)
    high1, low1, near1 = build("build_pair", [(1, 3)], row)
    terms = call(
        part(terms_kernel),
        "terms",
        jax.ShapeDtypeStruct((sh.devices, 8, LANES), F32),
        [anyw] + [vmem] * 5,
    )(near1, marks, block, row, even, odd)
    terms, even, odd = lax.optimization_barrier((exchange(terms), even, odd))
    high2, low2, near2 = build("build_rest", [(0, 3), (0, 3)], even, odd)

    wide = 3 * sh.points + 2 * LANES
    spread_shape = jax.ShapeDtypeStruct((9, sh.window, sh.points), BF16)
    payload, search, spread, rest, gram, image = call(
        part(first_kernel),
        "first",
        (
            jax.ShapeDtypeStruct((sh.devices, 1, wide), F32),
            jax.ShapeDtypeStruct((9, 8, sh.points), F32),
            spread_shape,
            spread_shape,
            jax.ShapeDtypeStruct((sh.landmarks, LANES), F32),
            field,
        ),
        [vmem] * 13,
        scratch=[pltpu.VMEM((sh.landmarks, 48), BF16)],
    )(row, even, odd, terms, near0, near1, near2, high0, high1, high2, low0, low1, low2)
    images = exchange(payload)

    line = jax.ShapeDtypeStruct((sh.devices, 1, LANES), F32)
    totals, sums, residual, following, product = call(
        part(second_kernel), "second", (line, tile, field, field, field), [vmem] * 13
    )(images, row, search, spread, rest, gram, image, high0, high1, high2, low0, low1, low2)
    totals = exchange(totals)

    out = jax.ShapeDtypeStruct(targets.shape, F32)
    return call(part(last_kernel), "last", (out, out), [vmem] * 7)(
        totals, sums, search, image, residual, following, product
    )


def fits_fast(positions, targets, landmark_index, coarse_matrix, nx, ny):
    owned = landmark_index.shape[2]
    return (
        nx * ny * owned == LANES
        and 6 * ny * owned + 4 <= LANES
        and nx >= 3
        and targets.shape[0] == 3
        and coarse_matrix.shape[0] == 8 * (LANES // 2 // (ny * owned))
    )


def local(positions, counts, targets, landmark_index, coarse_matrix):
    nx, ny = lax.axis_size("gx"), lax.axis_size("gy")
    if fits_fast(positions, targets, landmark_index, coarse_matrix, nx, ny):
        return local_fast(positions, counts, targets, landmark_index, coarse_matrix)
    return local_plain(positions, counts, targets, landmark_index, coarse_matrix)


def solution(mesh):
    return jax.shard_map(
        local,
        mesh=mesh,
        in_specs=(
            P(None, "gx", "gy", None, None),
            P("gx", "gy", None),
            P(None, "gx", "gy", None, None),
            P(),
            P("gy", "gx"),
        ),
        out_specs=(P(None, "gx", "gy", None, None), P(None, "gx", "gy", None, None)),
        check_vma=False,
    )
```

```python
import functools

import jax
import jax.numpy as jnp
from jax import lax
from jax.experimental import pallas as pl
from jax.experimental.pallas import tpu as pltpu
from jax.sharding import PartitionSpec as P

ITERS = 2


RIDGE_WEIGHT = 2.0
HIGHEST_PRECISION = lax.Precision.HIGHEST

F32 = jnp.float32
BF16 = jnp.bfloat16
LANES = 128
FAR = 4096.0
KERN_SCALE = 256.0
VMEM_BYTES = 8 * 2**20


def with_halo(x, sides, width):
    for axis, dim in sides:
        peers, length = (lax.axis_size(axis), x.shape[dim])
        up = [(i, (i + 1) % peers) for i in range(peers - 1)]
        down = [(j, i) for i, j in up]
        last = lax.slice_in_dim(x, length - width, length, axis=dim)
        leading = lax.slice_in_dim(x, 0, width, axis=dim)
        before = lax.ppermute(last, axis, up)
        after = lax.ppermute(leading, axis, down)
        x = jnp.concatenate([before, x, after], axis=dim)
    return x


def wendland(points_a, points_b):
    square_sum = jnp.zeros((points_a.shape[1], points_b.shape[1]), jnp.float32)
    for coord in range(3):
        offset = points_a[coord][:, None] - points_b[coord][None, :]
        square_sum = square_sum + offset * offset
    distance = jnp.sqrt(square_sum)
    remain = jnp.maximum(1.0 - distance, 0.0)
    remain = remain * remain
    return remain * remain * (4.0 * distance + 1.0)


def cell_rim(field):
    return with_halo(field, (("gx", 1), ("gy", 2)), 1)


def inner_sums(left, right):
    return jnp.sum(left * right, axis=(1, 2, 3, 4))


def per_component(values):
    return values[:, None, None, None, None]


def global_inner(values):
    return lax.psum(values, ("gx", "gy"))


def local_plain(positions, counts, targets, landmark_index, coarse_matrix):
    components = targets.shape[0]
    layer_count = positions.shape[3]
    slot_count = positions.shape[4]
    owned_count = landmark_index.shape[2]
    column_points = layer_count * slot_count
    slot_ids = jnp.arange(slot_count, dtype=jnp.int32)
    live_mask = (slot_ids[None, None, None, :] < counts[:, :, :, None]).astype(jnp.float32)
    live_flat = live_mask.reshape(1, column_points)
    rhs_field = live_mask[None] * targets
    ext_pos = cell_rim(positions)
    ext_cloud = ext_pos.reshape(3, 9 * column_points)
    own_points = positions.reshape(3, column_points)
    row_index = lax.axis_index("gx")
    col_index = lax.axis_index("gy")
    three_ids = jnp.arange(3, dtype=jnp.int32)
    near_rows = jnp.clip(row_index + three_ids - 1, 0, lax.axis_size("gx") - 1)
    near_cols = jnp.clip(col_index + three_ids - 1, 0, lax.axis_size("gy") - 1)
    near_index = landmark_index[near_rows[:, None], near_cols[None, :], :]
    ext_flat = ext_pos.reshape(3, 3, 3, column_points)
    near_pos = jnp.take_along_axis(ext_flat, near_index[None], axis=3)
    landmark_pos = near_pos[:, 1, 1, :]
    spread_kernel = wendland(own_points, near_pos.reshape(3, 9 * owned_count))

    def coarse_solve(terms):
        row_terms = lax.all_gather(terms, "gy", axis=0, tiled=True)
        return lax.psum_scatter(
            jnp.dot(coarse_matrix, row_terms, precision=HIGHEST_PRECISION),
            "gx",
            scatter_dimension=0,
            tiled=True,
        )

    def landmark_sums(vector):
        gather_kernel = wendland(landmark_pos, ext_cloud)
        ext_vec = cell_rim(vector).reshape(components, 9 * column_points)
        return jnp.einsum("kn,qn->kq", gather_kernel, ext_vec, precision=HIGHEST_PRECISION)

    def precondition(vector):
        terms = landmark_sums(vector)
        coarse = coarse_solve(terms)
        near_coarse = with_halo(
            coarse.reshape(1, 1, owned_count, components), (("gx", 0), ("gy", 1)), 1
        )
        near_coarse = near_coarse.reshape(9 * owned_count, components)
        spread = jnp.einsum("nm,mq->qn", spread_kernel, near_coarse, precision=HIGHEST_PRECISION)
        return vector / RIDGE_WEIGHT + (live_flat * spread).reshape(vector.shape)

    solution = jnp.zeros_like(rhs_field)
    residual = rhs_field
    search = precondition(residual)
    gamma = global_inner(inner_sums(residual, search))
    direction = search
    for iteration in range(ITERS):
        operator_ext_vec = cell_rim(direction)
        layer_out = []
        for layer in range(layer_count):
            low_layer = max(layer - 1, 0)
            high_layer = min(layer + 2, layer_count)
            near_points = ext_pos[:, :, :, low_layer:high_layer, :].reshape(3, -1)
            near_values = operator_ext_vec[:, :, :, low_layer:high_layer, :].reshape(components, -1)
            kern = wendland(positions[:, 0, 0, layer, :], near_points)
            layer_out.append(
                jnp.einsum("bn,qn->qb", kern, near_values, precision=HIGHEST_PRECISION)
            )
        product = jnp.stack(layer_out, axis=1).reshape(direction.shape)
        image = live_mask[None] * product + RIDGE_WEIGHT * direction
        alpha = gamma / global_inner(inner_sums(direction, image))
        solution = solution + per_component(alpha) * direction
        residual = residual - per_component(alpha) * image
        if iteration + 1 < ITERS:
            search = precondition(residual)
            gamma_new = global_inner(inner_sums(residual, search))
            direction = search + per_component(gamma_new / gamma) * direction
            gamma = gamma_new
    return (solution, residual)


def row_ids(lanes):
    return lax.broadcasted_iota(jnp.int32, (8, lanes), 0)


def lane_ids(rows, lanes):
    return lax.broadcasted_iota(jnp.int32, (rows, lanes), 1)


def split_three(values):
    high = values.astype(BF16).astype(F32)
    rest = values - high
    middle = rest.astype(BF16).astype(F32)
    low = (rest - middle).astype(BF16).astype(F32)
    return high, middle, low


def centred(column, centre):
    row = row_ids(column.shape[1])
    shift = jnp.where(row == 0, centre[0], jnp.where(row == 1, centre[1], centre[2]))
    xyz = jnp.where(row < 3, column - shift, 0.0)
    norm = 16.0 * jnp.sum(xyz * xyz, axis=0, keepdims=True)
    return row, xyz, norm + (1.0 - column[6:7, :]) * FAR


def near_features(column, centre):
    row, xyz, norm = centred(column, centre)
    high, middle, low = split_three(
        jnp.where(row == 3, norm, jnp.where(row == 4, 1.0, xyz))
    )
    return jnp.concatenate([high, middle, low, high, middle, high], axis=0)


def own_features(column, centre):
    row, xyz, norm = centred(column, centre)
    high, middle, low = split_three(
        jnp.where(row == 3, 1.0, jnp.where(row == 4, norm, -32.0 * xyz))
    )
    return jnp.concatenate([high, high, high, middle, middle, low], axis=0)


def scaled_wendland(square16):
    square16 = jnp.maximum(square16, 1e-6)
    four = square16 * lax.rsqrt(square16)
    remain = jnp.maximum(4.0 - four, 0.0)
    remain = remain * remain
    return remain * remain * (four + 1.0)


def bf16_dot(left, right):
    return jnp.dot(left, right, preferred_element_type=F32)


def full_dot(left, right, transposed=False):
    dims = (((1,), (1 if transposed else 0,)), ((), ()))
    return lax.dot_general(
        left, right, dims, precision=HIGHEST_PRECISION, preferred_element_type=F32
    )


def swap_partner(index, peers, odd):
    step = 1 - 2 * lax.rem(index + odd, 2)
    partner = index + step
    good = jnp.logical_and(partner >= 0, partner < peers)
    return jnp.where(good, partner, index)


def swap(x, axis, odd):
    peers = lax.axis_size(axis)
    pairs = []
    for i in range(odd, peers - 1, 2):
        pairs += [(i, i + 1), (i + 1, i)]
    return lax.ppermute(x, axis, pairs)


class Shape:
    def __init__(self, positions, landmark_index, nx, ny):
        self.nx, self.ny = nx, ny
        self.devices = nx * ny
        self.layers, self.slots = positions.shape[3], positions.shape[4]
        self.points = self.layers * self.slots
        self.owned = landmark_index.shape[2]
        self.row_landmarks = ny * self.owned
        self.landmarks = nx * self.row_landmarks
        self.window = 3 * self.row_landmarks
        self.blocks = []
        offset = 0
        for layer in range(self.layers):
            low, high = max(layer - 1, 0), min(layer + 2, self.layers)
            self.blocks.append((low, high, offset))
            offset += (high - low) * self.slots
        self.pairs = offset

    def centre(self, i, j):
        return (i.astype(F32) + 0.5, j.astype(F32) + 0.5, 0.5 * self.layers)

    def window_start(self, i):
        start = jnp.clip(i - 1, 0, self.nx - 3) * self.row_landmarks
        return pl.multiple_of(start, self.row_landmarks)

    def window_of(self, lanes, start):
        shift = lax.rem(LANES - start, LANES)
        return pltpu.roll(lanes, shift, axis=1)[:, : self.window]

    def near_ids(self, i, j):
        rows = [i, swap_partner(i, self.nx, 0), swap_partner(i, self.nx, 1)]
        cols = [j, swap_partner(j, self.ny, 0), swap_partner(j, self.ny, 1)]
        return rows, cols


def prepare_kernel(
    sh, pos_hbm, counts_hbm, tgt_hbm, index_hbm, coarse_hbm, own_ref, mark_ref, block_ref,
    pos_ref, counts_ref, tgt_ref, index_ref, coarse_ref, turned_ref, sems,
):
    copies = [
        pltpu.make_async_copy(source, target, sems.at[at])
        for at, (source, target) in enumerate(
            (
                (counts_hbm, counts_ref),
                (pos_hbm, pos_ref),
                (tgt_hbm, tgt_ref),
                (index_hbm, index_ref),
                (coarse_hbm, coarse_ref),
            )
        )
    ]
    for copy in copies:
        copy.start()
    for copy in copies:
        copy.wait()
    slot = lane_ids(1, sh.slots)
    for layer in range(sh.layers):
        live = (slot < counts_ref[0, 0, layer]).astype(F32)
        at = pl.ds(layer * sh.slots, sh.slots)
        own_ref[0:3, at] = pos_ref[:, 0, 0, layer, :]
        own_ref[3:6, at] = live * tgt_ref[:, 0, 0, layer, :]
        own_ref[6:7, at] = live
        own_ref[7:8, at] = jnp.zeros_like(live)
    i, j = lax.axis_index("gx"), lax.axis_index("gy")
    own = own_ref[...]
    lane = lane_ids(8, sh.points)
    lane8 = lane_ids(8, LANES)
    marks = jnp.zeros((8, LANES), F32)
    for k in range(sh.owned):
        hit = jnp.where(lane == index_ref[j, k, i], own, 0.0)
        marks = jnp.where(lane8 == k, jnp.sum(hit, axis=1, keepdims=True), marks)
    mark_ref[...] = marks
    count, width = coarse_ref.shape[1], coarse_ref.shape[0]
    fill = jnp.zeros((width, LANES - count), F32)
    turned_ref[...] = jnp.concatenate([coarse_ref[...], fill], axis=1).T
    groups = LANES // 2 // width
    pieces = [turned_ref[pl.ds(g, 8, stride=groups), :] for g in range(groups)]
    block_ref[...] = jnp.concatenate(pieces + pieces, axis=1)


def terms_kernel(
    sh, after_ref, mark_ref, block_ref, row_ref, even_ref, odd_ref, pay_ref,
):
    i, j = lax.axis_index("gx"), lax.axis_index("gy")
    row1 = lax.broadcasted_iota(jnp.int32, (8, 1), 0)
    marks = [mark_ref[:, k : k + 1] for k in range(sh.owned)]
    coords = []
    for coord in range(3):
        column = jnp.zeros((8, 1), F32)
        for k in range(sh.owned):
            column = jnp.where(row1 == k, marks[k][coord : coord + 1, :], column)
        coords.append(column)

    def add_column(column, sums):
        square = jnp.zeros((8, sh.points), F32)
        for coord in range(3):
            offset = column[coord : coord + 1, :] - coords[coord]
            square = square + offset * offset
        kern = scaled_wendland(16.0 * square)
        return tuple(
            total + kern * column[3 + q : 4 + q, :] for q, total in enumerate(sums)
        )

    sums = tuple(jnp.zeros((8, sh.points), F32) for _ in range(3))
    for ref in (row_ref, even_ref, odd_ref):
        for c in range(3):
            sums = add_column(ref[c], sums)
    terms = [jnp.sum(s, axis=1, keepdims=True) * (1.0 / KERN_SCALE) for s in sums]
    lane8 = lane_ids(8, LANES)
    row8 = row_ids(LANES)
    half = LANES // 2
    first = (i * sh.ny + j) * sh.owned
    tile = jnp.zeros((8, LANES), F32)
    for k in range(sh.owned):
        column = jnp.where(row1 < 3, marks[k], 0.0)
        for q in range(3):
            column = jnp.where(row1 == 3 + q, terms[q][k : k + 1, :], column)
        tile = jnp.where(lane8 == first + k, column, tile)
    block = block_ref[...]
    own_half = (lane8 >= half) == (first >= half)
    tile = jnp.where(own_half, tile, block)
    for d in range(sh.devices):
        pay_ref[d] = tile


def build_layer(sh, near, own, layer, high_ref, low_ref, to):
    low, high, offset = sh.blocks[layer]
    lhs = near[layer * sh.slots : (layer + 1) * sh.slots]
    for target in range(low, high):
        square = bf16_dot(lhs, own[:, target * sh.slots : (target + 1) * sh.slots])
        kern = scaled_wendland(square)
        at = slice(offset + (target - low) * sh.slots, offset + (target - low + 1) * sh.slots)
        high_ref[to, :, at] = kern.astype(BF16)
        head = high_ref[to, :, at].astype(F32)
        low_ref[to, :, at] = (kern - head).astype(BF16)


def build_kernel(sh, spans, own_ref, *refs):
    group_refs, (high_ref, low_ref, near_ref) = refs[: len(spans)], refs[len(spans) :]
    centre = sh.centre(lax.axis_index("gx"), lax.axis_index("gy"))
    own = own_features(own_ref[...], centre).astype(BF16)

    def one(ref, c, to):
        features = near_features(ref[c], centre).astype(BF16)
        near_ref[to] = features
        near = features.T
        for layer in range(sh.layers):
            build_layer(sh, near, own, layer, high_ref, low_ref, to)

    base = 0
    for ref, (start, stop) in zip(group_refs, spans):
        for c in range(start, stop):
            one(ref, c, base + c - start)
        base += stop - start


def built(refs, group, c):
    if group:
        return refs[2], (group - 1) * 3 + c
    return (refs[1], c - 1) if c else (refs[0], 0)


def split_rows(values):
    head = values.astype(BF16)
    tail = values - head.astype(F32)
    return head, jnp.concatenate([head.astype(F32), tail], axis=0).astype(BF16)


def apply_layer(sh, high_ref, low_ref, c, head, both, layer, out_ref):
    low, high, offset = sh.blocks[layer]
    at = slice(layer * sh.slots, (layer + 1) * sh.slots)
    width = (high - low) * sh.slots
    main = bf16_dot(both[:, at], high_ref[c, :, offset : offset + width])
    rest = bf16_dot(head[:, at], low_ref[c, :, offset : offset + width])
    out_ref[:, low * sh.slots : high * sh.slots] += main[:8] + main[8:] + rest


def apply_column(sh, high_ref, low_ref, c, values, out_ref):
    head, both = split_rows(values)
    for layer in range(sh.layers):
        apply_layer(sh, high_ref, low_ref, c, head, both, layer, out_ref)


def spread_dot(part, high, low):
    head, both = split_rows(part)
    main = bf16_dot(both, high)
    return main[:8] + main[8:] + bf16_dot(head, low)


def coarse_dot(terms, gram_ref):
    gram = gram_ref[...]
    high = gram.astype(BF16)
    return spread_dot(terms, high, (gram - high.astype(F32)).astype(BF16))


def gathered_matrix(sh, recv_ref, gram_ref):
    width = sh.row_landmarks
    half = LANES // 2
    groups = half // width
    lane = lane_ids(sh.ny * 8, LANES)
    for g in range(groups):
        total = jnp.zeros((sh.ny * 8, LANES), F32)
        for i in range(sh.nx):
            tiles = jnp.concatenate([recv_ref[i * sh.ny + j] for j in range(sh.ny)], axis=0)
            base = half if i * width < half else 0
            shift = (i * width - base - g * width) % LANES
            if shift:
                tiles = pltpu.roll(tiles, shift, axis=1)
            keep = jnp.logical_and(lane >= i * width, lane < (i + 1) * width)
            total = jnp.where(keep, tiles, total)
        for j in range(sh.ny):
            for r in range(8):
                p = groups * r + g
                at = (p // sh.owned) * width + j * sh.owned + p % sh.owned
                gram_ref[at : at + 1, :] = total[j * 8 + r : j * 8 + r + 1, :]


def rhs_rows(column, lanes):
    return jnp.where(
        row_ids(lanes) < 3, jnp.concatenate([column[3:8], column[0:3]], axis=0), 0.0
    )


def first_kernel(
    sh, row_ref, even_ref, odd_ref, recv_ref, near0_ref, near1_ref,
    high0_ref, high1_ref, low0_ref, low1_ref,
    pay_ref, search_ref, spread_ref, rest_ref, gram_ref, image_ref, high2_ref, low2_ref,
    mark_ref,
):
    high_refs = (high0_ref, high1_ref, high2_ref)
    low_refs = (low0_ref, low1_ref, low2_ref)
    i, j = lax.axis_index("gx"), lax.axis_index("gy")
    centre = sh.centre(i, j)
    half = LANES // 2
    totals = [jnp.zeros((8, LANES), F32), jnp.zeros((8, LANES), F32)]
    for d in range(sh.devices):
        side = 0 if d * sh.owned < half else 1
        totals[side] = totals[side] + recv_ref[d]
    gathered = jnp.where(lane_ids(8, LANES) < half, totals[0], totals[1])
    gathered = jnp.where(row_ids(LANES) == 6, 1.0, gathered)
    gathered_matrix(sh, recv_ref, gram_ref)
    mark_ref[...] = own_features(gathered, centre).T.astype(BF16)
    coarse = coarse_dot(rhs_rows(gathered, LANES), gram_ref)
    image_ref[...] = jnp.zeros_like(image_ref)
    rows, _ = sh.near_ids(i, j)
    marks, parts = [], []
    for near_row in rows:
        start = sh.window_start(near_row)
        marks.append(mark_ref[pl.ds(start, sh.window), :])
        parts.append(sh.window_of(coarse, start))
    column_refs = (row_ref, even_ref, odd_ref)
    near_values = {}

    def start_column(at):
        group, c = divmod(at, 3)
        near = near_values.pop(at) if group else (near1_ref[c - 1] if c else near0_ref[0])
        spread = scaled_wendland(bf16_dot(marks[c], near)) * (1.0 / KERN_SCALE)
        head = spread.astype(BF16)
        rest = (spread - head.astype(F32)).astype(BF16)
        spread_ref[at] = head
        rest_ref[at] = rest
        residual = rhs_rows(column_refs[group][c], sh.points)
        search = residual * (1.0 / RIDGE_WEIGHT) + spread_dot(parts[c], head, rest)
        search_ref[at] = search
        return at, split_rows(search)

    own_side = own_features(row_ref[0], centre).astype(BF16)
    waiting = [0, 1, 2]
    for step in range(6):
        group, c = divmod(step + 3, 3)
        features = near_features(column_refs[group][c], centre).astype(BF16)
        near_values[step + 3] = features
        near = features.T
        busy = [start_column(waiting.pop(0)) for _ in range(2 if len(waiting) > 1 else 1)]
        for layer in range(sh.layers):
            build_layer(sh, near, own_side, layer, high2_ref, low2_ref, step)
            for at, (head, both) in busy:
                high_ref, kern_at = built(high_refs, *divmod(at, 3))
                low_ref, _ = built(low_refs, *divmod(at, 3))
                apply_layer(sh, high_ref, low_ref, kern_at, head, both, layer, image_ref)
        waiting.append(step + 3)
    for at in waiting:
        at, (head, both) = start_column(at)
        high_ref, kern_at = built(high_refs, *divmod(at, 3))
        low_ref, _ = built(low_refs, *divmod(at, 3))
        for layer in range(sh.layers):
            apply_layer(sh, high_ref, low_ref, kern_at, head, both, layer, image_ref)
    residual = rhs_rows(row_ref[0], sh.points)
    search = search_ref[0]
    image = image_ref[...] * (1.0 / KERN_SCALE) + RIDGE_WEIGHT * search
    image_ref[...] = image
    gamma = jnp.sum(residual * search, axis=1, keepdims=True)
    delta = jnp.sum(search * image, axis=1, keepdims=True)
    head, both = split_rows(image)
    across = (((1,), (1,)), ((), ()))
    main = lax.dot_general(both, spread_ref[0], across, preferred_element_type=F32)
    tail = lax.dot_general(head, rest_ref[0], across, preferred_element_type=F32)
    window = main[:8] + main[8:] + tail
    lane = lane_ids(8, LANES)
    fill = jnp.zeros((8, LANES - sh.window), F32)
    tile = jnp.concatenate([window, fill], axis=1)
    tile = jnp.where(lane == 2 * sh.window, gamma, tile)
    tile = jnp.where(lane == 2 * sh.window + 1, delta, tile)
    moved = pltpu.roll(tile, sh.window, axis=1)
    lane1 = lane_ids(1, LANES)
    pair = jnp.where(
        jnp.logical_and(lane1 >= sh.window, lane1 < 2 * sh.window), moved[1:2], tile[0:1]
    )
    ends = jnp.where(lane1 == 2 * sh.window + 2, gamma[1:2], pair)
    ends = jnp.where(lane1 == 2 * sh.window + 3, delta[1:2], ends)
    lines = [ends, tile[2:3]]
    for d in range(sh.devices):
        for q in range(3):
            pay_ref[d, :, q * sh.points : (q + 1) * sh.points] = image[q : q + 1, :]
        for at, line in enumerate(lines):
            start = 3 * sh.points + at * LANES
            pay_ref[d, :, start : start + LANES] = line


def second_kernel(
    sh, recv_ref, row_ref, search_ref, spread_ref, rest_ref, gram_ref, image_ref, *refs,
):
    second_body(
        sh, recv_ref, row_ref, search_ref, spread_ref, rest_ref, gram_ref, image_ref,
        refs[0:3], refs[3:6], *refs[6:],
    )


def second_body(
    sh, recv_ref, row_ref, search_ref, spread_ref, rest_ref, gram_ref, image_ref,
    high_refs, low_refs, pay_ref, sums_ref, residual_ref, next_ref, product_ref,
):
    i, j = lax.axis_index("gx"), lax.axis_index("gy")
    lane = lane_ids(8, LANES)
    row8 = row_ids(LANES)
    terms = jnp.zeros((8, LANES), F32)
    scalars = jnp.zeros((8, LANES), F32)
    for a in range(sh.nx):
        lines = []
        for at in (3 * sh.points, 3 * sh.points + LANES):
            total = recv_ref[a * sh.ny, :, at : at + LANES]
            for b in range(1, sh.ny):
                total = total + recv_ref[a * sh.ny + b, :, at : at + LANES]
            lines.append(total)
        pair = jnp.broadcast_to(lines[0], (8, LANES))
        third = jnp.broadcast_to(lines[1], (8, LANES))
        tile = jnp.where(row8 == 2, third, pair)
        scalars = scalars + tile
        start = min(max(a - 1, 0), sh.nx - 3) * sh.row_landmarks
        first = pltpu.roll(tile, start, axis=1) if start else tile
        other = pltpu.roll(tile, (start - sh.window) % LANES, axis=1)
        inside = jnp.logical_and(lane >= start, lane < start + sh.window)
        value = jnp.where(row8 == 1, other, first)
        terms = terms + jnp.where(jnp.logical_and(inside, row8 < 3), value, 0.0)
    ends = 2 * sh.window

    def column(at):
        second = scalars[:, ends + 2 + at : ends + 3 + at]
        value = scalars[:, ends + at : ends + at + 1]
        return jnp.where(lax.broadcasted_iota(jnp.int32, (8, 1), 0) == 1, second, value)

    gamma, delta = column(0), column(1)
    row1 = lax.broadcasted_iota(jnp.int32, (8, 1), 0)
    alpha = jnp.where(row1 < 3, gamma / jnp.where(row1 < 3, delta, 1.0), 0.0)
    coarse = coarse_dot(terms, gram_ref)
    product_ref[...] = jnp.zeros_like(product_ref)
    rows, cols = sh.near_ids(i, j)
    zeros5 = jnp.zeros((5, sh.points), F32)
    parts = [sh.window_of(coarse, sh.window_start(near_row)) for near_row in rows]
    for group in range(3):
        for c in range(3):
            at = group * 3 + c
            high_ref, kern_at = built(high_refs, group, c)
            low_ref = built(low_refs, group, c)[0]
            source = rows[c] * sh.ny + cols[group]
            image = jnp.concatenate(
                [recv_ref[source, :, q * sh.points : (q + 1) * sh.points] for q in range(3)]
                + [zeros5],
                axis=0,
            )
            step = image * (1.0 / RIDGE_WEIGHT) + spread_dot(parts[c], spread_ref[at], rest_ref[at])
            search = search_ref[at] - alpha * step
            if at == 0:
                next_ref[...] = search
            apply_column(sh, high_ref, low_ref, kern_at, search, product_ref)
    residual = rhs_rows(row_ref[0], sh.points)
    image = image_ref[...]
    residual = residual - alpha * image
    residual_ref[...] = residual
    search = next_ref[...]
    product = product_ref[...] * (1.0 / KERN_SCALE) + RIDGE_WEIGHT * search
    product_ref[...] = product
    sums = [
        jnp.sum(residual * search, axis=1, keepdims=True),
        jnp.sum(search * product, axis=1, keepdims=True),
        jnp.sum(search * image, axis=1, keepdims=True)
        + jnp.sum(search_ref[0] * product, axis=1, keepdims=True),
    ]
    line = jnp.zeros((1, LANES), F32)
    lane1 = lane_ids(1, LANES)
    for at, value in enumerate(sums):
        for q in range(3):
            line = jnp.where(lane1 == 3 * at + q, value[q : q + 1, :], line)
    for d in range(sh.devices):
        pay_ref[d] = line
    sums_ref[...] = jnp.where(lane == 0, gamma, jnp.where(lane == 1, delta, 0.0))


def last_kernel(
    sh, recv_ref, sums_ref, search_ref, image_ref, residual_ref, next_ref, product_ref,
    solution_ref, final_ref,
):
    total = recv_ref[0]
    for d in range(1, sh.devices):
        total = total + recv_ref[d]
    row1 = lax.broadcasted_iota(jnp.int32, (8, 1), 0)
    good = row1 < 3

    def column(at):
        value = jnp.zeros((8, 1), F32)
        for q in range(3):
            value = jnp.where(row1 == q, total[:, 3 * at + q : 3 * at + q + 1], value)
        return value

    own = sums_ref[...]
    gamma, delta = own[:, 0:1], own[:, 1:2]
    gamma_new, inner, cross = column(0), column(1), column(2)
    safe_gamma = jnp.where(good, gamma, 1.0)
    safe_delta = jnp.where(good, delta, 1.0)
    alpha = gamma / safe_delta
    beta = gamma_new / safe_gamma
    curve = inner + beta * cross + beta * beta * delta
    step = gamma_new / jnp.where(good, curve, 1.0)
    direction = next_ref[...] + beta * search_ref[0]
    image = product_ref[...] + beta * image_ref[...]
    solution = alpha * search_ref[0] + step * direction
    residual = residual_ref[...] - step * image
    for layer in range(sh.layers):
        at = slice(layer * sh.slots, (layer + 1) * sh.slots)
        solution_ref[:, 0, 0, layer, :] = solution[0:3, at]
        final_ref[:, 0, 0, layer, :] = residual[0:3, at]


def local_fast(positions, counts, targets, landmark_index, coarse_matrix):
    both = ("gx", "gy")
    sh = Shape(positions, landmark_index, lax.axis_size("gx"), lax.axis_size("gy"))
    field = jax.ShapeDtypeStruct((8, sh.points), F32)
    vmem = pl.BlockSpec(memory_space=pltpu.VMEM)
    anyw = pl.BlockSpec(memory_space=pltpu.HBM)

    def call(kernel, name, out_shape, in_specs, cost=10**6, scratch=()):
        return pl.pallas_call(
            kernel,
            out_shape=out_shape,
            in_specs=in_specs,
            out_specs=jax.tree.map(lambda _: vmem, out_shape),
            scratch_shapes=scratch,
            name=name,
            compiler_params=pltpu.CompilerParams(vmem_limit_bytes=VMEM_BYTES),
            cost_estimate=pl.CostEstimate(flops=cost, bytes_accessed=10**5, transcendentals=0),
        )

    def part(kernel, *fixed):
        return functools.partial(kernel, sh, *fixed)

    def exchange(payload):
        return lax.all_to_all(payload, both, 0, 0)

    index = jnp.transpose(landmark_index, (1, 2, 0))
    turned = jnp.transpose(coarse_matrix)
    tile = jax.ShapeDtypeStruct((8, LANES), F32)
    own, marks, block = call(
        part(prepare_kernel),
        "prepare",
        (field, tile, tile),
        [anyw] * 5,
        scratch=[
            pltpu.VMEM(positions.shape, F32),
            pltpu.SMEM(counts.shape, jnp.int32),
            pltpu.VMEM(targets.shape, F32),
            pltpu.SMEM(index.shape, jnp.int32),
            pltpu.VMEM(turned.shape, F32),
            pltpu.VMEM((LANES, turned.shape[0]), F32),
            pltpu.SemaphoreType.DMA((5,)),
        ],
    )(*(pltpu.with_memory_space_constraint(x, pltpu.HBM)
        for x in (positions, counts, targets, index, turned)))
    row = jnp.stack([own, swap(own, "gx", 0), swap(own, "gx", 1)])

    def build(name, spans, *groups):
        columns = sum(stop - start for start, stop in spans)
        kern = jax.ShapeDtypeStruct((columns, sh.slots, sh.pairs), BF16)
        near = jax.ShapeDtypeStruct((columns, 48, sh.points), BF16)
        return call(
            part(build_kernel, spans),
            name,
            (kern, kern, near),
            [vmem] * (1 + len(groups)),
            cost=columns * 3 * 10**9,
        )(own, *groups)

    high0, low0, near0 = build("build_own", [(0, 1)], own[None])
    row, near0 = lax.optimization_barrier((row, near0))
    even, odd = swap(row, "gy", 0), swap(row, "gy", 1)
    high1, low1, near1 = build("build_pair", [(1, 3)], row)
    terms = call(
        part(terms_kernel),
        "terms",
        jax.ShapeDtypeStruct((sh.devices, 8, LANES), F32),
        [anyw] + [vmem] * 5,
    )(near1, marks, block, row, even, odd)
    terms, even, odd = lax.optimization_barrier((exchange(terms), even, odd))
    wide = 3 * sh.points + 2 * LANES
    spread_shape = jax.ShapeDtypeStruct((9, sh.window, sh.points), BF16)
    kern = jax.ShapeDtypeStruct((6, sh.slots, sh.pairs), BF16)
    payload, search, spread, rest, gram, image, high2, low2 = call(
        part(first_kernel),
        "first",
        (
            jax.ShapeDtypeStruct((sh.devices, 1, wide), F32),
            jax.ShapeDtypeStruct((9, 8, sh.points), F32),
            spread_shape,
            spread_shape,
            jax.ShapeDtypeStruct((sh.landmarks, LANES), F32),
            field,
            kern,
            kern,
        ),
        [vmem] * 10,
        scratch=[pltpu.VMEM((sh.landmarks, 48), BF16)],
    )(row, even, odd, terms, near0, near1, high0, high1, low0, low1)
    images = exchange(payload)

    line = jax.ShapeDtypeStruct((sh.devices, 1, LANES), F32)
    totals, sums, residual, following, product = call(
        part(second_kernel), "second", (line, tile, field, field, field), [vmem] * 13
    )(images, row, search, spread, rest, gram, image, high0, high1, high2, low0, low1, low2)
    totals = exchange(totals)

    out = jax.ShapeDtypeStruct(targets.shape, F32)
    return call(part(last_kernel), "last", (out, out), [vmem] * 7)(
        totals, sums, search, image, residual, following, product
    )


def fits_fast(positions, targets, landmark_index, coarse_matrix, nx, ny):
    owned = landmark_index.shape[2]
    return (
        nx * ny * owned == LANES
        and 6 * ny * owned + 4 <= LANES
        and nx >= 3
        and targets.shape[0] == 3
        and coarse_matrix.shape[0] == 8 * (LANES // 2 // (ny * owned))
    )


def local(positions, counts, targets, landmark_index, coarse_matrix):
    nx, ny = lax.axis_size("gx"), lax.axis_size("gy")
    if fits_fast(positions, targets, landmark_index, coarse_matrix, nx, ny):
        return local_fast(positions, counts, targets, landmark_index, coarse_matrix)
    return local_plain(positions, counts, targets, landmark_index, coarse_matrix)


def solution(mesh):
    return jax.shard_map(
        local,
        mesh=mesh,
        in_specs=(
            P(None, "gx", "gy", None, None),
            P("gx", "gy", None),
            P(None, "gx", "gy", None, None),
            P(),
            P("gy", "gx"),
        ),
        out_specs=(P(None, "gx", "gy", None, None), P(None, "gx", "gy", None, None)),
        check_vma=False,
    )
```

```python
import functools

import jax
import jax.numpy as jnp
from jax import lax
from jax.experimental import pallas as pl
from jax.experimental.pallas import tpu as pltpu
from jax.sharding import PartitionSpec as P

ITERS = 2


RIDGE_WEIGHT = 2.0
HIGHEST_PRECISION = lax.Precision.HIGHEST

F32 = jnp.float32
BF16 = jnp.bfloat16
LANES = 128
FAR = 4096.0
KERN_SCALE = 256.0
VMEM_BYTES = 8 * 2**20


def with_halo(x, sides, width):
    for axis, dim in sides:
        peers, length = (lax.axis_size(axis), x.shape[dim])
        up = [(i, (i + 1) % peers) for i in range(peers - 1)]
        down = [(j, i) for i, j in up]
        last = lax.slice_in_dim(x, length - width, length, axis=dim)
        leading = lax.slice_in_dim(x, 0, width, axis=dim)
        before = lax.ppermute(last, axis, up)
        after = lax.ppermute(leading, axis, down)
        x = jnp.concatenate([before, x, after], axis=dim)
    return x


def wendland(points_a, points_b):
    square_sum = jnp.zeros((points_a.shape[1], points_b.shape[1]), jnp.float32)
    for coord in range(3):
        offset = points_a[coord][:, None] - points_b[coord][None, :]
        square_sum = square_sum + offset * offset
    distance = jnp.sqrt(square_sum)
    remain = jnp.maximum(1.0 - distance, 0.0)
    remain = remain * remain
    return remain * remain * (4.0 * distance + 1.0)


def cell_rim(field):
    return with_halo(field, (("gx", 1), ("gy", 2)), 1)


def inner_sums(left, right):
    return jnp.sum(left * right, axis=(1, 2, 3, 4))


def per_component(values):
    return values[:, None, None, None, None]


def global_inner(values):
    return lax.psum(values, ("gx", "gy"))


def local_plain(positions, counts, targets, landmark_index, coarse_matrix):
    components = targets.shape[0]
    layer_count = positions.shape[3]
    slot_count = positions.shape[4]
    owned_count = landmark_index.shape[2]
    column_points = layer_count * slot_count
    slot_ids = jnp.arange(slot_count, dtype=jnp.int32)
    live_mask = (slot_ids[None, None, None, :] < counts[:, :, :, None]).astype(jnp.float32)
    live_flat = live_mask.reshape(1, column_points)
    rhs_field = live_mask[None] * targets
    ext_pos = cell_rim(positions)
    ext_cloud = ext_pos.reshape(3, 9 * column_points)
    own_points = positions.reshape(3, column_points)
    row_index = lax.axis_index("gx")
    col_index = lax.axis_index("gy")
    three_ids = jnp.arange(3, dtype=jnp.int32)
    near_rows = jnp.clip(row_index + three_ids - 1, 0, lax.axis_size("gx") - 1)
    near_cols = jnp.clip(col_index + three_ids - 1, 0, lax.axis_size("gy") - 1)
    near_index = landmark_index[near_rows[:, None], near_cols[None, :], :]
    ext_flat = ext_pos.reshape(3, 3, 3, column_points)
    near_pos = jnp.take_along_axis(ext_flat, near_index[None], axis=3)
    landmark_pos = near_pos[:, 1, 1, :]
    spread_kernel = wendland(own_points, near_pos.reshape(3, 9 * owned_count))

    def coarse_solve(terms):
        row_terms = lax.all_gather(terms, "gy", axis=0, tiled=True)
        return lax.psum_scatter(
            jnp.dot(coarse_matrix, row_terms, precision=HIGHEST_PRECISION),
            "gx",
            scatter_dimension=0,
            tiled=True,
        )

    def landmark_sums(vector):
        gather_kernel = wendland(landmark_pos, ext_cloud)
        ext_vec = cell_rim(vector).reshape(components, 9 * column_points)
        return jnp.einsum("kn,qn->kq", gather_kernel, ext_vec, precision=HIGHEST_PRECISION)

    def precondition(vector):
        terms = landmark_sums(vector)
        coarse = coarse_solve(terms)
        near_coarse = with_halo(
            coarse.reshape(1, 1, owned_count, components), (("gx", 0), ("gy", 1)), 1
        )
        near_coarse = near_coarse.reshape(9 * owned_count, components)
        spread = jnp.einsum("nm,mq->qn", spread_kernel, near_coarse, precision=HIGHEST_PRECISION)
        return vector / RIDGE_WEIGHT + (live_flat * spread).reshape(vector.shape)

    solution = jnp.zeros_like(rhs_field)
    residual = rhs_field
    search = precondition(residual)
    gamma = global_inner(inner_sums(residual, search))
    direction = search
    for iteration in range(ITERS):
        operator_ext_vec = cell_rim(direction)
        layer_out = []
        for layer in range(layer_count):
            low_layer = max(layer - 1, 0)
            high_layer = min(layer + 2, layer_count)
            near_points = ext_pos[:, :, :, low_layer:high_layer, :].reshape(3, -1)
            near_values = operator_ext_vec[:, :, :, low_layer:high_layer, :].reshape(components, -1)
            kern = wendland(positions[:, 0, 0, layer, :], near_points)
            layer_out.append(
                jnp.einsum("bn,qn->qb", kern, near_values, precision=HIGHEST_PRECISION)
            )
        product = jnp.stack(layer_out, axis=1).reshape(direction.shape)
        image = live_mask[None] * product + RIDGE_WEIGHT * direction
        alpha = gamma / global_inner(inner_sums(direction, image))
        solution = solution + per_component(alpha) * direction
        residual = residual - per_component(alpha) * image
        if iteration + 1 < ITERS:
            search = precondition(residual)
            gamma_new = global_inner(inner_sums(residual, search))
            direction = search + per_component(gamma_new / gamma) * direction
            gamma = gamma_new
    return (solution, residual)


def row_ids(lanes):
    return lax.broadcasted_iota(jnp.int32, (8, lanes), 0)


def lane_ids(rows, lanes):
    return lax.broadcasted_iota(jnp.int32, (rows, lanes), 1)


def split_three(values):
    high = values.astype(BF16).astype(F32)
    rest = values - high
    middle = rest.astype(BF16).astype(F32)
    low = (rest - middle).astype(BF16).astype(F32)
    return high, middle, low


def centred(column, centre):
    row = row_ids(column.shape[1])
    shift = jnp.where(row == 0, centre[0], jnp.where(row == 1, centre[1], centre[2]))
    xyz = jnp.where(row < 3, column - shift, 0.0)
    norm = 16.0 * jnp.sum(xyz * xyz, axis=0, keepdims=True)
    return row, xyz, norm + (1.0 - column[6:7, :]) * FAR


def near_features(column, centre):
    row, xyz, norm = centred(column, centre)
    high, middle, low = split_three(
        jnp.where(row == 3, norm, jnp.where(row == 4, 1.0, xyz))
    )
    return jnp.concatenate([high, middle, low, high, middle, high], axis=0)


def own_features(column, centre):
    row, xyz, norm = centred(column, centre)
    high, middle, low = split_three(
        jnp.where(row == 3, 1.0, jnp.where(row == 4, norm, -32.0 * xyz))
    )
    return jnp.concatenate([high, high, high, middle, middle, low], axis=0)


def scaled_wendland(square16):
    square16 = jnp.maximum(square16, 1e-6)
    four = square16 * lax.rsqrt(square16)
    remain = jnp.maximum(4.0 - four, 0.0)
    remain = remain * remain
    return remain * remain * (four + 1.0)


def bf16_dot(left, right):
    return jnp.dot(left, right, preferred_element_type=F32)


def full_dot(left, right, transposed=False):
    dims = (((1,), (1 if transposed else 0,)), ((), ()))
    return lax.dot_general(
        left, right, dims, precision=HIGHEST_PRECISION, preferred_element_type=F32
    )


def swap_partner(index, peers, odd):
    step = 1 - 2 * lax.rem(index + odd, 2)
    partner = index + step
    good = jnp.logical_and(partner >= 0, partner < peers)
    return jnp.where(good, partner, index)


def swap(x, axis, odd):
    peers = lax.axis_size(axis)
    pairs = []
    for i in range(odd, peers - 1, 2):
        pairs += [(i, i + 1), (i + 1, i)]
    return lax.ppermute(x, axis, pairs)


class Shape:
    def __init__(self, positions, landmark_index, nx, ny):
        self.nx, self.ny = nx, ny
        self.devices = nx * ny
        self.layers, self.slots = positions.shape[3], positions.shape[4]
        self.points = self.layers * self.slots
        self.owned = landmark_index.shape[2]
        self.row_landmarks = ny * self.owned
        self.landmarks = nx * self.row_landmarks
        self.window = 3 * self.row_landmarks
        self.blocks = []
        offset = 0
        for layer in range(self.layers):
            low, high = max(layer - 1, 0), min(layer + 2, self.layers)
            self.blocks.append((low, high, offset))
            offset += (high - low) * self.slots
        self.pairs = offset

    def centre(self, i, j):
        return (i.astype(F32) + 0.5, j.astype(F32) + 0.5, 0.5 * self.layers)

    def window_start(self, i):
        start = jnp.clip(i - 1, 0, self.nx - 3) * self.row_landmarks
        return pl.multiple_of(start, self.row_landmarks)

    def window_of(self, lanes, start):
        shift = lax.rem(LANES - start, LANES)
        return pltpu.roll(lanes, shift, axis=1)[:, : self.window]

    def near_ids(self, i, j):
        rows = [i, swap_partner(i, self.nx, 0), swap_partner(i, self.nx, 1)]
        cols = [j, swap_partner(j, self.ny, 0), swap_partner(j, self.ny, 1)]
        return rows, cols


def prepare_kernel(
    sh, pos_hbm, counts_hbm, tgt_hbm, index_hbm, coarse_hbm, own_ref, mark_ref, block_ref,
    pos_ref, counts_ref, tgt_ref, index_ref, coarse_ref, turned_ref, sems,
):
    copies = [
        pltpu.make_async_copy(source, target, sems.at[at])
        for at, (source, target) in enumerate(
            (
                (counts_hbm, counts_ref),
                (pos_hbm, pos_ref),
                (tgt_hbm, tgt_ref),
                (index_hbm, index_ref),
                (coarse_hbm, coarse_ref),
            )
        )
    ]
    for copy in copies:
        copy.start()
    for copy in copies:
        copy.wait()
    slot = lane_ids(1, sh.slots)
    for layer in range(sh.layers):
        live = (slot < counts_ref[0, 0, layer]).astype(F32)
        at = pl.ds(layer * sh.slots, sh.slots)
        own_ref[0:3, at] = pos_ref[:, 0, 0, layer, :]
        own_ref[3:6, at] = live * tgt_ref[:, 0, 0, layer, :]
        own_ref[6:7, at] = live
        own_ref[7:8, at] = jnp.zeros_like(live)
    i, j = lax.axis_index("gx"), lax.axis_index("gy")
    own = own_ref[...]
    lane = lane_ids(8, sh.points)
    lane8 = lane_ids(8, LANES)
    marks = jnp.zeros((8, LANES), F32)
    for k in range(sh.owned):
        hit = jnp.where(lane == index_ref[j, k, i], own, 0.0)
        marks = jnp.where(lane8 == k, jnp.sum(hit, axis=1, keepdims=True), marks)
    mark_ref[...] = marks
    count, width = coarse_ref.shape[1], coarse_ref.shape[0]
    fill = jnp.zeros((width, LANES - count), F32)
    turned_ref[...] = jnp.concatenate([coarse_ref[...], fill], axis=1).T
    groups = LANES // 2 // width
    pieces = [turned_ref[pl.ds(g, 8, stride=groups), :] for g in range(groups)]
    block_ref[...] = jnp.concatenate(pieces + pieces, axis=1)


def terms_kernel(
    sh, after_ref, mark_ref, block_ref, row_ref, even_ref, odd_ref, pay_ref,
):
    i, j = lax.axis_index("gx"), lax.axis_index("gy")
    row1 = lax.broadcasted_iota(jnp.int32, (8, 1), 0)
    marks = [mark_ref[:, k : k + 1] for k in range(sh.owned)]
    coords = []
    for coord in range(3):
        column = jnp.zeros((8, 1), F32)
        for k in range(sh.owned):
            column = jnp.where(row1 == k, marks[k][coord : coord + 1, :], column)
        coords.append(column)

    def add_column(column, sums):
        square = jnp.zeros((8, sh.points), F32)
        for coord in range(3):
            offset = column[coord : coord + 1, :] - coords[coord]
            square = square + offset * offset
        kern = scaled_wendland(16.0 * square)
        return tuple(
            total + kern * column[3 + q : 4 + q, :] for q, total in enumerate(sums)
        )

    sums = tuple(jnp.zeros((8, sh.points), F32) for _ in range(3))
    for ref in (row_ref, even_ref, odd_ref):
        for c in range(3):
            sums = add_column(ref[c], sums)
    terms = [jnp.sum(s, axis=1, keepdims=True) * (1.0 / KERN_SCALE) for s in sums]
    lane8 = lane_ids(8, LANES)
    row8 = row_ids(LANES)
    half = LANES // 2
    first = (i * sh.ny + j) * sh.owned
    tile = jnp.zeros((8, LANES), F32)
    for k in range(sh.owned):
        column = jnp.where(row1 < 3, marks[k], 0.0)
        for q in range(3):
            column = jnp.where(row1 == 3 + q, terms[q][k : k + 1, :], column)
        tile = jnp.where(lane8 == first + k, column, tile)
    block = block_ref[...]
    own_half = (lane8 >= half) == (first >= half)
    tile = jnp.where(own_half, tile, block)
    for d in range(sh.devices):
        pay_ref[d] = tile


def build_layer(sh, near, own, layer, high_ref, low_ref, to):
    low, high, offset = sh.blocks[layer]
    lhs = near[layer * sh.slots : (layer + 1) * sh.slots]
    for target in range(low, high):
        square = bf16_dot(lhs, own[:, target * sh.slots : (target + 1) * sh.slots])
        kern = scaled_wendland(square)
        at = slice(offset + (target - low) * sh.slots, offset + (target - low + 1) * sh.slots)
        high_ref[to, :, at] = kern.astype(BF16)
        head = high_ref[to, :, at].astype(F32)
        low_ref[to, :, at] = (kern - head).astype(BF16)


def build_kernel(sh, spans, own_ref, *refs):
    group_refs, (high_ref, low_ref, near_ref) = refs[: len(spans)], refs[len(spans) :]
    centre = sh.centre(lax.axis_index("gx"), lax.axis_index("gy"))
    own = own_features(own_ref[...], centre).astype(BF16)

    def one(ref, c, to):
        features = near_features(ref[c], centre).astype(BF16)
        near_ref[to] = features
        near = features.T
        for layer in range(sh.layers):
            build_layer(sh, near, own, layer, high_ref, low_ref, to)

    base = 0
    for ref, (start, stop) in zip(group_refs, spans):
        for c in range(start, stop):
            one(ref, c, base + c - start)
        base += stop - start


def built(refs, group, c):
    if group:
        return refs[2], (group - 1) * 3 + c
    return (refs[1], c - 1) if c else (refs[0], 0)


def split_rows(values):
    head = values.astype(BF16)
    tail = values - head.astype(F32)
    return head, jnp.concatenate([head.astype(F32), tail], axis=0).astype(BF16)


def apply_layer(sh, high_ref, low_ref, c, head, both, layer, out_ref):
    low, high, offset = sh.blocks[layer]
    at = slice(layer * sh.slots, (layer + 1) * sh.slots)
    width = (high - low) * sh.slots
    main = bf16_dot(both[:, at], high_ref[c, :, offset : offset + width])
    rest = bf16_dot(head[:, at], low_ref[c, :, offset : offset + width])
    out_ref[:, low * sh.slots : high * sh.slots] += main[:8] + main[8:] + rest


def apply_column(sh, high_ref, low_ref, c, values, out_ref):
    head, both = split_rows(values)
    for layer in range(sh.layers):
        apply_layer(sh, high_ref, low_ref, c, head, both, layer, out_ref)


def spread_dot(part, high, low):
    head, both = split_rows(part)
    main = bf16_dot(both, high)
    return main[:8] + main[8:] + bf16_dot(head, low)


def coarse_dot(terms, gram_ref):
    gram = gram_ref[...]
    high = gram.astype(BF16)
    return spread_dot(terms, high, (gram - high.astype(F32)).astype(BF16))


def gathered_matrix(sh, recv_ref, gram_ref):
    width = sh.row_landmarks
    half = LANES // 2
    groups = half // width
    lane = lane_ids(sh.ny * 8, LANES)
    for g in range(groups):
        total = jnp.zeros((sh.ny * 8, LANES), F32)
        for i in range(sh.nx):
            tiles = jnp.concatenate([recv_ref[i * sh.ny + j] for j in range(sh.ny)], axis=0)
            base = half if i * width < half else 0
            shift = (i * width - base - g * width) % LANES
            if shift:
                tiles = pltpu.roll(tiles, shift, axis=1)
            keep = jnp.logical_and(lane >= i * width, lane < (i + 1) * width)
            total = jnp.where(keep, tiles, total)
        for j in range(sh.ny):
            for r in range(8):
                p = groups * r + g
                at = (p // sh.owned) * width + j * sh.owned + p % sh.owned
                gram_ref[at : at + 1, :] = total[j * 8 + r : j * 8 + r + 1, :]


def rhs_rows(column, lanes):
    return jnp.where(
        row_ids(lanes) < 3, jnp.concatenate([column[3:8], column[0:3]], axis=0), 0.0
    )


def first_kernel(
    sh, row_ref, even_ref, odd_ref, recv_ref, near0_ref, near1_ref,
    high0_ref, high1_ref, low0_ref, low1_ref,
    pay_ref, search_ref, spread_ref, rest_ref, gram_ref, image_ref, high2_ref, low2_ref,
    mark_ref,
):
    high_refs = (high0_ref, high1_ref, high2_ref)
    low_refs = (low0_ref, low1_ref, low2_ref)
    i, j = lax.axis_index("gx"), lax.axis_index("gy")
    centre = sh.centre(i, j)
    half = LANES // 2
    image_ref[...] = jnp.zeros_like(image_ref)
    rows, _ = sh.near_ids(i, j)
    column_refs = (row_ref, even_ref, odd_ref)
    near_values, marks, parts, ready = {}, [], [], {}

    def gather():
        totals = [jnp.zeros((8, LANES), F32), jnp.zeros((8, LANES), F32)]
        for d in range(sh.devices):
            side = 0 if d * sh.owned < half else 1
            totals[side] = totals[side] + recv_ref[d]
        gathered = jnp.where(lane_ids(8, LANES) < half, totals[0], totals[1])
        gathered_matrix(sh, recv_ref, gram_ref)
        return jnp.where(row_ids(LANES) == 6, 1.0, gathered)

    def solve(gathered):
        mark_ref[...] = own_features(gathered, centre).T.astype(BF16)
        coarse = coarse_dot(rhs_rows(gathered, LANES), gram_ref)
        for near_row in rows:
            start = sh.window_start(near_row)
            marks.append(mark_ref[pl.ds(start, sh.window), :])
            parts.append(sh.window_of(coarse, start))

    def start_column(at):
        group, c = divmod(at, 3)
        near = near_values.pop(at) if group else (near1_ref[c - 1] if c else near0_ref[0])
        spread = scaled_wendland(bf16_dot(marks[c], near)) * (1.0 / KERN_SCALE)
        head = spread.astype(BF16)
        rest = (spread - head.astype(F32)).astype(BF16)
        spread_ref[at] = head
        rest_ref[at] = rest
        residual = rhs_rows(column_refs[group][c], sh.points)
        search = residual * (1.0 / RIDGE_WEIGHT) + spread_dot(parts[c], head, rest)
        search_ref[at] = search
        ready[at] = split_rows(search)

    def apply_piece(at, layer):
        head, both = ready[at]
        high_ref, kern_at = built(high_refs, *divmod(at, 3))
        low_ref, _ = built(low_refs, *divmod(at, 3))
        apply_layer(sh, high_ref, low_ref, kern_at, head, both, layer, image_ref)

    own_side = own_features(row_ref[0], centre).astype(BF16)
    plan = [[], [0, 1], [2, 3], [4, 5], [6], [7], [8]]
    for step in range(6):
        group, c = divmod(step + 3, 3)
        near_values[step + 3] = near_features(column_refs[group][c], centre).astype(BF16)
        near = near_values[step + 3].T
        following = list(plan[step + 1])
        for layer in range(sh.layers):
            build_layer(sh, near, own_side, layer, high2_ref, low2_ref, step)
            for at in plan[step]:
                apply_piece(at, layer)
            if step == 0 and layer == 0:
                gathered = gather()
            if step == 0 and layer == 1:
                solve(gathered)
            if layer >= 2 and following:
                start_column(following.pop(0))
    for at in plan[6]:
        for layer in range(sh.layers):
            apply_piece(at, layer)
    residual = rhs_rows(row_ref[0], sh.points)
    search = search_ref[0]
    image = image_ref[...] * (1.0 / KERN_SCALE) + RIDGE_WEIGHT * search
    image_ref[...] = image
    gamma = jnp.sum(residual * search, axis=1, keepdims=True)
    delta = jnp.sum(search * image, axis=1, keepdims=True)
    head, both = split_rows(image)
    across = (((1,), (1,)), ((), ()))
    main = lax.dot_general(both, spread_ref[0], across, preferred_element_type=F32)
    tail = lax.dot_general(head, rest_ref[0], across, preferred_element_type=F32)
    window = main[:8] + main[8:] + tail
    lane = lane_ids(8, LANES)
    fill = jnp.zeros((8, LANES - sh.window), F32)
    tile = jnp.concatenate([window, fill], axis=1)
    tile = jnp.where(lane == 2 * sh.window, gamma, tile)
    tile = jnp.where(lane == 2 * sh.window + 1, delta, tile)
    moved = pltpu.roll(tile, sh.window, axis=1)
    lane1 = lane_ids(1, LANES)
    pair = jnp.where(
        jnp.logical_and(lane1 >= sh.window, lane1 < 2 * sh.window), moved[1:2], tile[0:1]
    )
    ends = jnp.where(lane1 == 2 * sh.window + 2, gamma[1:2], pair)
    ends = jnp.where(lane1 == 2 * sh.window + 3, delta[1:2], ends)
    lines = [ends, tile[2:3]]
    for d in range(sh.devices):
        for q in range(3):
            pay_ref[d, :, q * sh.points : (q + 1) * sh.points] = image[q : q + 1, :]
        for at, line in enumerate(lines):
            start = 3 * sh.points + at * LANES
            pay_ref[d, :, start : start + LANES] = line


def second_kernel(
    sh, recv_ref, row_ref, search_ref, spread_ref, rest_ref, gram_ref, image_ref, *refs,
):
    second_body(
        sh, recv_ref, row_ref, search_ref, spread_ref, rest_ref, gram_ref, image_ref,
        refs[0:3], refs[3:6], *refs[6:],
    )


def second_body(
    sh, recv_ref, row_ref, search_ref, spread_ref, rest_ref, gram_ref, image_ref,
    high_refs, low_refs, pay_ref, sums_ref, residual_ref, next_ref, product_ref,
):
    i, j = lax.axis_index("gx"), lax.axis_index("gy")
    lane = lane_ids(8, LANES)
    row8 = row_ids(LANES)
    terms = jnp.zeros((8, LANES), F32)
    scalars = jnp.zeros((8, LANES), F32)
    for a in range(sh.nx):
        lines = []
        for at in (3 * sh.points, 3 * sh.points + LANES):
            total = recv_ref[a * sh.ny, :, at : at + LANES]
            for b in range(1, sh.ny):
                total = total + recv_ref[a * sh.ny + b, :, at : at + LANES]
            lines.append(total)
        pair = jnp.broadcast_to(lines[0], (8, LANES))
        third = jnp.broadcast_to(lines[1], (8, LANES))
        tile = jnp.where(row8 == 2, third, pair)
        scalars = scalars + tile
        start = min(max(a - 1, 0), sh.nx - 3) * sh.row_landmarks
        first = pltpu.roll(tile, start, axis=1) if start else tile
        other = pltpu.roll(tile, (start - sh.window) % LANES, axis=1)
        inside = jnp.logical_and(lane >= start, lane < start + sh.window)
        value = jnp.where(row8 == 1, other, first)
        terms = terms + jnp.where(jnp.logical_and(inside, row8 < 3), value, 0.0)
    ends = 2 * sh.window

    def column(at):
        second = scalars[:, ends + 2 + at : ends + 3 + at]
        value = scalars[:, ends + at : ends + at + 1]
        return jnp.where(lax.broadcasted_iota(jnp.int32, (8, 1), 0) == 1, second, value)

    gamma, delta = column(0), column(1)
    row1 = lax.broadcasted_iota(jnp.int32, (8, 1), 0)
    alpha = jnp.where(row1 < 3, gamma / jnp.where(row1 < 3, delta, 1.0), 0.0)
    coarse = coarse_dot(terms, gram_ref)
    product_ref[...] = jnp.zeros_like(product_ref)
    rows, cols = sh.near_ids(i, j)
    zeros5 = jnp.zeros((5, sh.points), F32)
    parts = [sh.window_of(coarse, sh.window_start(near_row)) for near_row in rows]
    for group in range(3):
        for c in range(3):
            at = group * 3 + c
            high_ref, kern_at = built(high_refs, group, c)
            low_ref = built(low_refs, group, c)[0]
            source = rows[c] * sh.ny + cols[group]
            image = jnp.concatenate(
                [recv_ref[source, :, q * sh.points : (q + 1) * sh.points] for q in range(3)]
                + [zeros5],
                axis=0,
            )
            step = image * (1.0 / RIDGE_WEIGHT) + spread_dot(parts[c], spread_ref[at], rest_ref[at])
            search = search_ref[at] - alpha * step
            if at == 0:
                next_ref[...] = search
            apply_column(sh, high_ref, low_ref, kern_at, search, product_ref)
    residual = rhs_rows(row_ref[0], sh.points)
    image = image_ref[...]
    residual = residual - alpha * image
    residual_ref[...] = residual
    search = next_ref[...]
    product = product_ref[...] * (1.0 / KERN_SCALE) + RIDGE_WEIGHT * search
    product_ref[...] = product
    sums = [
        jnp.sum(residual * search, axis=1, keepdims=True),
        jnp.sum(search * product, axis=1, keepdims=True),
        jnp.sum(search * image, axis=1, keepdims=True)
        + jnp.sum(search_ref[0] * product, axis=1, keepdims=True),
    ]
    line = jnp.zeros((1, LANES), F32)
    lane1 = lane_ids(1, LANES)
    for at, value in enumerate(sums):
        for q in range(3):
            line = jnp.where(lane1 == 3 * at + q, value[q : q + 1, :], line)
    for d in range(sh.devices):
        pay_ref[d] = line
    sums_ref[...] = jnp.where(lane == 0, gamma, jnp.where(lane == 1, delta, 0.0))


def last_kernel(
    sh, recv_ref, sums_ref, search_ref, image_ref, residual_ref, next_ref, product_ref,
    solution_ref, final_ref,
):
    total = recv_ref[0]
    for d in range(1, sh.devices):
        total = total + recv_ref[d]
    row1 = lax.broadcasted_iota(jnp.int32, (8, 1), 0)
    good = row1 < 3

    def column(at):
        value = jnp.zeros((8, 1), F32)
        for q in range(3):
            value = jnp.where(row1 == q, total[:, 3 * at + q : 3 * at + q + 1], value)
        return value

    own = sums_ref[...]
    gamma, delta = own[:, 0:1], own[:, 1:2]
    gamma_new, inner, cross = column(0), column(1), column(2)
    safe_gamma = jnp.where(good, gamma, 1.0)
    safe_delta = jnp.where(good, delta, 1.0)
    alpha = gamma / safe_delta
    beta = gamma_new / safe_gamma
    curve = inner + beta * cross + beta * beta * delta
    step = gamma_new / jnp.where(good, curve, 1.0)
    direction = next_ref[...] + beta * search_ref[0]
    image = product_ref[...] + beta * image_ref[...]
    solution = alpha * search_ref[0] + step * direction
    residual = residual_ref[...] - step * image
    for layer in range(sh.layers):
        at = slice(layer * sh.slots, (layer + 1) * sh.slots)
        solution_ref[:, 0, 0, layer, :] = solution[0:3, at]
        final_ref[:, 0, 0, layer, :] = residual[0:3, at]


def local_fast(positions, counts, targets, landmark_index, coarse_matrix):
    both = ("gx", "gy")
    sh = Shape(positions, landmark_index, lax.axis_size("gx"), lax.axis_size("gy"))
    field = jax.ShapeDtypeStruct((8, sh.points), F32)
    vmem = pl.BlockSpec(memory_space=pltpu.VMEM)
    anyw = pl.BlockSpec(memory_space=pltpu.HBM)

    def call(kernel, name, out_shape, in_specs, cost=10**6, scratch=()):
        return pl.pallas_call(
            kernel,
            out_shape=out_shape,
            in_specs=in_specs,
            out_specs=jax.tree.map(lambda _: vmem, out_shape),
            scratch_shapes=scratch,
            name=name,
            compiler_params=pltpu.CompilerParams(vmem_limit_bytes=VMEM_BYTES),
            cost_estimate=pl.CostEstimate(flops=cost, bytes_accessed=10**5, transcendentals=0),
        )

    def part(kernel, *fixed):
        return functools.partial(kernel, sh, *fixed)

    def exchange(payload):
        return lax.all_to_all(payload, both, 0, 0)

    index = jnp.transpose(landmark_index, (1, 2, 0))
    turned = jnp.transpose(coarse_matrix)
    tile = jax.ShapeDtypeStruct((8, LANES), F32)
    own, marks, block = call(
        part(prepare_kernel),
        "prepare",
        (field, tile, tile),
        [anyw] * 5,
        scratch=[
            pltpu.VMEM(positions.shape, F32),
            pltpu.SMEM(counts.shape, jnp.int32),
            pltpu.VMEM(targets.shape, F32),
            pltpu.SMEM(index.shape, jnp.int32),
            pltpu.VMEM(turned.shape, F32),
            pltpu.VMEM((LANES, turned.shape[0]), F32),
            pltpu.SemaphoreType.DMA((5,)),
        ],
    )(*(pltpu.with_memory_space_constraint(x, pltpu.HBM)
        for x in (positions, counts, targets, index, turned)))
    row = jnp.stack([own, swap(own, "gx", 0), swap(own, "gx", 1)])

    def build(name, spans, *groups):
        columns = sum(stop - start for start, stop in spans)
        kern = jax.ShapeDtypeStruct((columns, sh.slots, sh.pairs), BF16)
        near = jax.ShapeDtypeStruct((columns, 48, sh.points), BF16)
        return call(
            part(build_kernel, spans),
            name,
            (kern, kern, near),
            [vmem] * (1 + len(groups)),
            cost=columns * 3 * 10**9,
        )(own, *groups)

    high0, low0, near0 = build("build_own", [(0, 1)], own[None])
    row, near0 = lax.optimization_barrier((row, near0))
    even, odd = swap(row, "gy", 0), swap(row, "gy", 1)
    high1, low1, near1 = build("build_pair", [(1, 3)], row)
    terms = call(
        part(terms_kernel),
        "terms",
        jax.ShapeDtypeStruct((sh.devices, 8, LANES), F32),
        [anyw] + [vmem] * 5,
    )(near1, marks, block, row, even, odd)
    terms, even, odd = lax.optimization_barrier((exchange(terms), even, odd))
    wide = 3 * sh.points + 2 * LANES
    spread_shape = jax.ShapeDtypeStruct((9, sh.window, sh.points), BF16)
    kern = jax.ShapeDtypeStruct((6, sh.slots, sh.pairs), BF16)
    payload, search, spread, rest, gram, image, high2, low2 = call(
        part(first_kernel),
        "first",
        (
            jax.ShapeDtypeStruct((sh.devices, 1, wide), F32),
            jax.ShapeDtypeStruct((9, 8, sh.points), F32),
            spread_shape,
            spread_shape,
            jax.ShapeDtypeStruct((sh.landmarks, LANES), F32),
            field,
            kern,
            kern,
        ),
        [vmem] * 10,
        scratch=[pltpu.VMEM((sh.landmarks, 48), BF16)],
    )(row, even, odd, terms, near0, near1, high0, high1, low0, low1)
    images = exchange(payload)

    line = jax.ShapeDtypeStruct((sh.devices, 1, LANES), F32)
    totals, sums, residual, following, product = call(
        part(second_kernel), "second", (line, tile, field, field, field), [vmem] * 13
    )(images, row, search, spread, rest, gram, image, high0, high1, high2, low0, low1, low2)
    totals = exchange(totals)

    out = jax.ShapeDtypeStruct(targets.shape, F32)
    return call(part(last_kernel), "last", (out, out), [vmem] * 7)(
        totals, sums, search, image, residual, following, product
    )


def fits_fast(positions, targets, landmark_index, coarse_matrix, nx, ny):
    owned = landmark_index.shape[2]
    return (
        nx * ny * owned == LANES
        and 6 * ny * owned + 4 <= LANES
        and nx >= 3
        and targets.shape[0] == 3
        and coarse_matrix.shape[0] == 8 * (LANES // 2 // (ny * owned))
    )


def local(positions, counts, targets, landmark_index, coarse_matrix):
    nx, ny = lax.axis_size("gx"), lax.axis_size("gy")
    if fits_fast(positions, targets, landmark_index, coarse_matrix, nx, ny):
        return local_fast(positions, counts, targets, landmark_index, coarse_matrix)
    return local_plain(positions, counts, targets, landmark_index, coarse_matrix)


def solution(mesh):
    return jax.shard_map(
        local,
        mesh=mesh,
        in_specs=(
            P(None, "gx", "gy", None, None),
            P("gx", "gy", None),
            P(None, "gx", "gy", None, None),
            P(),
            P("gy", "gx"),
        ),
        out_specs=(P(None, "gx", "gy", None, None), P(None, "gx", "gy", None, None)),
        check_vma=False,
    )
```

```python
import functools

import jax
import jax.numpy as jnp
from jax import lax
from jax.experimental import pallas as pl
from jax.experimental.pallas import tpu as pltpu
from jax.sharding import PartitionSpec as P

ITERS = 2


RIDGE_WEIGHT = 2.0
HIGHEST_PRECISION = lax.Precision.HIGHEST

F32 = jnp.float32
BF16 = jnp.bfloat16
LANES = 128
FAR = 4096.0
KERN_SCALE = 256.0
VMEM_BYTES = 8 * 2**20


def with_halo(x, sides, width):
    for axis, dim in sides:
        peers, length = (lax.axis_size(axis), x.shape[dim])
        up = [(i, (i + 1) % peers) for i in range(peers - 1)]
        down = [(j, i) for i, j in up]
        last = lax.slice_in_dim(x, length - width, length, axis=dim)
        leading = lax.slice_in_dim(x, 0, width, axis=dim)
        before = lax.ppermute(last, axis, up)
        after = lax.ppermute(leading, axis, down)
        x = jnp.concatenate([before, x, after], axis=dim)
    return x


def wendland(points_a, points_b):
    square_sum = jnp.zeros((points_a.shape[1], points_b.shape[1]), jnp.float32)
    for coord in range(3):
        offset = points_a[coord][:, None] - points_b[coord][None, :]
        square_sum = square_sum + offset * offset
    distance = jnp.sqrt(square_sum)
    remain = jnp.maximum(1.0 - distance, 0.0)
    remain = remain * remain
    return remain * remain * (4.0 * distance + 1.0)


def cell_rim(field):
    return with_halo(field, (("gx", 1), ("gy", 2)), 1)


def inner_sums(left, right):
    return jnp.sum(left * right, axis=(1, 2, 3, 4))


def per_component(values):
    return values[:, None, None, None, None]


def global_inner(values):
    return lax.psum(values, ("gx", "gy"))


def local_plain(positions, counts, targets, landmark_index, coarse_matrix):
    components = targets.shape[0]
    layer_count = positions.shape[3]
    slot_count = positions.shape[4]
    owned_count = landmark_index.shape[2]
    column_points = layer_count * slot_count
    slot_ids = jnp.arange(slot_count, dtype=jnp.int32)
    live_mask = (slot_ids[None, None, None, :] < counts[:, :, :, None]).astype(jnp.float32)
    live_flat = live_mask.reshape(1, column_points)
    rhs_field = live_mask[None] * targets
    ext_pos = cell_rim(positions)
    ext_cloud = ext_pos.reshape(3, 9 * column_points)
    own_points = positions.reshape(3, column_points)
    row_index = lax.axis_index("gx")
    col_index = lax.axis_index("gy")
    three_ids = jnp.arange(3, dtype=jnp.int32)
    near_rows = jnp.clip(row_index + three_ids - 1, 0, lax.axis_size("gx") - 1)
    near_cols = jnp.clip(col_index + three_ids - 1, 0, lax.axis_size("gy") - 1)
    near_index = landmark_index[near_rows[:, None], near_cols[None, :], :]
    ext_flat = ext_pos.reshape(3, 3, 3, column_points)
    near_pos = jnp.take_along_axis(ext_flat, near_index[None], axis=3)
    landmark_pos = near_pos[:, 1, 1, :]
    spread_kernel = wendland(own_points, near_pos.reshape(3, 9 * owned_count))

    def coarse_solve(terms):
        row_terms = lax.all_gather(terms, "gy", axis=0, tiled=True)
        return lax.psum_scatter(
            jnp.dot(coarse_matrix, row_terms, precision=HIGHEST_PRECISION),
            "gx",
            scatter_dimension=0,
            tiled=True,
        )

    def landmark_sums(vector):
        gather_kernel = wendland(landmark_pos, ext_cloud)
        ext_vec = cell_rim(vector).reshape(components, 9 * column_points)
        return jnp.einsum("kn,qn->kq", gather_kernel, ext_vec, precision=HIGHEST_PRECISION)

    def precondition(vector):
        terms = landmark_sums(vector)
        coarse = coarse_solve(terms)
        near_coarse = with_halo(
            coarse.reshape(1, 1, owned_count, components), (("gx", 0), ("gy", 1)), 1
        )
        near_coarse = near_coarse.reshape(9 * owned_count, components)
        spread = jnp.einsum("nm,mq->qn", spread_kernel, near_coarse, precision=HIGHEST_PRECISION)
        return vector / RIDGE_WEIGHT + (live_flat * spread).reshape(vector.shape)

    solution = jnp.zeros_like(rhs_field)
    residual = rhs_field
    search = precondition(residual)
    gamma = global_inner(inner_sums(residual, search))
    direction = search
    for iteration in range(ITERS):
        operator_ext_vec = cell_rim(direction)
        layer_out = []
        for layer in range(layer_count):
            low_layer = max(layer - 1, 0)
            high_layer = min(layer + 2, layer_count)
            near_points = ext_pos[:, :, :, low_layer:high_layer, :].reshape(3, -1)
            near_values = operator_ext_vec[:, :, :, low_layer:high_layer, :].reshape(components, -1)
            kern = wendland(positions[:, 0, 0, layer, :], near_points)
            layer_out.append(
                jnp.einsum("bn,qn->qb", kern, near_values, precision=HIGHEST_PRECISION)
            )
        product = jnp.stack(layer_out, axis=1).reshape(direction.shape)
        image = live_mask[None] * product + RIDGE_WEIGHT * direction
        alpha = gamma / global_inner(inner_sums(direction, image))
        solution = solution + per_component(alpha) * direction
        residual = residual - per_component(alpha) * image
        if iteration + 1 < ITERS:
            search = precondition(residual)
            gamma_new = global_inner(inner_sums(residual, search))
            direction = search + per_component(gamma_new / gamma) * direction
            gamma = gamma_new
    return (solution, residual)


def row_ids(lanes):
    return lax.broadcasted_iota(jnp.int32, (8, lanes), 0)


def lane_ids(rows, lanes):
    return lax.broadcasted_iota(jnp.int32, (rows, lanes), 1)


def split_three(values):
    high = values.astype(BF16).astype(F32)
    rest = values - high
    middle = rest.astype(BF16).astype(F32)
    low = (rest - middle).astype(BF16).astype(F32)
    return high, middle, low


def centred(column, centre):
    row = row_ids(column.shape[1])
    shift = jnp.where(row == 0, centre[0], jnp.where(row == 1, centre[1], centre[2]))
    xyz = jnp.where(row < 3, column - shift, 0.0)
    norm = 16.0 * jnp.sum(xyz * xyz, axis=0, keepdims=True)
    return row, xyz, norm + (1.0 - column[6:7, :]) * FAR


def near_features(column, centre):
    row, xyz, norm = centred(column, centre)
    high, middle, low = split_three(
        jnp.where(row == 3, norm, jnp.where(row == 4, 1.0, xyz))
    )
    return jnp.concatenate([high, middle, low, high, middle, high], axis=0)


def own_features(column, centre):
    row, xyz, norm = centred(column, centre)
    high, middle, low = split_three(
        jnp.where(row == 3, 1.0, jnp.where(row == 4, norm, -32.0 * xyz))
    )
    return jnp.concatenate([high, high, high, middle, middle, low], axis=0)


def scaled_wendland(square16):
    square16 = jnp.maximum(square16, 1e-6)
    four = square16 * lax.rsqrt(square16)
    remain = jnp.maximum(4.0 - four, 0.0)
    remain = remain * remain
    return remain * remain * (four + 1.0)


def bf16_dot(left, right):
    return jnp.dot(left, right, preferred_element_type=F32)


def full_dot(left, right, transposed=False):
    dims = (((1,), (1 if transposed else 0,)), ((), ()))
    return lax.dot_general(
        left, right, dims, precision=HIGHEST_PRECISION, preferred_element_type=F32
    )


def swap_partner(index, peers, odd):
    step = 1 - 2 * lax.rem(index + odd, 2)
    partner = index + step
    good = jnp.logical_and(partner >= 0, partner < peers)
    return jnp.where(good, partner, index)


def swap(x, axis, odd):
    peers = lax.axis_size(axis)
    pairs = []
    for i in range(odd, peers - 1, 2):
        pairs += [(i, i + 1), (i + 1, i)]
    return lax.ppermute(x, axis, pairs)


class Shape:
    def __init__(self, positions, landmark_index, nx, ny):
        self.nx, self.ny = nx, ny
        self.devices = nx * ny
        self.layers, self.slots = positions.shape[3], positions.shape[4]
        self.points = self.layers * self.slots
        self.owned = landmark_index.shape[2]
        self.row_landmarks = ny * self.owned
        self.landmarks = nx * self.row_landmarks
        self.window = 3 * self.row_landmarks
        self.blocks = []
        offset = 0
        for layer in range(self.layers):
            low, high = max(layer - 1, 0), min(layer + 2, self.layers)
            self.blocks.append((low, high, offset))
            offset += (high - low) * self.slots
        self.pairs = offset

    def centre(self, i, j):
        return (i.astype(F32) + 0.5, j.astype(F32) + 0.5, 0.5 * self.layers)

    def window_start(self, i):
        start = jnp.clip(i - 1, 0, self.nx - 3) * self.row_landmarks
        return pl.multiple_of(start, self.row_landmarks)

    def window_of(self, lanes, start):
        shift = lax.rem(LANES - start, LANES)
        return pltpu.roll(lanes, shift, axis=1)[:, : self.window]

    def near_ids(self, i, j):
        rows = [i, swap_partner(i, self.nx, 0), swap_partner(i, self.nx, 1)]
        cols = [j, swap_partner(j, self.ny, 0), swap_partner(j, self.ny, 1)]
        return rows, cols


def prepare_kernel(
    sh, pos_hbm, counts_hbm, tgt_hbm, index_hbm, coarse_hbm, own_ref, mark_ref, block_ref,
    pos_ref, counts_ref, tgt_ref, index_ref, coarse_ref, turned_ref, sems,
):
    copies = [
        pltpu.make_async_copy(source, target, sems.at[at])
        for at, (source, target) in enumerate(
            (
                (counts_hbm, counts_ref),
                (pos_hbm, pos_ref),
                (tgt_hbm, tgt_ref),
                (index_hbm, index_ref),
                (coarse_hbm, coarse_ref),
            )
        )
    ]
    for copy in copies:
        copy.start()
    for copy in copies:
        copy.wait()
    slot = lane_ids(1, sh.slots)
    for layer in range(sh.layers):
        live = (slot < counts_ref[0, 0, layer]).astype(F32)
        at = pl.ds(layer * sh.slots, sh.slots)
        own_ref[0:3, at] = pos_ref[:, 0, 0, layer, :]
        own_ref[3:6, at] = live * tgt_ref[:, 0, 0, layer, :]
        own_ref[6:7, at] = live
        own_ref[7:8, at] = jnp.zeros_like(live)
    i, j = lax.axis_index("gx"), lax.axis_index("gy")
    own = own_ref[...]
    lane = lane_ids(8, sh.points)
    lane8 = lane_ids(8, LANES)
    marks = jnp.zeros((8, LANES), F32)
    for k in range(sh.owned):
        hit = jnp.where(lane == index_ref[j, k, i], own, 0.0)
        marks = jnp.where(lane8 == k, jnp.sum(hit, axis=1, keepdims=True), marks)
    mark_ref[...] = marks
    count, width = coarse_ref.shape[1], coarse_ref.shape[0]
    fill = jnp.zeros((width, LANES - count), F32)
    turned_ref[...] = jnp.concatenate([coarse_ref[...], fill], axis=1).T
    groups = LANES // 2 // width
    pieces = [turned_ref[pl.ds(g, 8, stride=groups), :] for g in range(groups)]
    block_ref[...] = jnp.concatenate(pieces + pieces, axis=1)


def terms_kernel(
    sh, after_ref, mark_ref, block_ref, row_ref, even_ref, odd_ref, pay_ref,
):
    i, j = lax.axis_index("gx"), lax.axis_index("gy")
    row1 = lax.broadcasted_iota(jnp.int32, (8, 1), 0)
    marks = [mark_ref[:, k : k + 1] for k in range(sh.owned)]
    coords = []
    for coord in range(3):
        column = jnp.zeros((8, 1), F32)
        for k in range(sh.owned):
            column = jnp.where(row1 == k, marks[k][coord : coord + 1, :], column)
        coords.append(column)

    def add_column(column, sums):
        square = jnp.zeros((8, sh.points), F32)
        for coord in range(3):
            offset = column[coord : coord + 1, :] - coords[coord]
            square = square + offset * offset
        kern = scaled_wendland(16.0 * square)
        return tuple(
            total + kern * column[3 + q : 4 + q, :] for q, total in enumerate(sums)
        )

    sums = tuple(jnp.zeros((8, sh.points), F32) for _ in range(3))
    for ref in (row_ref, even_ref, odd_ref):
        for c in range(3):
            sums = add_column(ref[c], sums)
    terms = [jnp.sum(s, axis=1, keepdims=True) * (1.0 / KERN_SCALE) for s in sums]
    lane8 = lane_ids(8, LANES)
    row8 = row_ids(LANES)
    half = LANES // 2
    first = (i * sh.ny + j) * sh.owned
    tile = jnp.zeros((8, LANES), F32)
    for k in range(sh.owned):
        column = jnp.where(row1 < 3, marks[k], 0.0)
        for q in range(3):
            column = jnp.where(row1 == 3 + q, terms[q][k : k + 1, :], column)
        tile = jnp.where(lane8 == first + k, column, tile)
    block = block_ref[...]
    own_half = (lane8 >= half) == (first >= half)
    tile = jnp.where(own_half, tile, block)
    for d in range(sh.devices):
        pay_ref[d] = tile


def build_layer(sh, near, own, layer, high_ref, low_ref, to):
    low, high, offset = sh.blocks[layer]
    lhs = near[layer * sh.slots : (layer + 1) * sh.slots]
    for target in range(low, high):
        square = bf16_dot(lhs, own[:, target * sh.slots : (target + 1) * sh.slots])
        kern = scaled_wendland(square)
        at = slice(offset + (target - low) * sh.slots, offset + (target - low + 1) * sh.slots)
        high_ref[to, :, at] = kern.astype(BF16)
        head = high_ref[to, :, at].astype(F32)
        low_ref[to, :, at] = (kern - head).astype(BF16)


def build_kernel(sh, spans, own_ref, *refs):
    group_refs, (high_ref, low_ref, near_ref) = refs[: len(spans)], refs[len(spans) :]
    centre = sh.centre(lax.axis_index("gx"), lax.axis_index("gy"))
    own = own_features(own_ref[...], centre).astype(BF16)

    def one(ref, c, to):
        features = near_features(ref[c], centre).astype(BF16)
        near_ref[to] = features
        near = features.T
        for layer in range(sh.layers):
            build_layer(sh, near, own, layer, high_ref, low_ref, to)

    base = 0
    for ref, (start, stop) in zip(group_refs, spans):
        for c in range(start, stop):
            one(ref, c, base + c - start)
        base += stop - start


def built(refs, group, c):
    if group:
        return refs[2], (group - 1) * 3 + c
    return (refs[1], c - 1) if c else (refs[0], 0)


def split_rows(values):
    head = values.astype(BF16)
    tail = values - head.astype(F32)
    return head, jnp.concatenate([head.astype(F32), tail], axis=0).astype(BF16)


def apply_layer(sh, high_ref, low_ref, c, head, both, layer, out_ref):
    low, high, offset = sh.blocks[layer]
    at = slice(layer * sh.slots, (layer + 1) * sh.slots)
    width = (high - low) * sh.slots
    main = bf16_dot(both[:, at], high_ref[c, :, offset : offset + width])
    rest = bf16_dot(head[:, at], low_ref[c, :, offset : offset + width])
    out_ref[:, low * sh.slots : high * sh.slots] += main[:8] + main[8:] + rest


def apply_column(sh, high_ref, low_ref, c, values, out_ref):
    head, both = split_rows(values)
    for layer in range(sh.layers):
        apply_layer(sh, high_ref, low_ref, c, head, both, layer, out_ref)


def spread_dot(part, high, low):
    head, both = split_rows(part)
    main = bf16_dot(both, high)
    return main[:8] + main[8:] + bf16_dot(head, low)


def coarse_dot(terms, gram_ref):
    gram = gram_ref[...]
    high = gram.astype(BF16)
    return spread_dot(terms, high, (gram - high.astype(F32)).astype(BF16))


def gathered_matrix(sh, recv_ref, gram_ref):
    width = sh.row_landmarks
    half = LANES // 2
    groups = half // width
    lane = lane_ids(sh.ny * 8, LANES)
    for g in range(groups):
        total = jnp.zeros((sh.ny * 8, LANES), F32)
        for i in range(sh.nx):
            tiles = jnp.concatenate([recv_ref[i * sh.ny + j] for j in range(sh.ny)], axis=0)
            base = half if i * width < half else 0
            shift = (i * width - base - g * width) % LANES
            if shift:
                tiles = pltpu.roll(tiles, shift, axis=1)
            keep = jnp.logical_and(lane >= i * width, lane < (i + 1) * width)
            total = jnp.where(keep, tiles, total)
        for j in range(sh.ny):
            for r in range(8):
                p = groups * r + g
                at = (p // sh.owned) * width + j * sh.owned + p % sh.owned
                gram_ref[at : at + 1, :] = total[j * 8 + r : j * 8 + r + 1, :]


def rhs_rows(column, lanes):
    return jnp.where(
        row_ids(lanes) < 3, jnp.concatenate([column[3:8], column[0:3]], axis=0), 0.0
    )


def first_kernel(
    sh, row_ref, even_ref, odd_ref, recv_ref, near0_ref, near1_ref,
    high0_ref, high1_ref, low0_ref, low1_ref,
    pay_ref, search_ref, spread_ref, rest_ref, gram_ref, image_ref, high2_ref, low2_ref,
    mark_ref,
):
    high_refs = (high0_ref, high1_ref, high2_ref)
    low_refs = (low0_ref, low1_ref, low2_ref)
    i, j = lax.axis_index("gx"), lax.axis_index("gy")
    centre = sh.centre(i, j)
    half = LANES // 2
    image_ref[...] = jnp.zeros_like(image_ref)
    rows, _ = sh.near_ids(i, j)
    column_refs = (row_ref, even_ref, odd_ref)
    near_values, marks, parts, ready = {}, [], [], {}

    def gather():
        totals = [jnp.zeros((8, LANES), F32), jnp.zeros((8, LANES), F32)]
        for d in range(sh.devices):
            side = 0 if d * sh.owned < half else 1
            totals[side] = totals[side] + recv_ref[d]
        gathered = jnp.where(lane_ids(8, LANES) < half, totals[0], totals[1])
        gathered_matrix(sh, recv_ref, gram_ref)
        return jnp.where(row_ids(LANES) == 6, 1.0, gathered)

    def solve(gathered):
        mark_ref[...] = own_features(gathered, centre).T.astype(BF16)
        coarse = coarse_dot(rhs_rows(gathered, LANES), gram_ref)
        for near_row in rows:
            start = sh.window_start(near_row)
            marks.append(mark_ref[pl.ds(start, sh.window), :])
            parts.append(sh.window_of(coarse, start))

    def start_column(at):
        group, c = divmod(at, 3)
        near = near_values.pop(at) if group else (near1_ref[c - 1] if c else near0_ref[0])
        spread = scaled_wendland(bf16_dot(marks[c], near)) * (1.0 / KERN_SCALE)
        head = spread.astype(BF16)
        rest = (spread - head.astype(F32)).astype(BF16)
        spread_ref[at] = head
        rest_ref[at] = rest
        residual = rhs_rows(column_refs[group][c], sh.points)
        search = residual * (1.0 / RIDGE_WEIGHT) + spread_dot(parts[c], head, rest)
        search_ref[at] = search
        ready[at] = split_rows(search)

    def apply_piece(at, layer):
        head, both = ready[at]
        high_ref, kern_at = built(high_refs, *divmod(at, 3))
        low_ref, _ = built(low_refs, *divmod(at, 3))
        apply_layer(sh, high_ref, low_ref, kern_at, head, both, layer, image_ref)

    own_side = own_features(row_ref[0], centre).astype(BF16)
    plan = [[], [0, 1], [2, 3], [4, 5], [6], [7], [8]]
    for step in range(6):
        group, c = divmod(step + 3, 3)
        near_values[step + 3] = near_features(column_refs[group][c], centre).astype(BF16)
        near = near_values[step + 3].T
        following = list(plan[step + 1])
        for layer in range(sh.layers):
            build_layer(sh, near, own_side, layer, high2_ref, low2_ref, step)
            for at in plan[step]:
                apply_piece(at, layer)
            if step == 5:
                if layer == 0:
                    start_column(following.pop(0))
                else:
                    apply_piece(8, layer - 1)
            if step == 0 and layer == 0:
                gathered = gather()
            if step == 0 and layer == 1:
                solve(gathered)
            if layer >= 2 and following:
                start_column(following.pop(0))
    apply_piece(8, sh.layers - 1)
    residual = rhs_rows(row_ref[0], sh.points)
    search = search_ref[0]
    image = image_ref[...] * (1.0 / KERN_SCALE) + RIDGE_WEIGHT * search
    image_ref[...] = image
    gamma = jnp.sum(residual * search, axis=1, keepdims=True)
    delta = jnp.sum(search * image, axis=1, keepdims=True)
    head, both = split_rows(image)
    across = (((1,), (1,)), ((), ()))
    main = lax.dot_general(both, spread_ref[0], across, preferred_element_type=F32)
    tail = lax.dot_general(head, rest_ref[0], across, preferred_element_type=F32)
    window = main[:8] + main[8:] + tail
    lane = lane_ids(8, LANES)
    fill = jnp.zeros((8, LANES - sh.window), F32)
    tile = jnp.concatenate([window, fill], axis=1)
    tile = jnp.where(lane == 2 * sh.window, gamma, tile)
    tile = jnp.where(lane == 2 * sh.window + 1, delta, tile)
    moved = pltpu.roll(tile, sh.window, axis=1)
    lane1 = lane_ids(1, LANES)
    pair = jnp.where(
        jnp.logical_and(lane1 >= sh.window, lane1 < 2 * sh.window), moved[1:2], tile[0:1]
    )
    ends = jnp.where(lane1 == 2 * sh.window + 2, gamma[1:2], pair)
    ends = jnp.where(lane1 == 2 * sh.window + 3, delta[1:2], ends)
    lines = [ends, tile[2:3]]
    for d in range(sh.devices):
        for q in range(3):
            pay_ref[d, :, q * sh.points : (q + 1) * sh.points] = image[q : q + 1, :]
        for at, line in enumerate(lines):
            start = 3 * sh.points + at * LANES
            pay_ref[d, :, start : start + LANES] = line


def second_kernel(
    sh, recv_ref, row_ref, search_ref, spread_ref, rest_ref, gram_ref, image_ref, *refs,
):
    second_body(
        sh, recv_ref, row_ref, search_ref, spread_ref, rest_ref, gram_ref, image_ref,
        refs[0:3], refs[3:6], *refs[6:],
    )


def second_body(
    sh, recv_ref, row_ref, search_ref, spread_ref, rest_ref, gram_ref, image_ref,
    high_refs, low_refs, pay_ref, sums_ref, residual_ref, next_ref, product_ref,
):
    i, j = lax.axis_index("gx"), lax.axis_index("gy")
    lane = lane_ids(8, LANES)
    row8 = row_ids(LANES)
    terms = jnp.zeros((8, LANES), F32)
    scalars = jnp.zeros((8, LANES), F32)
    for a in range(sh.nx):
        lines = []
        for at in (3 * sh.points, 3 * sh.points + LANES):
            total = recv_ref[a * sh.ny, :, at : at + LANES]
            for b in range(1, sh.ny):
                total = total + recv_ref[a * sh.ny + b, :, at : at + LANES]
            lines.append(total)
        pair = jnp.broadcast_to(lines[0], (8, LANES))
        third = jnp.broadcast_to(lines[1], (8, LANES))
        tile = jnp.where(row8 == 2, third, pair)
        scalars = scalars + tile
        start = min(max(a - 1, 0), sh.nx - 3) * sh.row_landmarks
        first = pltpu.roll(tile, start, axis=1) if start else tile
        other = pltpu.roll(tile, (start - sh.window) % LANES, axis=1)
        inside = jnp.logical_and(lane >= start, lane < start + sh.window)
        value = jnp.where(row8 == 1, other, first)
        terms = terms + jnp.where(jnp.logical_and(inside, row8 < 3), value, 0.0)
    ends = 2 * sh.window

    def column(at):
        second = scalars[:, ends + 2 + at : ends + 3 + at]
        value = scalars[:, ends + at : ends + at + 1]
        return jnp.where(lax.broadcasted_iota(jnp.int32, (8, 1), 0) == 1, second, value)

    gamma, delta = column(0), column(1)
    row1 = lax.broadcasted_iota(jnp.int32, (8, 1), 0)
    alpha = jnp.where(row1 < 3, gamma / jnp.where(row1 < 3, delta, 1.0), 0.0)
    coarse = coarse_dot(terms, gram_ref)
    product_ref[...] = jnp.zeros_like(product_ref)
    rows, cols = sh.near_ids(i, j)
    zeros5 = jnp.zeros((5, sh.points), F32)
    parts = [sh.window_of(coarse, sh.window_start(near_row)) for near_row in rows]
    for group in range(3):
        for c in range(3):
            at = group * 3 + c
            high_ref, kern_at = built(high_refs, group, c)
            low_ref = built(low_refs, group, c)[0]
            source = rows[c] * sh.ny + cols[group]
            image = jnp.concatenate(
                [recv_ref[source, :, q * sh.points : (q + 1) * sh.points] for q in range(3)]
                + [zeros5],
                axis=0,
            )
            step = image * (1.0 / RIDGE_WEIGHT) + spread_dot(parts[c], spread_ref[at], rest_ref[at])
            search = search_ref[at] - alpha * step
            if at == 0:
                next_ref[...] = search
            apply_column(sh, high_ref, low_ref, kern_at, search, product_ref)
    residual = rhs_rows(row_ref[0], sh.points)
    image = image_ref[...]
    residual = residual - alpha * image
    residual_ref[...] = residual
    search = next_ref[...]
    product = product_ref[...] * (1.0 / KERN_SCALE) + RIDGE_WEIGHT * search
    product_ref[...] = product
    sums = [
        jnp.sum(residual * search, axis=1, keepdims=True),
        jnp.sum(search * product, axis=1, keepdims=True),
        jnp.sum(search * image, axis=1, keepdims=True)
        + jnp.sum(search_ref[0] * product, axis=1, keepdims=True),
    ]
    line = jnp.zeros((1, LANES), F32)
    lane1 = lane_ids(1, LANES)
    for at, value in enumerate(sums):
        for q in range(3):
            line = jnp.where(lane1 == 3 * at + q, value[q : q + 1, :], line)
    for d in range(sh.devices):
        pay_ref[d] = line
    sums_ref[...] = jnp.where(lane == 0, gamma, jnp.where(lane == 1, delta, 0.0))


def last_kernel(
    sh, recv_ref, sums_ref, search_ref, image_ref, residual_ref, next_ref, product_ref,
    solution_ref, final_ref,
):
    total = recv_ref[0]
    for d in range(1, sh.devices):
        total = total + recv_ref[d]
    row1 = lax.broadcasted_iota(jnp.int32, (8, 1), 0)
    good = row1 < 3

    def column(at):
        value = jnp.zeros((8, 1), F32)
        for q in range(3):
            value = jnp.where(row1 == q, total[:, 3 * at + q : 3 * at + q + 1], value)
        return value

    own = sums_ref[...]
    gamma, delta = own[:, 0:1], own[:, 1:2]
    gamma_new, inner, cross = column(0), column(1), column(2)
    safe_gamma = jnp.where(good, gamma, 1.0)
    safe_delta = jnp.where(good, delta, 1.0)
    alpha = gamma / safe_delta
    beta = gamma_new / safe_gamma
    curve = inner + beta * cross + beta * beta * delta
    step = gamma_new / jnp.where(good, curve, 1.0)
    direction = next_ref[...] + beta * search_ref[0]
    image = product_ref[...] + beta * image_ref[...]
    solution = alpha * search_ref[0] + step * direction
    residual = residual_ref[...] - step * image
    for layer in range(sh.layers):
        at = slice(layer * sh.slots, (layer + 1) * sh.slots)
        solution_ref[:, 0, 0, layer, :] = solution[0:3, at]
        final_ref[:, 0, 0, layer, :] = residual[0:3, at]


def local_fast(positions, counts, targets, landmark_index, coarse_matrix):
    both = ("gx", "gy")
    sh = Shape(positions, landmark_index, lax.axis_size("gx"), lax.axis_size("gy"))
    field = jax.ShapeDtypeStruct((8, sh.points), F32)
    vmem = pl.BlockSpec(memory_space=pltpu.VMEM)
    anyw = pl.BlockSpec(memory_space=pltpu.HBM)

    def call(kernel, name, out_shape, in_specs, cost=10**6, scratch=()):
        return pl.pallas_call(
            kernel,
            out_shape=out_shape,
            in_specs=in_specs,
            out_specs=jax.tree.map(lambda _: vmem, out_shape),
            scratch_shapes=scratch,
            name=name,
            compiler_params=pltpu.CompilerParams(vmem_limit_bytes=VMEM_BYTES),
            cost_estimate=pl.CostEstimate(flops=cost, bytes_accessed=10**5, transcendentals=0),
        )

    def part(kernel, *fixed):
        return functools.partial(kernel, sh, *fixed)

    def exchange(payload):
        return lax.all_to_all(payload, both, 0, 0)

    index = jnp.transpose(landmark_index, (1, 2, 0))
    turned = jnp.transpose(coarse_matrix)
    tile = jax.ShapeDtypeStruct((8, LANES), F32)
    own, marks, block = call(
        part(prepare_kernel),
        "prepare",
        (field, tile, tile),
        [anyw] * 5,
        scratch=[
            pltpu.VMEM(positions.shape, F32),
            pltpu.SMEM(counts.shape, jnp.int32),
            pltpu.VMEM(targets.shape, F32),
            pltpu.SMEM(index.shape, jnp.int32),
            pltpu.VMEM(turned.shape, F32),
            pltpu.VMEM((LANES, turned.shape[0]), F32),
            pltpu.SemaphoreType.DMA((5,)),
        ],
    )(*(pltpu.with_memory_space_constraint(x, pltpu.HBM)
        for x in (positions, counts, targets, index, turned)))
    row = jnp.stack([own, swap(own, "gx", 0), swap(own, "gx", 1)])

    def build(name, spans, *groups):
        columns = sum(stop - start for start, stop in spans)
        kern = jax.ShapeDtypeStruct((columns, sh.slots, sh.pairs), BF16)
        near = jax.ShapeDtypeStruct((columns, 48, sh.points), BF16)
        return call(
            part(build_kernel, spans),
            name,
            (kern, kern, near),
            [vmem] * (1 + len(groups)),
            cost=columns * 3 * 10**9,
        )(own, *groups)

    high0, low0, near0 = build("build_own", [(0, 1)], own[None])
    row, near0 = lax.optimization_barrier((row, near0))
    even, odd = swap(row, "gy", 0), swap(row, "gy", 1)
    high1, low1, near1 = build("build_pair", [(1, 3)], row)
    terms = call(
        part(terms_kernel),
        "terms",
        jax.ShapeDtypeStruct((sh.devices, 8, LANES), F32),
        [anyw] + [vmem] * 5,
    )(near1, marks, block, row, even, odd)
    terms, even, odd = lax.optimization_barrier((exchange(terms), even, odd))
    wide = 3 * sh.points + 2 * LANES
    spread_shape = jax.ShapeDtypeStruct((9, sh.window, sh.points), BF16)
    kern = jax.ShapeDtypeStruct((6, sh.slots, sh.pairs), BF16)
    payload, search, spread, rest, gram, image, high2, low2 = call(
        part(first_kernel),
        "first",
        (
            jax.ShapeDtypeStruct((sh.devices, 1, wide), F32),
            jax.ShapeDtypeStruct((9, 8, sh.points), F32),
            spread_shape,
            spread_shape,
            jax.ShapeDtypeStruct((sh.landmarks, LANES), F32),
            field,
            kern,
            kern,
        ),
        [vmem] * 10,
        scratch=[pltpu.VMEM((sh.landmarks, 48), BF16)],
    )(row, even, odd, terms, near0, near1, high0, high1, low0, low1)
    images = exchange(payload)

    line = jax.ShapeDtypeStruct((sh.devices, 1, LANES), F32)
    totals, sums, residual, following, product = call(
        part(second_kernel), "second", (line, tile, field, field, field), [vmem] * 13
    )(images, row, search, spread, rest, gram, image, high0, high1, high2, low0, low1, low2)
    totals = exchange(totals)

    out = jax.ShapeDtypeStruct(targets.shape, F32)
    return call(part(last_kernel), "last", (out, out), [vmem] * 7)(
        totals, sums, search, image, residual, following, product
    )


def fits_fast(positions, targets, landmark_index, coarse_matrix, nx, ny):
    owned = landmark_index.shape[2]
    return (
        nx * ny * owned == LANES
        and 6 * ny * owned + 4 <= LANES
        and nx >= 3
        and targets.shape[0] == 3
        and coarse_matrix.shape[0] == 8 * (LANES // 2 // (ny * owned))
    )


def local(positions, counts, targets, landmark_index, coarse_matrix):
    nx, ny = lax.axis_size("gx"), lax.axis_size("gy")
    if fits_fast(positions, targets, landmark_index, coarse_matrix, nx, ny):
        return local_fast(positions, counts, targets, landmark_index, coarse_matrix)
    return local_plain(positions, counts, targets, landmark_index, coarse_matrix)


def solution(mesh):
    return jax.shard_map(
        local,
        mesh=mesh,
        in_specs=(
            P(None, "gx", "gy", None, None),
            P("gx", "gy", None),
            P(None, "gx", "gy", None, None),
            P(),
            P("gy", "gx"),
        ),
        out_specs=(P(None, "gx", "gy", None, None), P(None, "gx", "gy", None, None)),
        check_vma=False,
    )
```

```python
import functools

import jax
import jax.numpy as jnp
from jax import lax
from jax.experimental import pallas as pl
from jax.experimental.pallas import tpu as pltpu
from jax.sharding import PartitionSpec as P

ITERS = 2


RIDGE_WEIGHT = 2.0
HIGHEST_PRECISION = lax.Precision.HIGHEST

F32 = jnp.float32
BF16 = jnp.bfloat16
LANES = 128
FAR = 4096.0
KERN_SCALE = 256.0
VMEM_BYTES = 8 * 2**20


def with_halo(x, sides, width):
    for axis, dim in sides:
        peers, length = (lax.axis_size(axis), x.shape[dim])
        up = [(i, (i + 1) % peers) for i in range(peers - 1)]
        down = [(j, i) for i, j in up]
        last = lax.slice_in_dim(x, length - width, length, axis=dim)
        leading = lax.slice_in_dim(x, 0, width, axis=dim)
        before = lax.ppermute(last, axis, up)
        after = lax.ppermute(leading, axis, down)
        x = jnp.concatenate([before, x, after], axis=dim)
    return x


def wendland(points_a, points_b):
    square_sum = jnp.zeros((points_a.shape[1], points_b.shape[1]), jnp.float32)
    for coord in range(3):
        offset = points_a[coord][:, None] - points_b[coord][None, :]
        square_sum = square_sum + offset * offset
    distance = jnp.sqrt(square_sum)
    remain = jnp.maximum(1.0 - distance, 0.0)
    remain = remain * remain
    return remain * remain * (4.0 * distance + 1.0)


def cell_rim(field):
    return with_halo(field, (("gx", 1), ("gy", 2)), 1)


def inner_sums(left, right):
    return jnp.sum(left * right, axis=(1, 2, 3, 4))


def per_component(values):
    return values[:, None, None, None, None]


def global_inner(values):
    return lax.psum(values, ("gx", "gy"))


def local_plain(positions, counts, targets, landmark_index, coarse_matrix):
    components = targets.shape[0]
    layer_count = positions.shape[3]
    slot_count = positions.shape[4]
    owned_count = landmark_index.shape[2]
    column_points = layer_count * slot_count
    slot_ids = jnp.arange(slot_count, dtype=jnp.int32)
    live_mask = (slot_ids[None, None, None, :] < counts[:, :, :, None]).astype(jnp.float32)
    live_flat = live_mask.reshape(1, column_points)
    rhs_field = live_mask[None] * targets
    ext_pos = cell_rim(positions)
    ext_cloud = ext_pos.reshape(3, 9 * column_points)
    own_points = positions.reshape(3, column_points)
    row_index = lax.axis_index("gx")
    col_index = lax.axis_index("gy")
    three_ids = jnp.arange(3, dtype=jnp.int32)
    near_rows = jnp.clip(row_index + three_ids - 1, 0, lax.axis_size("gx") - 1)
    near_cols = jnp.clip(col_index + three_ids - 1, 0, lax.axis_size("gy") - 1)
    near_index = landmark_index[near_rows[:, None], near_cols[None, :], :]
    ext_flat = ext_pos.reshape(3, 3, 3, column_points)
    near_pos = jnp.take_along_axis(ext_flat, near_index[None], axis=3)
    landmark_pos = near_pos[:, 1, 1, :]
    spread_kernel = wendland(own_points, near_pos.reshape(3, 9 * owned_count))

    def coarse_solve(terms):
        row_terms = lax.all_gather(terms, "gy", axis=0, tiled=True)
        return lax.psum_scatter(
            jnp.dot(coarse_matrix, row_terms, precision=HIGHEST_PRECISION),
            "gx",
            scatter_dimension=0,
            tiled=True,
        )

    def landmark_sums(vector):
        gather_kernel = wendland(landmark_pos, ext_cloud)
        ext_vec = cell_rim(vector).reshape(components, 9 * column_points)
        return jnp.einsum("kn,qn->kq", gather_kernel, ext_vec, precision=HIGHEST_PRECISION)

    def precondition(vector):
        terms = landmark_sums(vector)
        coarse = coarse_solve(terms)
        near_coarse = with_halo(
            coarse.reshape(1, 1, owned_count, components), (("gx", 0), ("gy", 1)), 1
        )
        near_coarse = near_coarse.reshape(9 * owned_count, components)
        spread = jnp.einsum("nm,mq->qn", spread_kernel, near_coarse, precision=HIGHEST_PRECISION)
        return vector / RIDGE_WEIGHT + (live_flat * spread).reshape(vector.shape)

    solution = jnp.zeros_like(rhs_field)
    residual = rhs_field
    search = precondition(residual)
    gamma = global_inner(inner_sums(residual, search))
    direction = search
    for iteration in range(ITERS):
        operator_ext_vec = cell_rim(direction)
        layer_out = []
        for layer in range(layer_count):
            low_layer = max(layer - 1, 0)
            high_layer = min(layer + 2, layer_count)
            near_points = ext_pos[:, :, :, low_layer:high_layer, :].reshape(3, -1)
            near_values = operator_ext_vec[:, :, :, low_layer:high_layer, :].reshape(components, -1)
            kern = wendland(positions[:, 0, 0, layer, :], near_points)
            layer_out.append(
                jnp.einsum("bn,qn->qb", kern, near_values, precision=HIGHEST_PRECISION)
            )
        product = jnp.stack(layer_out, axis=1).reshape(direction.shape)
        image = live_mask[None] * product + RIDGE_WEIGHT * direction
        alpha = gamma / global_inner(inner_sums(direction, image))
        solution = solution + per_component(alpha) * direction
        residual = residual - per_component(alpha) * image
        if iteration + 1 < ITERS:
            search = precondition(residual)
            gamma_new = global_inner(inner_sums(residual, search))
            direction = search + per_component(gamma_new / gamma) * direction
            gamma = gamma_new
    return (solution, residual)


def row_ids(lanes):
    return lax.broadcasted_iota(jnp.int32, (8, lanes), 0)


def lane_ids(rows, lanes):
    return lax.broadcasted_iota(jnp.int32, (rows, lanes), 1)


def split_three(values):
    high = values.astype(BF16).astype(F32)
    rest = values - high
    middle = rest.astype(BF16).astype(F32)
    low = (rest - middle).astype(BF16).astype(F32)
    return high, middle, low


def centred(column, centre):
    row = row_ids(column.shape[1])
    shift = jnp.where(row == 0, centre[0], jnp.where(row == 1, centre[1], centre[2]))
    xyz = jnp.where(row < 3, column - shift, 0.0)
    norm = 16.0 * jnp.sum(xyz * xyz, axis=0, keepdims=True)
    return row, xyz, norm + (1.0 - column[6:7, :]) * FAR


def near_features(column, centre):
    row, xyz, norm = centred(column, centre)
    high, middle, low = split_three(
        jnp.where(row == 3, norm, jnp.where(row == 4, 1.0, xyz))
    )
    return jnp.concatenate([high, middle, low, high, middle, high], axis=0)


def own_features(column, centre):
    row, xyz, norm = centred(column, centre)
    high, middle, low = split_three(
        jnp.where(row == 3, 1.0, jnp.where(row == 4, norm, -32.0 * xyz))
    )
    return jnp.concatenate([high, high, high, middle, middle, low], axis=0)


def scaled_wendland(square16):
    square16 = jnp.maximum(square16, 1e-6)
    four = square16 * lax.rsqrt(square16)
    remain = jnp.maximum(4.0 - four, 0.0)
    remain = remain * remain
    return remain * remain * (four + 1.0)


def bf16_dot(left, right):
    return jnp.dot(left, right, preferred_element_type=F32)


def full_dot(left, right, transposed=False):
    dims = (((1,), (1 if transposed else 0,)), ((), ()))
    return lax.dot_general(
        left, right, dims, precision=HIGHEST_PRECISION, preferred_element_type=F32
    )


def swap_partner(index, peers, odd):
    step = 1 - 2 * lax.rem(index + odd, 2)
    partner = index + step
    good = jnp.logical_and(partner >= 0, partner < peers)
    return jnp.where(good, partner, index)


def swap(x, axis, odd):
    peers = lax.axis_size(axis)
    pairs = []
    for i in range(odd, peers - 1, 2):
        pairs += [(i, i + 1), (i + 1, i)]
    return lax.ppermute(x, axis, pairs)


class Shape:
    def __init__(self, positions, landmark_index, nx, ny):
        self.nx, self.ny = nx, ny
        self.devices = nx * ny
        self.layers, self.slots = positions.shape[3], positions.shape[4]
        self.points = self.layers * self.slots
        self.owned = landmark_index.shape[2]
        self.row_landmarks = ny * self.owned
        self.landmarks = nx * self.row_landmarks
        self.window = 3 * self.row_landmarks
        self.blocks = []
        offset = 0
        for layer in range(self.layers):
            low, high = max(layer - 1, 0), min(layer + 2, self.layers)
            self.blocks.append((low, high, offset))
            offset += (high - low) * self.slots
        self.pairs = offset

    def centre(self, i, j):
        return (i.astype(F32) + 0.5, j.astype(F32) + 0.5, 0.5 * self.layers)

    def window_start(self, i):
        start = jnp.clip(i - 1, 0, self.nx - 3) * self.row_landmarks
        return pl.multiple_of(start, self.row_landmarks)

    def window_of(self, lanes, start):
        shift = lax.rem(LANES - start, LANES)
        return pltpu.roll(lanes, shift, axis=1)[:, : self.window]

    def near_ids(self, i, j):
        rows = [i, swap_partner(i, self.nx, 0), swap_partner(i, self.nx, 1)]
        cols = [j, swap_partner(j, self.ny, 0), swap_partner(j, self.ny, 1)]
        return rows, cols


def prepare_kernel(
    sh, pos_hbm, counts_hbm, tgt_hbm, index_hbm, coarse_hbm, own_ref, mark_ref, block_ref,
    pos_ref, counts_ref, tgt_ref, index_ref, coarse_ref, turned_ref, sems,
):
    copies = [
        pltpu.make_async_copy(source, target, sems.at[at])
        for at, (source, target) in enumerate(
            (
                (counts_hbm, counts_ref),
                (pos_hbm, pos_ref),
                (tgt_hbm, tgt_ref),
                (index_hbm, index_ref),
                (coarse_hbm, coarse_ref),
            )
        )
    ]
    for copy in copies:
        copy.start()
    for copy in copies:
        copy.wait()
    slot = lane_ids(1, sh.slots)
    for layer in range(sh.layers):
        live = (slot < counts_ref[0, 0, layer]).astype(F32)
        at = pl.ds(layer * sh.slots, sh.slots)
        own_ref[0:3, at] = pos_ref[:, 0, 0, layer, :]
        own_ref[3:6, at] = live * tgt_ref[:, 0, 0, layer, :]
        own_ref[6:7, at] = live
        own_ref[7:8, at] = jnp.zeros_like(live)
    i, j = lax.axis_index("gx"), lax.axis_index("gy")
    own = own_ref[...]
    lane = lane_ids(8, sh.points)
    lane8 = lane_ids(8, LANES)
    marks = jnp.zeros((8, LANES), F32)
    for k in range(sh.owned):
        hit = jnp.where(lane == index_ref[j, k, i], own, 0.0)
        marks = jnp.where(lane8 == k, jnp.sum(hit, axis=1, keepdims=True), marks)
    mark_ref[...] = marks
    count, width = coarse_ref.shape[1], coarse_ref.shape[0]
    fill = jnp.zeros((width, LANES - count), F32)
    turned_ref[...] = jnp.concatenate([coarse_ref[...], fill], axis=1).T
    groups = LANES // 2 // width
    pieces = [turned_ref[pl.ds(g, 8, stride=groups), :] for g in range(groups)]
    block_ref[...] = jnp.concatenate(pieces + pieces, axis=1)


def terms_kernel(
    sh, after_ref, mark_ref, block_ref, row_ref, even_ref, odd_ref, pay_ref,
):
    i, j = lax.axis_index("gx"), lax.axis_index("gy")
    row1 = lax.broadcasted_iota(jnp.int32, (8, 1), 0)
    marks = [mark_ref[:, k : k + 1] for k in range(sh.owned)]
    coords = []
    for coord in range(3):
        column = jnp.zeros((8, 1), F32)
        for k in range(sh.owned):
            column = jnp.where(row1 == k, marks[k][coord : coord + 1, :], column)
        coords.append(column)

    def add_column(column, sums):
        square = jnp.zeros((8, sh.points), F32)
        for coord in range(3):
            offset = column[coord : coord + 1, :] - coords[coord]
            square = square + offset * offset
        kern = scaled_wendland(16.0 * square)
        return tuple(
            total + kern * column[3 + q : 4 + q, :] for q, total in enumerate(sums)
        )

    sums = tuple(jnp.zeros((8, sh.points), F32) for _ in range(3))
    for ref in (row_ref, even_ref, odd_ref):
        for c in range(3):
            sums = add_column(ref[c], sums)
    terms = [jnp.sum(s, axis=1, keepdims=True) * (1.0 / KERN_SCALE) for s in sums]
    lane8 = lane_ids(8, LANES)
    row8 = row_ids(LANES)
    half = LANES // 2
    first = (i * sh.ny + j) * sh.owned
    tile = jnp.zeros((8, LANES), F32)
    for k in range(sh.owned):
        column = jnp.where(row1 < 3, marks[k], 0.0)
        for q in range(3):
            column = jnp.where(row1 == 3 + q, terms[q][k : k + 1, :], column)
        tile = jnp.where(lane8 == first + k, column, tile)
    block = block_ref[...]
    own_half = (lane8 >= half) == (first >= half)
    tile = jnp.where(own_half, tile, block)
    for d in range(sh.devices):
        pay_ref[d] = tile


def build_layer(sh, near, own, layer, high_ref, low_ref, to):
    low, high, offset = sh.blocks[layer]
    lhs = near[layer * sh.slots : (layer + 1) * sh.slots]
    for target in range(low, high):
        square = bf16_dot(lhs, own[:, target * sh.slots : (target + 1) * sh.slots])
        kern = scaled_wendland(square)
        at = slice(offset + (target - low) * sh.slots, offset + (target - low + 1) * sh.slots)
        high_ref[to, :, at] = kern.astype(BF16)
        head = high_ref[to, :, at].astype(F32)
        low_ref[to, :, at] = (kern - head).astype(BF16)


def build_kernel(sh, spans, own_ref, *refs):
    group_refs, (high_ref, low_ref, near_ref) = refs[: len(spans)], refs[len(spans) :]
    centre = sh.centre(lax.axis_index("gx"), lax.axis_index("gy"))
    own = own_features(own_ref[...], centre).astype(BF16)

    def one(ref, c, to):
        features = near_features(ref[c], centre).astype(BF16)
        near_ref[to] = features
        near = features.T
        for layer in range(sh.layers):
            build_layer(sh, near, own, layer, high_ref, low_ref, to)

    base = 0
    for ref, (start, stop) in zip(group_refs, spans):
        for c in range(start, stop):
            one(ref, c, base + c - start)
        base += stop - start


def built(refs, group, c):
    if group:
        return refs[2], (group - 1) * 3 + c
    return (refs[1], c - 1) if c else (refs[0], 0)


def split_rows(values):
    head = values.astype(BF16)
    tail = values - head.astype(F32)
    return head, jnp.concatenate([head.astype(F32), tail], axis=0).astype(BF16)


def apply_layer(sh, high_ref, low_ref, c, head, both, layer, out_ref):
    low, high, offset = sh.blocks[layer]
    at = slice(layer * sh.slots, (layer + 1) * sh.slots)
    width = (high - low) * sh.slots
    main = bf16_dot(both[:, at], high_ref[c, :, offset : offset + width])
    rest = bf16_dot(head[:, at], low_ref[c, :, offset : offset + width])
    out_ref[:, low * sh.slots : high * sh.slots] += main[:8] + main[8:] + rest


def apply_column(sh, high_ref, low_ref, c, values, out_ref):
    head, both = split_rows(values)
    for layer in range(sh.layers):
        apply_layer(sh, high_ref, low_ref, c, head, both, layer, out_ref)


def spread_dot(part, high, low):
    head, both = split_rows(part)
    main = bf16_dot(both, high)
    return main[:8] + main[8:] + bf16_dot(head, low)


def coarse_dot(terms, gram_ref):
    gram = gram_ref[...]
    high = gram.astype(BF16)
    return spread_dot(terms, high, (gram - high.astype(F32)).astype(BF16))


def gathered_matrix(sh, recv_ref, gram_ref):
    width = sh.row_landmarks
    half = LANES // 2
    groups = half // width
    lane = lane_ids(sh.ny * 8, LANES)
    for g in range(groups):
        total = jnp.zeros((sh.ny * 8, LANES), F32)
        for i in range(sh.nx):
            tiles = jnp.concatenate([recv_ref[i * sh.ny + j] for j in range(sh.ny)], axis=0)
            base = half if i * width < half else 0
            shift = (i * width - base - g * width) % LANES
            if shift:
                tiles = pltpu.roll(tiles, shift, axis=1)
            keep = jnp.logical_and(lane >= i * width, lane < (i + 1) * width)
            total = jnp.where(keep, tiles, total)
        for j in range(sh.ny):
            for r in range(8):
                p = groups * r + g
                at = (p // sh.owned) * width + j * sh.owned + p % sh.owned
                gram_ref[at : at + 1, :] = total[j * 8 + r : j * 8 + r + 1, :]


def rhs_rows(column, lanes):
    return jnp.where(
        row_ids(lanes) < 3, jnp.concatenate([column[3:8], column[0:3]], axis=0), 0.0
    )


def first_kernel(
    sh, row_ref, even_ref, odd_ref, recv_ref, near0_ref, near1_ref,
    high0_ref, high1_ref, low0_ref, low1_ref,
    pay_ref, search_ref, spread_ref, rest_ref, gram_ref, image_ref, high2_ref, low2_ref,
    mark_ref,
):
    high_refs = (high0_ref, high1_ref, high2_ref)
    low_refs = (low0_ref, low1_ref, low2_ref)
    i, j = lax.axis_index("gx"), lax.axis_index("gy")
    centre = sh.centre(i, j)
    half = LANES // 2
    image_ref[...] = jnp.zeros_like(image_ref)
    rows, _ = sh.near_ids(i, j)
    column_refs = (row_ref, even_ref, odd_ref)
    near_values, marks, parts, ready = {}, [], [], {}

    def gather():
        totals = [jnp.zeros((8, LANES), F32), jnp.zeros((8, LANES), F32)]
        for d in range(sh.devices):
            side = 0 if d * sh.owned < half else 1
            totals[side] = totals[side] + recv_ref[d]
        gathered = jnp.where(lane_ids(8, LANES) < half, totals[0], totals[1])
        gathered_matrix(sh, recv_ref, gram_ref)
        return jnp.where(row_ids(LANES) == 6, 1.0, gathered)

    def solve(gathered):
        mark_ref[...] = own_features(gathered, centre).T.astype(BF16)
        coarse = coarse_dot(rhs_rows(gathered, LANES), gram_ref)
        for near_row in rows:
            start = sh.window_start(near_row)
            marks.append(mark_ref[pl.ds(start, sh.window), :])
            parts.append(sh.window_of(coarse, start))

    def start_column(at):
        group, c = divmod(at, 3)
        near = near_values.pop(at) if group else (near1_ref[c - 1] if c else near0_ref[0])
        spread = scaled_wendland(bf16_dot(marks[c], near)) * (1.0 / KERN_SCALE)
        head = spread.astype(BF16)
        rest = (spread - head.astype(F32)).astype(BF16)
        spread_ref[at] = head
        rest_ref[at] = rest
        residual = rhs_rows(column_refs[group][c], sh.points)
        search = residual * (1.0 / RIDGE_WEIGHT) + spread_dot(parts[c], head, rest)
        search_ref[at] = search
        ready[at] = split_rows(search)

    def apply_piece(at, layer):
        head, both = ready[at]
        high_ref, kern_at = built(high_refs, *divmod(at, 3))
        low_ref, _ = built(low_refs, *divmod(at, 3))
        apply_layer(sh, high_ref, low_ref, kern_at, head, both, layer, image_ref)

    own_side = own_features(row_ref[0], centre).astype(BF16)
    plan = [[], [0, 1], [2, 3], [4, 5], [6], [7], [8]]
    for step in range(6):
        group, c = divmod(step + 3, 3)
        near_values[step + 3] = near_features(column_refs[group][c], centre).astype(BF16)
        near = near_values[step + 3].T
        following = list(plan[step + 1])
        for layer in range(sh.layers):
            build_layer(sh, near, own_side, layer, high2_ref, low2_ref, step)
            for at in plan[step]:
                apply_piece(at, layer)
            if step == 0 and layer == 0:
                gathered = gather()
            if step == 0 and layer == 1:
                solve(gathered)
            if layer >= 2 and following:
                start_column(following.pop(0))
    for at in plan[6]:
        for layer in range(sh.layers):
            apply_piece(at, layer)
    residual = rhs_rows(row_ref[0], sh.points)
    search = search_ref[0]
    image = image_ref[...] * (1.0 / KERN_SCALE) + RIDGE_WEIGHT * search
    image_ref[...] = image
    gamma = jnp.sum(residual * search, axis=1, keepdims=True)
    delta = jnp.sum(search * image, axis=1, keepdims=True)
    head, both = split_rows(image)
    across = (((1,), (1,)), ((), ()))
    main = lax.dot_general(both, spread_ref[0], across, preferred_element_type=F32)
    tail = lax.dot_general(head, rest_ref[0], across, preferred_element_type=F32)
    window = main[:8] + main[8:] + tail
    lane = lane_ids(8, LANES)
    fill = jnp.zeros((8, LANES - sh.window), F32)
    tile = jnp.concatenate([window, fill], axis=1)
    tile = jnp.where(lane == 2 * sh.window, gamma, tile)
    tile = jnp.where(lane == 2 * sh.window + 1, delta, tile)
    moved = pltpu.roll(tile, sh.window, axis=1)
    lane1 = lane_ids(1, LANES)
    pair = jnp.where(
        jnp.logical_and(lane1 >= sh.window, lane1 < 2 * sh.window), moved[1:2], tile[0:1]
    )
    ends = jnp.where(lane1 == 2 * sh.window + 2, gamma[1:2], pair)
    ends = jnp.where(lane1 == 2 * sh.window + 3, delta[1:2], ends)
    lines = [ends, tile[2:3]]
    for d in range(sh.devices):
        for q in range(3):
            pay_ref[d, :, q * sh.points : (q + 1) * sh.points] = image[q : q + 1, :]
        for at, line in enumerate(lines):
            start = 3 * sh.points + at * LANES
            pay_ref[d, :, start : start + LANES] = line


def second_kernel(
    sh, recv_ref, row_ref, search_ref, spread_ref, rest_ref, gram_ref, image_ref, *refs,
):
    second_body(
        sh, recv_ref, row_ref, search_ref, spread_ref, rest_ref, gram_ref, image_ref,
        refs[0:3], refs[3:6], *refs[6:],
    )


def second_body(
    sh, recv_ref, row_ref, search_ref, spread_ref, rest_ref, gram_ref, image_ref,
    high_refs, low_refs, pay_ref, sums_ref, residual_ref, next_ref, product_ref,
):
    i, j = lax.axis_index("gx"), lax.axis_index("gy")
    lane = lane_ids(8, LANES)
    row8 = row_ids(LANES)
    terms = jnp.zeros((8, LANES), F32)
    scalars = jnp.zeros((8, LANES), F32)
    for a in range(sh.nx):
        lines = []
        for at in (3 * sh.points, 3 * sh.points + LANES):
            total = recv_ref[a * sh.ny, :, at : at + LANES]
            for b in range(1, sh.ny):
                total = total + recv_ref[a * sh.ny + b, :, at : at + LANES]
            lines.append(total)
        pair = jnp.broadcast_to(lines[0], (8, LANES))
        third = jnp.broadcast_to(lines[1], (8, LANES))
        tile = jnp.where(row8 == 2, third, pair)
        scalars = scalars + tile
        start = min(max(a - 1, 0), sh.nx - 3) * sh.row_landmarks
        first = pltpu.roll(tile, start, axis=1) if start else tile
        other = pltpu.roll(tile, (start - sh.window) % LANES, axis=1)
        inside = jnp.logical_and(lane >= start, lane < start + sh.window)
        value = jnp.where(row8 == 1, other, first)
        terms = terms + jnp.where(jnp.logical_and(inside, row8 < 3), value, 0.0)
    ends = 2 * sh.window

    def column(at):
        second = scalars[:, ends + 2 + at : ends + 3 + at]
        value = scalars[:, ends + at : ends + at + 1]
        return jnp.where(lax.broadcasted_iota(jnp.int32, (8, 1), 0) == 1, second, value)

    gamma, delta = column(0), column(1)
    row1 = lax.broadcasted_iota(jnp.int32, (8, 1), 0)
    alpha = jnp.where(row1 < 3, gamma / jnp.where(row1 < 3, delta, 1.0), 0.0)
    coarse = coarse_dot(terms, gram_ref)
    product_ref[...] = jnp.zeros_like(product_ref)
    rows, cols = sh.near_ids(i, j)
    zeros5 = jnp.zeros((5, sh.points), F32)
    pending = []
    parts = [sh.window_of(coarse, sh.window_start(near_row)) for near_row in rows]
    for group in range(3):
        for c in range(3):
            at = group * 3 + c
            high_ref, kern_at = built(high_refs, group, c)
            low_ref = built(low_refs, group, c)[0]
            source = rows[c] * sh.ny + cols[group]
            image = jnp.concatenate(
                [recv_ref[source, :, q * sh.points : (q + 1) * sh.points] for q in range(3)]
                + [zeros5],
                axis=0,
            )
            step = image * (1.0 / RIDGE_WEIGHT) + spread_dot(parts[c], spread_ref[at], rest_ref[at])
            search = search_ref[at] - alpha * step
            if at == 0:
                next_ref[...] = search
            if pending:
                apply_column(sh, *pending.pop(), product_ref)
            pending.append((high_ref, low_ref, kern_at, search))
    apply_column(sh, *pending.pop(), product_ref)
    residual = rhs_rows(row_ref[0], sh.points)
    image = image_ref[...]
    residual = residual - alpha * image
    residual_ref[...] = residual
    search = next_ref[...]
    product = product_ref[...] * (1.0 / KERN_SCALE) + RIDGE_WEIGHT * search
    product_ref[...] = product
    sums = [
        jnp.sum(residual * search, axis=1, keepdims=True),
        jnp.sum(search * product, axis=1, keepdims=True),
        jnp.sum(search * image, axis=1, keepdims=True)
        + jnp.sum(search_ref[0] * product, axis=1, keepdims=True),
    ]
    line = jnp.zeros((1, LANES), F32)
    lane1 = lane_ids(1, LANES)
    for at, value in enumerate(sums):
        for q in range(3):
            line = jnp.where(lane1 == 3 * at + q, value[q : q + 1, :], line)
    for d in range(sh.devices):
        pay_ref[d] = line
    sums_ref[...] = jnp.where(lane == 0, gamma, jnp.where(lane == 1, delta, 0.0))


def last_kernel(
    sh, recv_ref, sums_ref, search_ref, image_ref, residual_ref, next_ref, product_ref,
    solution_ref, final_ref,
):
    total = recv_ref[0]
    for d in range(1, sh.devices):
        total = total + recv_ref[d]
    row1 = lax.broadcasted_iota(jnp.int32, (8, 1), 0)
    good = row1 < 3

    def column(at):
        value = jnp.zeros((8, 1), F32)
        for q in range(3):
            value = jnp.where(row1 == q, total[:, 3 * at + q : 3 * at + q + 1], value)
        return value

    own = sums_ref[...]
    gamma, delta = own[:, 0:1], own[:, 1:2]
    gamma_new, inner, cross = column(0), column(1), column(2)
    safe_gamma = jnp.where(good, gamma, 1.0)
    safe_delta = jnp.where(good, delta, 1.0)
    alpha = gamma / safe_delta
    beta = gamma_new / safe_gamma
    curve = inner + beta * cross + beta * beta * delta
    step = gamma_new / jnp.where(good, curve, 1.0)
    direction = next_ref[...] + beta * search_ref[0]
    image = product_ref[...] + beta * image_ref[...]
    solution = alpha * search_ref[0] + step * direction
    residual = residual_ref[...] - step * image
    for layer in range(sh.layers):
        at = slice(layer * sh.slots, (layer + 1) * sh.slots)
        solution_ref[:, 0, 0, layer, :] = solution[0:3, at]
        final_ref[:, 0, 0, layer, :] = residual[0:3, at]


def local_fast(positions, counts, targets, landmark_index, coarse_matrix):
    both = ("gx", "gy")
    sh = Shape(positions, landmark_index, lax.axis_size("gx"), lax.axis_size("gy"))
    field = jax.ShapeDtypeStruct((8, sh.points), F32)
    vmem = pl.BlockSpec(memory_space=pltpu.VMEM)
    anyw = pl.BlockSpec(memory_space=pltpu.HBM)

    def call(kernel, name, out_shape, in_specs, cost=10**6, scratch=()):
        return pl.pallas_call(
            kernel,
            out_shape=out_shape,
            in_specs=in_specs,
            out_specs=jax.tree.map(lambda _: vmem, out_shape),
            scratch_shapes=scratch,
            name=name,
            compiler_params=pltpu.CompilerParams(vmem_limit_bytes=VMEM_BYTES),
            cost_estimate=pl.CostEstimate(flops=cost, bytes_accessed=10**5, transcendentals=0),
        )

    def part(kernel, *fixed):
        return functools.partial(kernel, sh, *fixed)

    def exchange(payload):
        return lax.all_to_all(payload, both, 0, 0)

    index = jnp.transpose(landmark_index, (1, 2, 0))
    turned = jnp.transpose(coarse_matrix)
    tile = jax.ShapeDtypeStruct((8, LANES), F32)
    own, marks, block = call(
        part(prepare_kernel),
        "prepare",
        (field, tile, tile),
        [anyw] * 5,
        scratch=[
            pltpu.VMEM(positions.shape, F32),
            pltpu.SMEM(counts.shape, jnp.int32),
            pltpu.VMEM(targets.shape, F32),
            pltpu.SMEM(index.shape, jnp.int32),
            pltpu.VMEM(turned.shape, F32),
            pltpu.VMEM((LANES, turned.shape[0]), F32),
            pltpu.SemaphoreType.DMA((5,)),
        ],
    )(*(pltpu.with_memory_space_constraint(x, pltpu.HBM)
        for x in (positions, counts, targets, index, turned)))
    row = jnp.stack([own, swap(own, "gx", 0), swap(own, "gx", 1)])

    def build(name, spans, *groups):
        columns = sum(stop - start for start, stop in spans)
        kern = jax.ShapeDtypeStruct((columns, sh.slots, sh.pairs), BF16)
        near = jax.ShapeDtypeStruct((columns, 48, sh.points), BF16)
        return call(
            part(build_kernel, spans),
            name,
            (kern, kern, near),
            [vmem] * (1 + len(groups)),
            cost=columns * 3 * 10**9,
        )(own, *groups)

    high0, low0, near0 = build("build_own", [(0, 1)], own[None])
    row, near0 = lax.optimization_barrier((row, near0))
    even, odd = swap(row, "gy", 0), swap(row, "gy", 1)
    high1, low1, near1 = build("build_pair", [(1, 3)], row)
    terms = call(
        part(terms_kernel),
        "terms",
        jax.ShapeDtypeStruct((sh.devices, 8, LANES), F32),
        [anyw] + [vmem] * 5,
    )(near1, marks, block, row, even, odd)
    terms, even, odd = lax.optimization_barrier((exchange(terms), even, odd))
    wide = 3 * sh.points + 2 * LANES
    spread_shape = jax.ShapeDtypeStruct((9, sh.window, sh.points), BF16)
    kern = jax.ShapeDtypeStruct((6, sh.slots, sh.pairs), BF16)
    payload, search, spread, rest, gram, image, high2, low2 = call(
        part(first_kernel),
        "first",
        (
            jax.ShapeDtypeStruct((sh.devices, 1, wide), F32),
            jax.ShapeDtypeStruct((9, 8, sh.points), F32),
            spread_shape,
            spread_shape,
            jax.ShapeDtypeStruct((sh.landmarks, LANES), F32),
            field,
            kern,
            kern,
        ),
        [vmem] * 10,
        scratch=[pltpu.VMEM((sh.landmarks, 48), BF16)],
    )(row, even, odd, terms, near0, near1, high0, high1, low0, low1)
    images = exchange(payload)

    line = jax.ShapeDtypeStruct((sh.devices, 1, LANES), F32)
    totals, sums, residual, following, product = call(
        part(second_kernel), "second", (line, tile, field, field, field), [vmem] * 13
    )(images, row, search, spread, rest, gram, image, high0, high1, high2, low0, low1, low2)
    totals = exchange(totals)

    out = jax.ShapeDtypeStruct(targets.shape, F32)
    return call(part(last_kernel), "last", (out, out), [vmem] * 7)(
        totals, sums, search, image, residual, following, product
    )


def fits_fast(positions, targets, landmark_index, coarse_matrix, nx, ny):
    owned = landmark_index.shape[2]
    return (
        nx * ny * owned == LANES
        and 6 * ny * owned + 4 <= LANES
        and nx >= 3
        and targets.shape[0] == 3
        and coarse_matrix.shape[0] == 8 * (LANES // 2 // (ny * owned))
    )


def local(positions, counts, targets, landmark_index, coarse_matrix):
    nx, ny = lax.axis_size("gx"), lax.axis_size("gy")
    if fits_fast(positions, targets, landmark_index, coarse_matrix, nx, ny):
        return local_fast(positions, counts, targets, landmark_index, coarse_matrix)
    return local_plain(positions, counts, targets, landmark_index, coarse_matrix)


def solution(mesh):
    return jax.shard_map(
        local,
        mesh=mesh,
        in_specs=(
            P(None, "gx", "gy", None, None),
            P("gx", "gy", None),
            P(None, "gx", "gy", None, None),
            P(),
            P("gy", "gx"),
        ),
        out_specs=(P(None, "gx", "gy", None, None), P(None, "gx", "gy", None, None)),
        check_vma=False,
    )
```
